32 devices in a mesh: freq: 4 (over z), tm: 4 (over x, core), grp: 2 (over y).
Axes of the slice: x: 2, y: 2, z: 4, core: 2. Of those that a mesh axis runs over, the one named last changes fastest.
Arguments:
- voltages: bfloat16 [4, 2, 1024, 4096], P(None, None, ('freq', 'grp'), 'tm'), may hold values from -6 to 6
- prior_gains: float32 [4, 2, 1024], P('freq'), may hold values from -4.2 to 4.2
- station_flags: int32 [512], replicated, may hold values 0 or 1
- ingest_map: int32 [512], replicated, may hold values from 0 to 511, each once
- station_coords: float32 [2, 512], replicated, may hold values from -40 to 40
- pointing: int32 [2, 256], replicated, may hold values from 0 to 63
- corr_channels: int32 [4], replicated, may hold values from 0 to 3, each once
- beam_channels: int32 [4], replicated, may hold values from 0 to 3, each once
Outputs:
- visibilities: float32 [4, 2, 1024, 1024], P('freq', None, 'grp', 'tm')
- solved_gains: float32 [4, 2, 1024], P('freq')
- tied_beams: bfloat16 [4, 2, 2, 256, 4096], P('freq', None, None, 'grp', 'tm')
The draws below stay inside these ranges and needn't reach their ends.
Inputs may be any that keep to these rules, and one draw needn't show every extreme that they name: `ingest_map`: each station appears in exactly one ingest slot. `corr_channels`: each channel is handled by exactly one correlator slot. `beam_channels`: each channel is handled by exactly one beamformer slot.
All inputs are finite; a program needn't handle non-finite values.
Results may differ from the reference program's by a relative error of at most 0.0049.
Values may be sent and summed in bfloat16 or wider, within the bound.
A program may use at most 64 MiB of HBM per device.

```python
import math
import jax
import jax.numpy as jnp
from jax import lax

S = 512
NBEAM = 256
ITERS = 4
NIN = 1024
C = 4
TIME = 4096


def plant(drawn, rng, least, top_value):
    spot = [jax.random.randint(jax.random.fold_in(rng, axis), (), 0, length) for axis, length in enumerate(drawn.shape)]
    longest = drawn.shape.index(max(drawn.shape))
    beside = spot[:longest] + [(spot[longest] + 1) % drawn.shape[longest]] + spot[longest + 1:]
    return drawn.at[tuple(spot)].set(least).at[tuple(beside)].set(top_value)


def block_levels(stream_key, dims, pieces, low, top_value):
    gain, own = 1.0, jax.random.fold_in(stream_key, 6)
    for position, parts in pieces:
        heights = jnp.exp(jax.random.uniform(jax.random.fold_in(own, position), (parts,), jnp.float32, low / len(pieces), top_value / len(pieces)))
        gain = gain * jnp.repeat(heights, dims[position] // parts).reshape([-1 if axis == position else 1 for axis in range(len(dims))])
    return gain


def gaussian(stream_key, dims, spread, most, shards=(), held_as=jnp.bfloat16):
    array = spread * jax.random.normal(stream_key, dims, jnp.float32)
    if shards:
        array = array * block_levels(stream_key, dims, shards, -0.22, 0.18)
    return jnp.clip(array, -most, most).astype(held_as)


def setup_inputs(seed: int = 0) -> dict:
    keys = jax.random.split(jax.random.key(seed), 9)
    return {
        "voltages": gaussian(keys[0], (C, 2, NIN, TIME), 1.0, 6.0, ((2, 8), (3, 4))),
        "prior_gains": gaussian(keys[1], (C, 2, NIN), 0.7, 4.2, ((0, 4),), jnp.float32),
        "station_flags": plant((jax.random.randint(keys[2], (S,), 0, 16) < 1).astype(jnp.int32), jax.random.fold_in(keys[2], 1), 0, 1),
        "ingest_map": jax.random.permutation(keys[3], S).astype(jnp.int32),
        "station_coords": jnp.clip(jax.random.uniform(keys[4], (2, S), jnp.float32, -40.0, 40.0), -40.0, 40.0),
        "pointing": plant(jax.random.randint(keys[5], (2, NBEAM), 0, 64), jax.random.fold_in(keys[5], 1), 0, 63).astype(jnp.int32),
        "corr_channels": jax.random.permutation(keys[6], C).astype(jnp.int32),
        "beam_channels": jax.random.permutation(keys[7], C).astype(jnp.int32),
    }


grid_cells = 64.0

def keep_inputs(station_flags, ingest_map):
    slot_keep = 1 - jnp.take(station_flags, ingest_map)
    return jnp.concatenate([slot_keep, slot_keep]).astype(jnp.bfloat16)

def correlate(block):
    left_real = jnp.concatenate([block[0], block[1]], axis=1)
    left_imag = jnp.concatenate([block[1], -block[0]], axis=1)
    real_part = jnp.dot(left_real, left_real.T, preferred_element_type=jnp.float32)
    imag_part = jnp.dot(left_imag, left_real.T, preferred_element_type=jnp.float32)
    return jnp.stack([real_part, imag_part]) * (1.0 / TIME)

def solve(visibilities, prior_gains):
    gains = prior_gains
    highest = lax.Precision.HIGHEST
    for iteration in range(ITERS):
        power = lax.optimization_barrier(jnp.sum(gains * gains, axis=(1, 2))) + 1e-06
        real_real = jnp.einsum('cij,cj->ci', visibilities[:, 0], gains[:, 0], precision=highest)
        imag_imag = jnp.einsum('cij,cj->ci', visibilities[:, 1], gains[:, 1], precision=highest)
        real_imag = jnp.einsum('cij,cj->ci', visibilities[:, 0], gains[:, 1], precision=highest)
        imag_real = jnp.einsum('cij,cj->ci', visibilities[:, 1], gains[:, 0], precision=highest)
        update = jnp.stack([real_real - imag_imag, imag_real + real_imag], axis=1)
        gains = 0.5 * (gains + 2 * S * update / power[:, None, None])
    return gains

def weights_for(gains_sel, ratio, pointing_part, slot_coords):
    east_dir = (pointing_part[0].astype(jnp.float32) + 0.5) / grid_cells - 0.5
    north_dir = (pointing_part[1].astype(jnp.float32) + 0.5) / grid_cells - 0.5
    phase = 2.0 * math.pi * ratio * (east_dir[:, None] * slot_coords[0][None, :] + north_dir[:, None] * slot_coords[1][None, :])
    cosine = jnp.cos(phase)
    sine = jnp.sin(phase)
    gain_real = gains_sel[0].reshape(2, S)
    gain_imag = gains_sel[1].reshape(2, S)
    denom = jnp.maximum(gain_real * gain_real + gain_imag * gain_imag, 0.5)
    along_real = gain_real / denom
    along_imag = gain_imag / denom
    factor = 1.0 / math.sqrt(S)
    w_real = (cosine[None] * along_real[:, None, :] - sine[None] * along_imag[:, None, :]) * factor
    w_imag = -(cosine[None] * along_imag[:, None, :] + sine[None] * along_real[:, None, :]) * factor
    upper = jnp.stack([w_real, -w_imag], axis=2)
    lower = jnp.stack([w_imag, w_real], axis=2)
    return jnp.stack([upper, lower], axis=1).astype(jnp.bfloat16)

def reference(voltages, prior_gains, station_flags, ingest_map, station_coords, pointing, corr_channels, beam_channels):
    keep = keep_inputs(station_flags, ingest_map)

    def corr_slot(channel):
        block = voltages[channel] * keep[None, :, None]
        return correlate(block)
    visibilities = lax.map(corr_slot, corr_channels)
    solved = solve(visibilities, prior_gains)
    slot_coords = jnp.take(station_coords, ingest_map, axis=1)

    def beam_slot(channel):
        onehot = (corr_channels == channel).astype(jnp.float32)
        gains_sel = jnp.einsum('k,kri->ri', onehot, solved, precision=lax.Precision.HIGHEST)
        ratio = 0.875 + 0.25 * (channel.astype(jnp.float32) + 0.5) / C
        weights = weights_for(gains_sel, ratio, pointing, slot_coords)
        block = (voltages[channel] * keep[None, :, None]).reshape(2, 2, S, TIME)
        beams = jnp.einsum('pobrq,rpqt->pobt', weights.astype(jnp.float32), block.astype(jnp.float32))
        return beams.astype(jnp.bfloat16)
    tied_beams = lax.map(beam_slot, beam_channels)
    return (visibilities, solved, tied_beams)
```

```python
import functools
import math

import jax
import jax.numpy as jnp
from jax import lax
from jax.experimental import pallas as pl
from jax.experimental.pallas import tpu as pltpu
from jax.sharding import PartitionSpec as P

ITERS = 4
LANES = 128
grid_cells = 64.0
MESH = pl.DeviceIdType.MESH


def partner(index, mask, count):
    result, bit = 0, 1
    while bit < count:
        digit = (index // bit) % 2
        result = result + bit * ((1 - digit) if mask & bit else digit)
        bit *= 2
    return result


def nt_dot(a, b):
    return lax.dot_general(a, b, (((1,), (1,)), ((), ())), preferred_element_type=jnp.float32)


class Plan:
    def __init__(self, nf, nt, ng, per_input, samples):
        self.nf, self.nt, self.ng = nf, nt, ng
        self.per_input, self.samples = per_input, samples
        self.inputs = nf * ng * per_input
        self.rows = self.inputs // ng
        self.cols = self.inputs // nt
        self.blocks = self.cols // per_input
        self.row_tiles = nt // ng
        quarter = per_input // 4
        self.late = quarter if quarter % 16 == 0 else 0
        self.early = per_input - self.late
        step = min(per_input, 32)
        self.chunks = tuple((part, first, step) for first in range(0, per_input, step) for part in (0, 1))
        half = self.cols // 2
        early_rows, late_rows = self.blocks * self.early, self.blocks * self.late
        units = [(0, early_rows, 0, half), (0, early_rows, half, half)]
        if late_rows:
            units.append((early_rows, late_rows, 0, self.cols))
        self.units = tuple(units)
        segments = [(b * self.early, self.early, b * per_input) for b in range(self.blocks)]
        if self.late:
            base = self.blocks * self.early
            segments += [(base + b * self.late, self.late, b * per_input + self.early) for b in range(self.blocks)]
        self.segments = tuple(segments)

    def held_row(self, first):
        if first < self.early:
            return self.early, first
        return self.late, self.blocks * self.early + first - self.early

    def unit_shape(self, unit):
        _, seg, _, lanes = self.units[unit]
        return self.row_tiles * seg, lanes


def kernel(plan, *refs):
    nf, nt, ng = plan.nf, plan.nt, plan.ng
    nu = len(plan.units)
    operands, refs = refs[:8], refs[8:]
    vis_hbm, gains_out, beams_hbm = refs[:3]
    refs = refs[3:]

    def take(count):
        nonlocal refs
        taken, refs = refs[:count], refs[count:]
        return taken

    src, corr, keep, cosine, sine, to_held, to_natural, left, right, beams_out, vis_out, gram = take(12)
    priors, updates, z, gains = take(4)
    stage_a, landed_a, stage_b, landed_b = (take(nu) for _ in range(4))
    first_src, mid, second_src, landed = (take(nu) for _ in range(4))
    zs, zr, ys, yr, own_sem, qs, qr, us, ur, gs, gr, as_, ar, bs, br, fs, fr, ss, sr, out_sem, in_sem = take(21)
    held = refs
    voltages, prior, flags, slots, coords, pointing, corr_channels, beam_channels = held
    loads = [pltpu.make_async_copy(operands[i], held[i], in_sem.at[i]) for i in range(8)]
    for load in loads:
        load.start()
    f = lax.axis_index("freq")
    t = lax.axis_index("tm")
    g = lax.axis_index("grp")
    per_input, samples = plan.per_input, plan.samples
    inputs, rows, cols = plan.inputs, plan.rows, plan.cols
    stations = inputs // 2
    chunks = plan.chunks
    offsets = [(dt, dg) for dg in range(ng) for dt in range(nt) if (dt, dg) != (0, 0)]
    masks = list(range(nf - 1, 0, -1))
    peers = {k: partner(f, k, nf) for k in range(nf)}
    tiles = {d: partner(t, d, nt) for d in range(nt)}

    def group(dt, dg):
        return {"freq": f, "tm": (t + dt) % nt, "grp": (g + dg) % ng}

    def along_freq(k):
        return {"freq": peers[k], "tm": t, "grp": g}

    def along_tm(d):
        return {"freq": f, "tm": tiles[d], "grp": g}

    barrier = pltpu.get_barrier_semaphore()
    for k in masks:
        pl.semaphore_signal(barrier, inc=1, device_id=along_freq(k), device_id_type=MESH)
    for dt, dg in offsets:
        pl.semaphore_signal(barrier, inc=1, device_id=group(dt, dg), device_id_type=MESH)
    for load in loads:
        load.wait()

    slot_rows = jnp.broadcast_to(slots[...].astype(jnp.float32), (LANES, stations)).T
    flagged = jnp.zeros((stations, LANES), jnp.float32)
    for first in range(0, stations, LANES):
        lane = lax.broadcasted_iota(jnp.int32, (stations, LANES), 1) + first
        flag = flags[0:1, first : first + LANES].astype(jnp.float32)
        flagged += jnp.where(slot_rows == lane.astype(jnp.float32), flag, 0.0)
    flagged = jnp.sum(flagged, axis=1, keepdims=True)
    keep[...] = jnp.broadcast_to(1.0 - flagged, (stations, LANES))
    first_slot = pl.multiple_of(((f * ng + g) * per_input) % stations, per_input)
    kept = keep[pl.ds(first_slot, per_input), 0:1].astype(jnp.bfloat16)

    for k in masks + [0]:
        for part in (0, 1):
            src[peers[k], part] = voltages[beam_channels[peers[k]], part] * kept

    pl.semaphore_wait(barrier, len(masks) + len(offsets))

    def held_start(owner, member, first, count):
        block = owner * ng + member
        stride, constant = plan.held_row(first)
        start = (block // plan.blocks) * cols + (block % plan.blocks) * stride + constant
        return pl.multiple_of(start, math.gcd(math.gcd(cols, stride), math.gcd(constant, count)))

    def place(owner, chunk):
        part, first, count = chunk
        return corr.at[part, pl.ds(held_start(owner, g, first, count), count), :]

    def z_copy(k, ci):
        part, first, count = chunks[ci]
        return pltpu.make_async_remote_copy(
            src_ref=src.at[peers[k], part, pl.ds(first, count), :],
            dst_ref=place(f, chunks[ci]),
            send_sem=zs.at[k - 1, ci],
            recv_sem=zr.at[k - 1, ci],
            device_id=along_freq(k),
            device_id_type=MESH,
        )

    def y_copy(k, ci, dg):
        part, first, count = chunks[ci]
        spot = place(peers[k], chunks[ci])
        return pltpu.make_async_remote_copy(
            src_ref=src.at[f, part, pl.ds(first, count), :] if k == 0 else spot,
            dst_ref=spot,
            send_sem=ys.at[dg - 1, k, ci],
            recv_sem=yr.at[dg - 1, k, ci],
            device_id=group(0, dg),
            device_id_type=MESH,
        )

    def forward(k, ci):
        for dg in range(1, ng):
            y_copy(k, ci, dg).start()

    own_parts = [(0, plan.early)] + ([(plan.early, plan.late)] if plan.late else [])
    own_copies = [
        pltpu.make_async_copy(
            src.at[f, :, pl.ds(first, count), :],
            corr.at[:, pl.ds(held_start(f, g, first, count), count), :],
            own_sem.at[i],
        )
        for i, (first, count) in enumerate(own_parts)
    ]

    def prior_copy(k):
        return pltpu.make_async_remote_copy(
            src_ref=prior.at[0],
            dst_ref=priors.at[f],
            send_sem=qs.at[k - 1],
            recv_sem=qr.at[k - 1],
            device_id=along_freq(k),
            device_id_type=MESH,
        )

    all_chunks = range(len(chunks))
    early_chunks = [ci for ci in all_chunks if chunks[ci][1] < plan.early]
    late_chunks = [ci for ci in all_chunks if chunks[ci][1] >= plan.early]
    for ci in all_chunks:
        for k in masks:
            z_copy(k, ci).start()
        if ci == 0:
            for k in masks:
                prior_copy(k).start()
    for ci in all_chunks:
        forward(0, ci)
    for copy in own_copies:
        copy.start()
    priors[f] = prior[0]

    n_beams = pointing.shape[1]
    beams = n_beams // ng
    my_beam = beam_channels[f]
    permuted = len(plan.segments) > 1 and bool(plan.late)

    def natural(held_index):
        result = held_index
        for start, size, target in plan.segments:
            inside = (held_index >= start) & (held_index < start + size)
            result = jnp.where(inside, held_index + (target - start), result)
        return result

    if permuted:
        along_rows = lax.broadcasted_iota(jnp.int32, (cols, cols), 0)
        along_lanes = lax.broadcasted_iota(jnp.int32, (cols, cols), 1)
        to_held[...] = jnp.where(natural(along_lanes) == along_rows, 1.0, 0.0)
        to_natural[...] = jnp.where(natural(along_rows) == along_lanes, 1.0, 0.0)

    def reorder(row_vector, matrix):
        if not permuted:
            return row_vector
        moved = [
            jnp.dot(
                row_vector[:, first : first + cols],
                matrix[...],
                precision=lax.Precision.HIGHEST,
                preferred_element_type=jnp.float32,
            )
            for first in range(0, row_vector.shape[1], cols)
        ]
        return jnp.concatenate(moved, axis=1)

    def point_phases():
        ratio = 0.875 + 0.25 * (my_beam.astype(jnp.float32) + 0.5) / nf
        mine = pl.ds(pl.multiple_of(g * beams, beams), beams)
        east_dir, north_dir = (
            jnp.broadcast_to((pointing[d : d + 1, mine].astype(jnp.float32) + 0.5) / grid_cells - 0.5, (LANES, beams)).T
            for d in (0, 1)
        )
        east, north = (jnp.broadcast_to(coords[d : d + 1, :], (LANES, stations)).T for d in (0, 1))
        station = lax.broadcasted_iota(jnp.int32, (stations, LANES), 0)
        slot_east, slot_north = [], []
        for first in range(0, stations, LANES):
            lanes = slice(first, first + LANES)
            match = station == slots[0:1, lanes]
            slot_east.append(jnp.sum(jnp.where(match, east, 0.0), axis=0, keepdims=True))
            slot_north.append(jnp.sum(jnp.where(match, north, 0.0), axis=0, keepdims=True))
        where = jnp.concatenate(
            [jnp.concatenate(slot_east, axis=1), jnp.concatenate(slot_north, axis=1)] * 4, axis=0
        )
        where = reorder(where, to_held)
        for first in range(0, stations, LANES):
            lanes = slice(first, first + LANES)
            phase = 2.0 * math.pi * ratio * (east_dir * where[0:1, lanes] + north_dir * where[1:2, lanes])
            cosine[:, lanes] = jnp.cos(phase)
            sine[:, lanes] = jnp.sin(phase)

    point_phases()

    scale = 1.0 / (samples * nt)
    odds = list(range(nt - 1, 0, -2))
    evens = [d - 1 for d in odds]

    def a_copy(u):
        return pltpu.make_async_remote_copy(
            src_ref=stage_a[u],
            dst_ref=landed_a[u],
            send_sem=as_.at[u],
            recv_sem=ar.at[u],
            device_id=along_tm(1),
            device_id_type=MESH,
        )

    def b_copy(u, d):
        return pltpu.make_async_remote_copy(
            src_ref=stage_b[u].at[d // 2 - 1],
            dst_ref=landed_b[u].at[d // 2 - 1],
            send_sem=bs.at[u, d // 2 - 1],
            recv_sem=br.at[u, d // 2 - 1],
            device_id=along_tm(d),
            device_id_type=MESH,
        )

    def first_copy(u, k):
        return pltpu.make_async_remote_copy(
            src_ref=first_src[u].at[peers[k]],
            dst_ref=mid[u].at[f],
            send_sem=fs.at[u, k - 1],
            recv_sem=fr.at[u, k - 1],
            device_id=along_freq(k),
            device_id_type=MESH,
        )

    def second_copy(u, k):
        return pltpu.make_async_remote_copy(
            src_ref=second_src[u].at[k - 1],
            dst_ref=landed[u].at[f],
            send_sem=ss.at[u, k - 1],
            recv_sem=sr.at[u, k - 1],
            device_id=along_freq(k),
            device_id_type=MESH,
        )

    def gram_lanes(u, d):
        _, _, lane, lanes = plan.units[u]
        return pl.ds(pl.multiple_of(tiles[d] * cols + lane, LANES), lanes)

    def correlate(u):
        seg, seg_rows, lane, lanes = plan.units[u]

        def stacked(part):
            pieces = []
            for r in range(plan.row_tiles):
                start = pl.multiple_of(g * rows + r * cols + seg, math.gcd(cols, seg_rows))
                pieces.append(corr[part, pl.ds(start, seg_rows), :])
            return jnp.concatenate(pieces, axis=0)

        mine_r, mine_i = stacked(0), stacked(1)
        for odd, members in ((True, odds), (False, evens)):
            others = [
                jnp.concatenate([corr[part, gram_lanes(u, d), :] for d in members], axis=0) for part in (0, 1)
            ]
            real = (nt_dot(mine_r, others[0]) + nt_dot(mine_i, others[1])) * scale
            imag = (nt_dot(mine_i, others[0]) - nt_dot(mine_r, others[1])) * scale
            for part, value in ((0, real), (1, imag)):
                for j, d in enumerate(members):
                    for r in range(plan.row_tiles):
                        gram[part, r * cols + seg : r * cols + seg + seg_rows, gram_lanes(u, d)] = value[
                            r * seg_rows : (r + 1) * seg_rows, j * lanes : (j + 1) * lanes
                        ]
                if odd:
                    stage_a[u][part] = value.astype(jnp.bfloat16)
        a_copy(u).start()

    def from_gram(u, part, d):
        seg, seg_rows, _, _ = plan.units[u]
        return jnp.concatenate(
            [gram[part, r * cols + seg : r * cols + seg + seg_rows, gram_lanes(u, d)] for r in range(plan.row_tiles)],
            axis=0,
        )

    def sum_pair(u):
        lanes = plan.units[u][3]
        a_copy(u).wait_recv()
        for j, d in enumerate(evens):
            if d:
                for part in (0, 1):
                    theirs = landed_a[u][part, :, j * lanes : (j + 1) * lanes].astype(jnp.float32)
                    stage_b[u][d // 2 - 1, part] = (from_gram(u, part, d) + theirs).astype(jnp.bfloat16)
        for d in evens:
            if d:
                b_copy(u, d).start()

    def sum_rest(u):
        total_rows, lanes = plan.unit_shape(u)
        piece = total_rows // nf
        for d in evens:
            if d:
                b_copy(u, d).wait_recv()
        j = len(evens) - 1
        for part in (0, 1):
            total = from_gram(u, part, 0) + landed_a[u][part, :, j * lanes : (j + 1) * lanes].astype(jnp.float32)
            for d in evens:
                if d:
                    total = total + landed_b[u][d // 2 - 1, part].astype(jnp.float32)
            total = total.astype(jnp.bfloat16)
            for p in range(nf):
                first_src[u][p, part] = total[p * piece : (p + 1) * piece]
        mid[u][f] = first_src[u][f]
        for k in masks:
            first_copy(u, k).start()

    def source_of(slot):
        wanted = corr_channels[slot]
        source = 0
        for s in range(nf):
            source = jnp.where(beam_channels[s] == wanted, s, source)
        return source

    def hand_on(u):
        for k in masks:
            first_copy(u, k).wait_recv()
        for k in masks:
            second_src[u][k - 1] = mid[u][source_of(peers[k])]
        landed[u][f] = mid[u][source_of(f)]
        for k in masks:
            second_copy(u, k).start()

    for ci in early_chunks:
        for k in masks:
            z_copy(k, ci).wait_recv()
            forward(k, ci)
    for copy in own_copies:
        copy.wait()
    for ci in early_chunks:
        for k in range(nf):
            for dg in range(1, ng):
                y_copy(k, ci, dg).wait_recv()
    jobs = [(ci, k) for ci in late_chunks for k in masks]

    def forward_late(count):
        for ci, k in jobs[:count]:
            z_copy(k, ci).wait_recv()
            forward(k, ci)
        del jobs[:count]

    if plan.late:
        correlate(0)
        forward_late(nf - 2)
        sum_pair(0)
        forward_late(nf - 2)
        sum_rest(0)
    forward_late(len(jobs))
    for ci in late_chunks:
        for k in range(nf):
            for dg in range(1, ng):
                y_copy(k, ci, dg).wait_recv()
    last_units = [u for u in range(nu) if u > 0 or not plan.late]
    for u in last_units:
        correlate(u)

    for k in masks:
        prior_copy(k).wait_recv()
    slot_of_mine = 0
    for k in range(nf):
        slot_of_mine = jnp.where(corr_channels[k] == my_beam, k, slot_of_mine)
    z[...] = reorder(priors[slot_of_mine], to_held)
    slot = g * nt + t
    strip = LANES

    def update_copy(iteration, o):
        dt, dg = offsets[o]
        return pltpu.make_async_remote_copy(
            src_ref=updates.at[iteration, slot],
            dst_ref=updates.at[iteration, slot],
            send_sem=us.at[iteration, o],
            recv_sem=ur.at[iteration, o],
            device_id=group(dt, dg),
            device_id_type=MESH,
        )

    beside = {i: [] for i in range(ITERS)}
    beside[0] += [functools.partial(sum_pair, u) for u in last_units]
    if plan.late:
        beside[1].append(functools.partial(hand_on, 0))
    beside[2].append(functools.partial(sum_rest, last_units[0]))
    beside[3] += [functools.partial(sum_rest, u) for u in last_units[1:]]
    for iteration in range(ITERS):
        power = jnp.sum(z[...] * z[...]) + 1e-06

        def product(r, carry):
            here = pl.ds(pl.multiple_of(r * strip, strip), strip)
            total_r = jnp.zeros((strip, LANES), jnp.float32)
            total_i = jnp.zeros((strip, LANES), jnp.float32)
            for c in range(inputs // LANES):
                lanes = slice(c * LANES, (c + 1) * LANES)
                part_r = gram[0, here, lanes]
                part_i = gram[1, here, lanes]
                gain_r = z[0:1, lanes]
                gain_i = z[1:2, lanes]
                total_r += part_r * gain_r - part_i * gain_i
                total_i += part_i * gain_r + part_r * gain_i
            updates[iteration, slot, 0:1, here] = jnp.sum(total_r.T, axis=0, keepdims=True)
            updates[iteration, slot, 1:2, here] = jnp.sum(total_i.T, axis=0, keepdims=True)
            return carry

        lax.fori_loop(0, rows // strip, product, 0)
        for o in range(len(offsets)):
            update_copy(iteration, o).start()
        for work in beside[iteration]:
            work()
        for o in range(len(offsets)):
            update_copy(iteration, o).wait_recv()
        for h in range(ng):
            total = updates[iteration, h * nt]
            for other in range(1, nt):
                total = total + updates[iteration, h * nt + other]
            lanes = slice(h * rows, (h + 1) * rows)
            z[:, lanes] = 0.5 * (z[:, lanes] + inputs * total / power)

    gains[f] = reorder(z[...], to_natural)

    def gain_copy(k):
        return pltpu.make_async_remote_copy(
            src_ref=gains.at[f],
            dst_ref=gains.at[f],
            send_sem=gs.at[k - 1],
            recv_sem=gr.at[k - 1],
            device_id=along_freq(k),
            device_id_type=MESH,
        )

    factor = 1.0 / math.sqrt(stations)
    for p in (0, 1):
        gain_r = z[0:1, p * stations : (p + 1) * stations]
        gain_i = z[1:2, p * stations : (p + 1) * stations]
        denom = jnp.maximum(gain_r * gain_r + gain_i * gain_i, 0.5)
        along_r = gain_r / denom
        along_i = gain_i / denom
        cos = cosine[...]
        sin = sine[...]
        w_r = ((cos * along_r - sin * along_i) * factor).astype(jnp.bfloat16)
        w_i = (-(cos * along_i + sin * along_r) * factor).astype(jnp.bfloat16)
        left[p, 0:beams] = w_r
        left[p, beams:] = w_i
        right[p, 0:beams] = -w_i
        right[p, beams:] = w_r
    for k in masks:
        gain_copy(k).start()
    hand_on(last_units[0])

    beam_copies = [
        pltpu.make_async_copy(beams_out.at[:, p], beams_hbm.at[:, p], out_sem.at[p]) for p in (0, 1)
    ]

    def beamform(p):
        rows_p = slice(p * stations, (p + 1) * stations)
        result = jnp.dot(left[p], corr[0, rows_p, :], preferred_element_type=jnp.float32)
        result = result + jnp.dot(right[p], corr[1, rows_p, :], preferred_element_type=jnp.float32)
        result = result.astype(jnp.bfloat16)
        beams_out[0, p, 0] = result[:beams]
        beams_out[0, p, 1] = result[beams:]

    beamform(0)
    for u in last_units[1:]:
        hand_on(u)
    beamform(1)
    for copy in beam_copies:
        copy.start()

    for k in masks:
        gain_copy(k).wait_recv()
    gains_out[0] = gains[source_of(f)]

    for u in range(nu):
        for k in masks:
            second_copy(u, k).wait_recv()
    vis_copies = [pltpu.make_async_copy(vis_out.at[:, part], vis_hbm.at[:, part], out_sem.at[2 + part]) for part in (0, 1)]
    for part in (0, 1):
        strips = [
            jnp.concatenate([landed[u][p, part] for p in range(nf)], axis=0) for u in range(nu)
        ]
        for r in range(plan.row_tiles):
            tile_rows = []
            seg_rows = plan.units[0][1]
            here = slice(r * seg_rows, (r + 1) * seg_rows)
            tile_rows.append(jnp.concatenate([strips[0][here], strips[1][here]], axis=1))
            if plan.late:
                seg_rows = plan.units[2][1]
                tile_rows.append(strips[2][r * seg_rows : (r + 1) * seg_rows])
            tile = jnp.concatenate(tile_rows, axis=0)
            if not permuted:
                vis_out[0, part, r * cols : (r + 1) * cols, :] = tile
                continue
            tile = jnp.dot(
                tile, to_natural[...].astype(jnp.bfloat16), preferred_element_type=jnp.float32
            ).astype(jnp.bfloat16)
            for start, size, target in plan.segments:
                vis_out[0, part, r * cols + target : r * cols + target + size, :] = tile[start : start + size]
    for copy in vis_copies:
        copy.start()

    for k in masks:
        prior_copy(k).wait_send()
        gain_copy(k).wait_send()
    for ci in all_chunks:
        for k in masks:
            z_copy(k, ci).wait_send()
        for k in range(nf):
            for dg in range(1, ng):
                y_copy(k, ci, dg).wait_send()
    for u in range(nu):
        a_copy(u).wait_send()
        for d in evens:
            if d:
                b_copy(u, d).wait_send()
        for k in masks:
            first_copy(u, k).wait_send()
            second_copy(u, k).wait_send()
    for iteration in range(ITERS):
        for o in range(len(offsets)):
            update_copy(iteration, o).wait_send()
    for copy in beam_copies + vis_copies:
        copy.wait()


def body(
    voltages,
    prior_gains,
    station_flags,
    ingest_map,
    station_coords,
    pointing,
    corr_channels,
    beam_channels,
):
    nf = lax.axis_size("freq")
    nt = lax.axis_size("tm")
    ng = lax.axis_size("grp")
    _, _, per_input, samples = voltages.shape
    stations = ingest_map.shape[0]
    plan = Plan(nf, nt, ng, per_input, samples)
    inputs, rows, cols = plan.inputs, plan.rows, plan.cols
    part_beams = pointing.shape[1] // ng
    nc, nu = len(plan.chunks), len(plan.units)
    pairs = nt // 2
    dma = pltpu.SemaphoreType.DMA
    vmem = pl.BlockSpec(memory_space=pltpu.VMEM)
    hbm = pl.BlockSpec(memory_space=pltpu.HBM)
    shapes = [plan.unit_shape(u) for u in range(nu)]

    def bf16(*shape):
        return pltpu.VMEM(shape, jnp.bfloat16)

    def f32(*shape):
        return pltpu.VMEM(shape, jnp.float32)

    vis, gains, beams = pl.pallas_call(
        functools.partial(kernel, plan),
        out_shape=(
            jax.ShapeDtypeStruct((1, 2, rows, cols), jnp.bfloat16),
            jax.ShapeDtypeStruct((1, 2, inputs), jnp.float32),
            jax.ShapeDtypeStruct((1, 2, 2, part_beams, samples), jnp.bfloat16),
        ),
        in_specs=[hbm] * 8,
        out_specs=(hbm, vmem, hbm),
        scratch_shapes=[
            bf16(nf, 2, per_input, samples),
            bf16(2, inputs, samples),
            f32(stations, LANES),
            f32(part_beams, stations),
            f32(part_beams, stations),
            f32(cols, cols),
            f32(cols, cols),
            bf16(2, 2 * part_beams, stations),
            bf16(2, 2 * part_beams, stations),
            bf16(1, 2, 2, part_beams, samples),
            bf16(1, 2, rows, cols),
            f32(2, rows, inputs),
            f32(nf, 2, inputs),
            f32(ITERS, ng * nt, 2, rows),
            f32(2, inputs),
            f32(nf, 2, inputs),
        ]
        + [bf16(2, r, pairs * w) for r, w in shapes] * 2
        + [bf16(pairs - 1, 2, r, w) for r, w in shapes] * 2
        + [bf16(nf, 2, r // nf, w) for r, w in shapes] * 2
        + [bf16(nf - 1, 2, r // nf, w) for r, w in shapes]
        + [bf16(nf, 2, r // nf, w) for r, w in shapes]
        + [
            dma((nf - 1, nc)),
            dma((nf - 1, nc)),
            dma((ng - 1, nf, nc)),
            dma((ng - 1, nf, nc)),
            dma((2,)),
            dma((nf - 1,)),
            dma((nf - 1,)),
            dma((ITERS, ng * nt - 1)),
            dma((ITERS, ng * nt - 1)),
            dma((nf - 1,)),
            dma((nf - 1,)),
            dma((nu,)),
            dma((nu,)),
            dma((nu, pairs - 1)),
            dma((nu, pairs - 1)),
            dma((nu, nf - 1)),
            dma((nu, nf - 1)),
            dma((nu, nf - 1)),
            dma((nu, nf - 1)),
            dma((4,)),
            dma((8,)),
            pltpu.VMEM(voltages.shape, jnp.bfloat16),
            pltpu.VMEM(prior_gains.shape, jnp.float32),
            pltpu.VMEM((1, stations), jnp.int32),
            pltpu.VMEM((1, stations), jnp.int32),
            pltpu.VMEM(station_coords.shape, jnp.float32),
            pltpu.VMEM(pointing.shape, jnp.int32),
            pltpu.SMEM(corr_channels.shape, jnp.int32),
            pltpu.SMEM(beam_channels.shape, jnp.int32),
        ],
        compiler_params=pltpu.CompilerParams(
            collective_id=0, has_side_effects=True, vmem_limit_bytes=67043328
        ),
    )(
        voltages,
        prior_gains,
        station_flags[None],
        ingest_map[None],
        station_coords,
        pointing,
        corr_channels,
        beam_channels,
    )
    return vis.astype(jnp.float32), gains, beams


def solution(mesh):
    return jax.shard_map(
        body,
        mesh=mesh,
        in_specs=(
            P(None, None, ("freq", "grp"), "tm"),
            P("freq", None, None),
            P(),
            P(),
            P(),
            P(),
            P(),
            P(),
        ),
        out_specs=(
            P("freq", None, "grp", "tm"),
            P("freq", None, None),
            P("freq", None, None, "grp", "tm"),
        ),
        check_vma=False,
    )
```

```python
import functools
import math

import jax
import jax.numpy as jnp
from jax import lax
from jax.experimental import pallas as pl
from jax.experimental.pallas import tpu as pltpu
from jax.sharding import PartitionSpec as P

ITERS = 4
LANES = 128
grid_cells = 64.0
MESH = pl.DeviceIdType.MESH


def partner(index, mask, count):
    result, bit = 0, 1
    while bit < count:
        digit = (index // bit) % 2
        result = result + bit * ((1 - digit) if mask & bit else digit)
        bit *= 2
    return result


def nt_dot(a, b):
    return lax.dot_general(a, b, (((1,), (1,)), ((), ())), preferred_element_type=jnp.float32)


class Plan:
    def __init__(self, nf, nt, ng, per_input, samples):
        self.nf, self.nt, self.ng = nf, nt, ng
        self.per_input, self.samples = per_input, samples
        self.inputs = nf * ng * per_input
        self.rows = self.inputs // ng
        self.cols = self.inputs // nt
        self.blocks = self.cols // per_input
        self.row_tiles = nt // ng
        self.levels = 4 if per_input % 64 == 0 else 1
        self.step = per_input // self.levels
        self.level_rows = self.cols // self.levels
        self.chunks = tuple((part, q * self.step, self.step) for q in range(self.levels) for part in (0, 1))
        half, tiles = self.cols // 2, tuple(range(self.row_tiles))
        if self.levels > 1:
            most = self.cols - self.level_rows
            units = [(tiles, 0, most, 0, half)]
            units += [((r,), 0, most, half, half) for r in tiles]
            units += [(tiles, most, self.level_rows, 0, self.cols)]
        else:
            units = [(tiles, 0, self.cols, 0, half), (tiles, 0, self.cols, half, half)]
        self.units = tuple(units)
        self.segments = tuple(
            (q * self.level_rows + b * self.step, self.step, b * per_input + q * self.step)
            for q in range(self.levels)
            for b in range(self.blocks)
        )

    def unit_shape(self, unit):
        tiles, _, seg_rows, _, lanes = self.units[unit]
        return len(tiles) * seg_rows, lanes


def kernel(plan, *refs):
    nf, nt, ng = plan.nf, plan.nt, plan.ng
    nu = len(plan.units)
    operands, refs = refs[:8], refs[8:]
    vis_hbm, gains_out, beams_hbm = refs[:3]
    refs = refs[3:]

    def take(count):
        nonlocal refs
        taken, refs = refs[:count], refs[count:]
        return taken

    src, corr, keep, cosine, sine, to_held, to_natural, left, right, beams_out, vis_out, gram = take(12)
    priors, updates, z, gains = take(4)
    stage_a, landed_a, stage_b, landed_b = (take(nu) for _ in range(4))
    first_src, mid, second_src, landed = (take(nu) for _ in range(4))
    zs, zr, ys, yr, own_sem, qs, qr, us, ur, gs, gr, as_, ar, bs, br, fs, fr, ss, sr, out_sem, in_sem = take(21)
    held = refs
    voltages, prior, flags, slots, coords, pointing, corr_channels, beam_channels = held
    loads = [pltpu.make_async_copy(operands[i], held[i], in_sem.at[i]) for i in range(8)]
    for load in loads:
        load.start()
    f = lax.axis_index("freq")
    t = lax.axis_index("tm")
    g = lax.axis_index("grp")
    per_input, samples = plan.per_input, plan.samples
    inputs, rows, cols = plan.inputs, plan.rows, plan.cols
    stations = inputs // 2
    chunks = plan.chunks
    offsets = [(dt, dg) for dg in range(ng) for dt in range(nt) if (dt, dg) != (0, 0)]
    masks = list(range(nf - 1, 0, -1))
    peers = {k: partner(f, k, nf) for k in range(nf)}
    tiles = {d: partner(t, d, nt) for d in range(nt)}

    def group(dt, dg):
        return {"freq": f, "tm": (t + dt) % nt, "grp": (g + dg) % ng}

    def along_freq(k):
        return {"freq": peers[k], "tm": t, "grp": g}

    def along_tm(d):
        return {"freq": f, "tm": tiles[d], "grp": g}

    barrier = pltpu.get_barrier_semaphore()
    for k in masks:
        pl.semaphore_signal(barrier, inc=1, device_id=along_freq(k), device_id_type=MESH)
    for dt, dg in offsets:
        pl.semaphore_signal(barrier, inc=1, device_id=group(dt, dg), device_id_type=MESH)
    for load in loads:
        load.wait()

    slot_rows = jnp.broadcast_to(slots[...].astype(jnp.float32), (LANES, stations)).T
    flagged = jnp.zeros((stations, LANES), jnp.float32)
    for first in range(0, stations, LANES):
        lane = lax.broadcasted_iota(jnp.int32, (stations, LANES), 1) + first
        flag = flags[0:1, first : first + LANES].astype(jnp.float32)
        flagged += jnp.where(slot_rows == lane.astype(jnp.float32), flag, 0.0)
    flagged = jnp.sum(flagged, axis=1, keepdims=True)
    keep[...] = jnp.broadcast_to(1.0 - flagged, (stations, LANES))
    first_slot = pl.multiple_of(((f * ng + g) * per_input) % stations, per_input)
    kept = keep[pl.ds(first_slot, per_input), 0:1].astype(jnp.bfloat16)

    for k in masks + [0]:
        for part in (0, 1):
            src[peers[k], part] = voltages[beam_channels[peers[k]], part] * kept

    pl.semaphore_wait(barrier, len(masks) + len(offsets))

    def held_start(owner, member, first):
        block = owner * ng + member
        level = first // plan.step
        start = (block // plan.blocks) * cols + level * plan.level_rows + (block % plan.blocks) * plan.step
        return pl.multiple_of(start, plan.step)

    def place(owner, chunk):
        part, first, count = chunk
        return corr.at[part, pl.ds(held_start(owner, g, first), count), :]

    def z_copy(k, ci):
        part, first, count = chunks[ci]
        return pltpu.make_async_remote_copy(
            src_ref=src.at[peers[k], part, pl.ds(first, count), :],
            dst_ref=place(f, chunks[ci]),
            send_sem=zs.at[k - 1, ci],
            recv_sem=zr.at[k - 1, ci],
            device_id=along_freq(k),
            device_id_type=MESH,
        )

    def y_copy(k, ci, dg):
        part, first, count = chunks[ci]
        spot = place(peers[k], chunks[ci])
        return pltpu.make_async_remote_copy(
            src_ref=src.at[f, part, pl.ds(first, count), :] if k == 0 else spot,
            dst_ref=spot,
            send_sem=ys.at[dg - 1, k, ci],
            recv_sem=yr.at[dg - 1, k, ci],
            device_id=group(0, dg),
            device_id_type=MESH,
        )

    def forward(k, ci):
        for dg in range(1, ng):
            y_copy(k, ci, dg).start()

    own_copies = [
        pltpu.make_async_copy(
            src.at[f, :, pl.ds(first, plan.step), :],
            corr.at[:, pl.ds(held_start(f, g, first), plan.step), :],
            own_sem.at[first // plan.step],
        )
        for first in range(0, per_input, plan.step)
    ]

    def prior_copy(k):
        return pltpu.make_async_remote_copy(
            src_ref=prior.at[0],
            dst_ref=priors.at[f],
            send_sem=qs.at[k - 1],
            recv_sem=qr.at[k - 1],
            device_id=along_freq(k),
            device_id_type=MESH,
        )

    all_chunks = range(len(chunks))
    ahead = 2

    def send_chunk(ci):
        if ci < len(chunks):
            for k in masks:
                z_copy(k, ci).start()

    for ci in range(ahead):
        send_chunk(ci)
        if ci == 0:
            for k in masks:
                prior_copy(k).start()
    for ci in all_chunks:
        forward(0, ci)
    for copy in own_copies:
        copy.start()
    priors[f] = prior[0]

    n_beams = pointing.shape[1]
    beams = n_beams // ng
    my_beam = beam_channels[f]
    permuted = plan.levels > 1

    def natural(held_index):
        result = held_index
        for start, size, target in plan.segments:
            inside = (held_index >= start) & (held_index < start + size)
            result = jnp.where(inside, held_index + (target - start), result)
        return result

    if permuted:
        along_rows = lax.broadcasted_iota(jnp.int32, (cols, cols), 0)
        along_lanes = lax.broadcasted_iota(jnp.int32, (cols, cols), 1)
        to_held[...] = jnp.where(natural(along_lanes) == along_rows, 1.0, 0.0)
        to_natural[...] = jnp.where(natural(along_rows) == along_lanes, 1.0, 0.0)

    def reorder(row_vector, matrix):
        if not permuted:
            return row_vector
        moved = [
            jnp.dot(
                row_vector[:, first : first + cols],
                matrix[...],
                precision=lax.Precision.HIGHEST,
                preferred_element_type=jnp.float32,
            )
            for first in range(0, row_vector.shape[1], cols)
        ]
        return jnp.concatenate(moved, axis=1)

    def point_phases():
        ratio = 0.875 + 0.25 * (my_beam.astype(jnp.float32) + 0.5) / nf
        mine = pl.ds(pl.multiple_of(g * beams, beams), beams)
        east_dir, north_dir = (
            jnp.broadcast_to((pointing[d : d + 1, mine].astype(jnp.float32) + 0.5) / grid_cells - 0.5, (LANES, beams)).T
            for d in (0, 1)
        )
        east, north = (jnp.broadcast_to(coords[d : d + 1, :], (LANES, stations)).T for d in (0, 1))
        station = lax.broadcasted_iota(jnp.int32, (stations, LANES), 0)
        slot_east, slot_north = [], []
        for first in range(0, stations, LANES):
            lanes = slice(first, first + LANES)
            match = station == slots[0:1, lanes]
            slot_east.append(jnp.sum(jnp.where(match, east, 0.0), axis=0, keepdims=True))
            slot_north.append(jnp.sum(jnp.where(match, north, 0.0), axis=0, keepdims=True))
        where = jnp.concatenate(
            [jnp.concatenate(slot_east, axis=1), jnp.concatenate(slot_north, axis=1)] * 4, axis=0
        )
        where = reorder(where, to_held)
        for first in range(0, stations, LANES):
            lanes = slice(first, first + LANES)
            phase = 2.0 * math.pi * ratio * (east_dir * where[0:1, lanes] + north_dir * where[1:2, lanes])
            cosine[:, lanes] = jnp.cos(phase)
            sine[:, lanes] = jnp.sin(phase)

    point_phases()

    scale = 1.0 / (samples * nt)
    odds = list(range(nt - 1, 0, -2))
    evens = [d - 1 for d in odds]

    def a_copy(u):
        return pltpu.make_async_remote_copy(
            src_ref=stage_a[u],
            dst_ref=landed_a[u],
            send_sem=as_.at[u],
            recv_sem=ar.at[u],
            device_id=along_tm(1),
            device_id_type=MESH,
        )

    def b_copy(u, d):
        return pltpu.make_async_remote_copy(
            src_ref=stage_b[u].at[d // 2 - 1],
            dst_ref=landed_b[u].at[d // 2 - 1],
            send_sem=bs.at[u, d // 2 - 1],
            recv_sem=br.at[u, d // 2 - 1],
            device_id=along_tm(d),
            device_id_type=MESH,
        )

    def first_copy(u, k):
        return pltpu.make_async_remote_copy(
            src_ref=first_src[u].at[peers[k]],
            dst_ref=mid[u].at[f],
            send_sem=fs.at[u, k - 1],
            recv_sem=fr.at[u, k - 1],
            device_id=along_freq(k),
            device_id_type=MESH,
        )

    def second_copy(u, k):
        return pltpu.make_async_remote_copy(
            src_ref=second_src[u].at[k - 1],
            dst_ref=landed[u].at[f],
            send_sem=ss.at[u, k - 1],
            recv_sem=sr.at[u, k - 1],
            device_id=along_freq(k),
            device_id_type=MESH,
        )

    def correlate(seg, seg_rows, lane, lanes):
        def stacked(part):
            pieces = []
            for r in range(plan.row_tiles):
                start = pl.multiple_of(g * rows + r * cols + seg, plan.level_rows)
                pieces.append(corr[part, pl.ds(start, seg_rows), :])
            return pieces

        mine = jnp.concatenate(stacked(0) + stacked(1), axis=0)
        count = plan.row_tiles * seg_rows
        others = [
            jnp.concatenate(
                [corr[part, tile * cols + lane : tile * cols + lane + lanes, :] for tile in range(nt)], axis=0
            )
            for part in (0, 1)
        ]
        with_r = nt_dot(mine, others[0])
        with_i = nt_dot(mine, others[1])
        real = (with_r[:count] + with_i[count:]) * scale
        imag = (with_r[count:] - with_i[:count]) * scale
        for part, value in ((0, real), (1, imag)):
            for tile in range(nt):
                for r in range(plan.row_tiles):
                    gram[part, tile, r * cols + seg : r * cols + seg + seg_rows, lane : lane + lanes] = value[
                        r * seg_rows : (r + 1) * seg_rows, tile * lanes : (tile + 1) * lanes
                    ]

    def correlate_level(q):
        size = plan.level_rows
        correlate(0, (q + 1) * size, q * size, size)
        if q >= 2:
            correlate(q * size, size, 0, 2 * size)
        if q % 2:
            correlate(q * size, size, (q - 1) * size, size)

    def from_gram(u, part, d):
        row_tiles, seg, seg_rows, lane, lanes = plan.units[u]
        return jnp.concatenate(
            [
                gram[part, tiles[d], r * cols + seg : r * cols + seg + seg_rows, lane : lane + lanes]
                for r in row_tiles
            ],
            axis=0,
        )

    def send_pair(u):
        lanes = plan.units[u][4]
        for j, d in enumerate(odds):
            for part in (0, 1):
                stage_a[u][part, :, j * lanes : (j + 1) * lanes] = from_gram(u, part, d).astype(jnp.bfloat16)
        a_copy(u).start()

    def sum_pair(u):
        lanes = plan.units[u][4]
        a_copy(u).wait_recv()
        for j, d in enumerate(evens):
            if d:
                for part in (0, 1):
                    theirs = landed_a[u][part, :, j * lanes : (j + 1) * lanes].astype(jnp.float32)
                    stage_b[u][d // 2 - 1, part] = (from_gram(u, part, d) + theirs).astype(jnp.bfloat16)
        for d in evens:
            if d:
                b_copy(u, d).start()

    def sum_rest(u):
        total_rows, lanes = plan.unit_shape(u)
        piece = total_rows // nf
        for d in evens:
            if d:
                b_copy(u, d).wait_recv()
        j = len(evens) - 1
        for part in (0, 1):
            total = from_gram(u, part, 0) + landed_a[u][part, :, j * lanes : (j + 1) * lanes].astype(jnp.float32)
            for d in evens:
                if d:
                    total = total + landed_b[u][d // 2 - 1, part].astype(jnp.float32)
            total = total.astype(jnp.bfloat16)
            for p in range(nf):
                first_src[u][p, part] = total[p * piece : (p + 1) * piece]
        mid[u][f] = first_src[u][f]
        for k in masks:
            first_copy(u, k).start()

    def source_of(slot):
        wanted = corr_channels[slot]
        source = 0
        for s in range(nf):
            source = jnp.where(beam_channels[s] == wanted, s, source)
        return source

    def hand_on(u):
        for k in masks:
            first_copy(u, k).wait_recv()
        for k in masks:
            second_src[u][k - 1] = mid[u][source_of(peers[k])]
        landed[u][f] = mid[u][source_of(f)]
        for k in masks:
            second_copy(u, k).start()

    def relay(ci):
        for k in masks:
            z_copy(k, ci).wait_recv()
            forward(k, ci)
        send_chunk(ci + ahead)

    def await_level(q):
        own_copies[q].wait()
        for ci in (2 * q, 2 * q + 1):
            for k in range(nf):
                for dg in range(1, ng):
                    y_copy(k, ci, dg).wait_recv()

    last = plan.levels - 1
    early_units = [0] if last else []
    late_units = [u for u in range(nu) if u not in early_units]
    for q in range(plan.levels):
        relay(2 * q)
        if q:
            await_level(q - 1)
            correlate_level(q - 1)
            if q == last:
                for u in early_units:
                    send_pair(u)
        relay(2 * q + 1)
        if q == last:
            for u in early_units:
                sum_pair(u)
    await_level(last)
    correlate_level(last)
    for u in late_units:
        send_pair(u)
    for u in early_units:
        sum_rest(u)

    for k in masks:
        prior_copy(k).wait_recv()
    slot_of_mine = 0
    for k in range(nf):
        slot_of_mine = jnp.where(corr_channels[k] == my_beam, k, slot_of_mine)
    z[...] = reorder(priors[slot_of_mine], to_held)
    slot = g * nt + t
    strip = LANES
    per_tile = cols // LANES

    def update_copy(iteration, o):
        dt, dg = offsets[o]
        return pltpu.make_async_remote_copy(
            src_ref=updates.at[iteration, slot],
            dst_ref=updates.at[iteration, slot],
            send_sem=us.at[iteration, o],
            recv_sem=ur.at[iteration, o],
            device_id=group(dt, dg),
            device_id_type=MESH,
        )

    beside = {i: [] for i in range(ITERS + 1)}

    def plan_work(iteration, work, u):
        beside[min(iteration, ITERS)].append(functools.partial(work, u))

    for u in early_units:
        plan_work(1, hand_on, u)
    for i, u in enumerate(late_units):
        plan_work(i // 2, sum_pair, u)
        plan_work(i // 2 + 1, sum_rest, u)
        plan_work(i // 2 + 2, hand_on, u)
    for iteration in range(ITERS):
        power = jnp.sum(z[...] * z[...]) + 1e-06

        def product(r, carry):
            here = pl.ds(pl.multiple_of(r * strip, strip), strip)
            total_r = jnp.zeros((strip, LANES), jnp.float32)
            total_i = jnp.zeros((strip, LANES), jnp.float32)
            for c in range(inputs // LANES):
                lanes = slice(c * LANES, (c + 1) * LANES)
                tile, inner = c // per_tile, slice(c % per_tile * LANES, (c % per_tile + 1) * LANES)
                part_r = gram[0, tile, here, inner]
                part_i = gram[1, tile, here, inner]
                gain_r = z[0:1, lanes]
                gain_i = z[1:2, lanes]
                total_r += part_r * gain_r - part_i * gain_i
                total_i += part_i * gain_r + part_r * gain_i
            updates[iteration, slot, 0:1, here] = jnp.sum(total_r.T, axis=0, keepdims=True)
            updates[iteration, slot, 1:2, here] = jnp.sum(total_i.T, axis=0, keepdims=True)
            return carry

        lax.fori_loop(0, rows // strip, product, 0)
        for o in range(len(offsets)):
            update_copy(iteration, o).start()
        for work in beside[iteration]:
            work()
        for o in range(len(offsets)):
            update_copy(iteration, o).wait_recv()
        for h in range(ng):
            total = updates[iteration, h * nt]
            for other in range(1, nt):
                total = total + updates[iteration, h * nt + other]
            lanes = slice(h * rows, (h + 1) * rows)
            z[:, lanes] = 0.5 * (z[:, lanes] + inputs * total / power)

    gains[f] = reorder(z[...], to_natural)

    def gain_copy(k):
        return pltpu.make_async_remote_copy(
            src_ref=gains.at[f],
            dst_ref=gains.at[f],
            send_sem=gs.at[k - 1],
            recv_sem=gr.at[k - 1],
            device_id=along_freq(k),
            device_id_type=MESH,
        )

    factor = 1.0 / math.sqrt(stations)
    for p in (0, 1):
        gain_r = z[0:1, p * stations : (p + 1) * stations]
        gain_i = z[1:2, p * stations : (p + 1) * stations]
        denom = jnp.maximum(gain_r * gain_r + gain_i * gain_i, 0.5)
        along_r = gain_r / denom
        along_i = gain_i / denom
        cos = cosine[...]
        sin = sine[...]
        w_r = ((cos * along_r - sin * along_i) * factor).astype(jnp.bfloat16)
        w_i = (-(cos * along_i + sin * along_r) * factor).astype(jnp.bfloat16)
        left[p, 0:beams] = w_r
        left[p, beams:] = w_i
        right[p, 0:beams] = -w_i
        right[p, beams:] = w_r
    for k in masks:
        gain_copy(k).start()

    beam_copies = [
        pltpu.make_async_copy(beams_out.at[:, p], beams_hbm.at[:, p], out_sem.at[p]) for p in (0, 1)
    ]

    def beamform(p):
        rows_p = slice(p * stations, (p + 1) * stations)
        result = jnp.dot(left[p], corr[0, rows_p, :], preferred_element_type=jnp.float32)
        result = result + jnp.dot(right[p], corr[1, rows_p, :], preferred_element_type=jnp.float32)
        result = result.astype(jnp.bfloat16)
        beams_out[0, p, 0] = result[:beams]
        beams_out[0, p, 1] = result[beams:]

    for work in beside[ITERS]:
        work()
    for p in (0, 1):
        beamform(p)
        beam_copies[p].start()

    for k in masks:
        gain_copy(k).wait_recv()
    gains_out[0] = gains[source_of(f)]

    for u in range(nu):
        for k in masks:
            second_copy(u, k).wait_recv()
    vis_copies = [pltpu.make_async_copy(vis_out.at[:, part], vis_hbm.at[:, part], out_sem.at[2 + part]) for part in (0, 1)]
    for part in (0, 1):
        strips = [
            jnp.concatenate([landed[u][p, part] for p in range(nf)], axis=0) for u in range(nu)
        ]
        for r in range(plan.row_tiles):
            most = plan.units[0][2]
            here = slice(r * most, (r + 1) * most)
            if permuted:
                tile_rows = [
                    jnp.concatenate([strips[0][here], strips[1 + r]], axis=1),
                    strips[-1][r * plan.level_rows : (r + 1) * plan.level_rows],
                ]
            else:
                tile_rows = [jnp.concatenate([strips[0][here], strips[1][here]], axis=1)]
            tile = jnp.concatenate(tile_rows, axis=0)
            if not permuted:
                vis_out[0, part, r * cols : (r + 1) * cols, :] = tile
                continue
            tile = jnp.dot(
                tile, to_natural[...].astype(jnp.bfloat16), preferred_element_type=jnp.float32
            ).astype(jnp.bfloat16)
            for start, size, target in plan.segments:
                vis_out[0, part, r * cols + target : r * cols + target + size, :] = tile[start : start + size]
    for copy in vis_copies:
        copy.start()

    for k in masks:
        prior_copy(k).wait_send()
        gain_copy(k).wait_send()
    for ci in all_chunks:
        for k in masks:
            z_copy(k, ci).wait_send()
        for k in range(nf):
            for dg in range(1, ng):
                y_copy(k, ci, dg).wait_send()
    for u in range(nu):
        a_copy(u).wait_send()
        for d in evens:
            if d:
                b_copy(u, d).wait_send()
        for k in masks:
            first_copy(u, k).wait_send()
            second_copy(u, k).wait_send()
    for iteration in range(ITERS):
        for o in range(len(offsets)):
            update_copy(iteration, o).wait_send()
    for copy in beam_copies + vis_copies:
        copy.wait()


def body(
    voltages,
    prior_gains,
    station_flags,
    ingest_map,
    station_coords,
    pointing,
    corr_channels,
    beam_channels,
):
    nf = lax.axis_size("freq")
    nt = lax.axis_size("tm")
    ng = lax.axis_size("grp")
    _, _, per_input, samples = voltages.shape
    stations = ingest_map.shape[0]
    plan = Plan(nf, nt, ng, per_input, samples)
    inputs, rows, cols = plan.inputs, plan.rows, plan.cols
    part_beams = pointing.shape[1] // ng
    nc, nu = len(plan.chunks), len(plan.units)
    pairs = nt // 2
    dma = pltpu.SemaphoreType.DMA
    vmem = pl.BlockSpec(memory_space=pltpu.VMEM)
    hbm = pl.BlockSpec(memory_space=pltpu.HBM)
    shapes = [plan.unit_shape(u) for u in range(nu)]

    def bf16(*shape):
        return pltpu.VMEM(shape, jnp.bfloat16)

    def f32(*shape):
        return pltpu.VMEM(shape, jnp.float32)

    vis, gains, beams = pl.pallas_call(
        functools.partial(kernel, plan),
        out_shape=(
            jax.ShapeDtypeStruct((1, 2, rows, cols), jnp.bfloat16),
            jax.ShapeDtypeStruct((1, 2, inputs), jnp.float32),
            jax.ShapeDtypeStruct((1, 2, 2, part_beams, samples), jnp.bfloat16),
        ),
        in_specs=[hbm] * 8,
        out_specs=(hbm, vmem, hbm),
        scratch_shapes=[
            bf16(nf, 2, per_input, samples),
            bf16(2, inputs, samples),
            f32(stations, LANES),
            f32(part_beams, stations),
            f32(part_beams, stations),
            f32(cols, cols),
            f32(cols, cols),
            bf16(2, 2 * part_beams, stations),
            bf16(2, 2 * part_beams, stations),
            bf16(1, 2, 2, part_beams, samples),
            bf16(1, 2, rows, cols),
            f32(2, nt, rows, cols),
            f32(nf, 2, inputs),
            f32(ITERS, ng * nt, 2, rows),
            f32(2, inputs),
            f32(nf, 2, inputs),
        ]
        + [bf16(2, r, pairs * w) for r, w in shapes] * 2
        + [bf16(pairs - 1, 2, r, w) for r, w in shapes] * 2
        + [bf16(nf, 2, r // nf, w) for r, w in shapes] * 2
        + [bf16(nf - 1, 2, r // nf, w) for r, w in shapes]
        + [bf16(nf, 2, r // nf, w) for r, w in shapes]
        + [
            dma((nf - 1, nc)),
            dma((nf - 1, nc)),
            dma((ng - 1, nf, nc)),
            dma((ng - 1, nf, nc)),
            dma((plan.levels,)),
            dma((nf - 1,)),
            dma((nf - 1,)),
            dma((ITERS, ng * nt - 1)),
            dma((ITERS, ng * nt - 1)),
            dma((nf - 1,)),
            dma((nf - 1,)),
            dma((nu,)),
            dma((nu,)),
            dma((nu, pairs - 1)),
            dma((nu, pairs - 1)),
            dma((nu, nf - 1)),
            dma((nu, nf - 1)),
            dma((nu, nf - 1)),
            dma((nu, nf - 1)),
            dma((4,)),
            dma((8,)),
            pltpu.VMEM(voltages.shape, jnp.bfloat16),
            pltpu.VMEM(prior_gains.shape, jnp.float32),
            pltpu.VMEM((1, stations), jnp.int32),
            pltpu.VMEM((1, stations), jnp.int32),
            pltpu.VMEM(station_coords.shape, jnp.float32),
            pltpu.VMEM(pointing.shape, jnp.int32),
            pltpu.SMEM(corr_channels.shape, jnp.int32),
            pltpu.SMEM(beam_channels.shape, jnp.int32),
        ],
        compiler_params=pltpu.CompilerParams(
            collective_id=0, has_side_effects=True, vmem_limit_bytes=67043328
        ),
    )(
        voltages,
        prior_gains,
        station_flags[None],
        ingest_map[None],
        station_coords,
        pointing,
        corr_channels,
        beam_channels,
    )
    return vis.astype(jnp.float32), gains, beams


def solution(mesh):
    return jax.shard_map(
        body,
        mesh=mesh,
        in_specs=(
            P(None, None, ("freq", "grp"), "tm"),
            P("freq", None, None),
            P(),
            P(),
            P(),
            P(),
            P(),
            P(),
        ),
        out_specs=(
            P("freq", None, "grp", "tm"),
            P("freq", None, None),
            P("freq", None, None, "grp", "tm"),
        ),
        check_vma=False,
    )
```

```python
import functools
import math

import jax
import jax.numpy as jnp
from jax import lax
from jax.experimental import pallas as pl
from jax.experimental.pallas import tpu as pltpu
from jax.sharding import PartitionSpec as P

ITERS = 4
LANES = 128
grid_cells = 64.0
MESH = pl.DeviceIdType.MESH


def partner(index, mask, count):
    result, bit = 0, 1
    while bit < count:
        digit = (index // bit) % 2
        result = result + bit * ((1 - digit) if mask & bit else digit)
        bit *= 2
    return result


def nt_dot(a, b):
    return lax.dot_general(a, b, (((1,), (1,)), ((), ())), preferred_element_type=jnp.float32)


class Plan:
    def __init__(self, nf, nt, ng, per_input, samples):
        self.nf, self.nt, self.ng = nf, nt, ng
        self.per_input, self.samples = per_input, samples
        self.inputs = nf * ng * per_input
        self.rows = self.inputs // ng
        self.cols = self.inputs // nt
        self.blocks = self.cols // per_input
        self.row_tiles = nt // ng
        self.levels = 4 if per_input % 64 == 0 else 1
        self.step = per_input // self.levels
        self.level_rows = self.cols // self.levels
        count = 16 if self.step % 16 == 0 else self.step
        self.chunks = tuple((part, first, count) for first in range(0, per_input, count) for part in (0, 1))
        half, tiles = self.cols // 2, tuple(range(self.row_tiles))
        if self.levels > 1:
            most = self.cols - self.level_rows
            units = [((r,), 0, most, lane, half) for lane in (0, half) for r in tiles]
            units += [(tiles, most, self.level_rows, 0, self.cols)]
        else:
            units = [(tiles, 0, self.cols, 0, half), (tiles, 0, self.cols, half, half)]
        self.units = tuple(units)
        self.segments = tuple(
            (q * self.level_rows + b * self.step, self.step, b * per_input + q * self.step)
            for q in range(self.levels)
            for b in range(self.blocks)
        )

    def unit_shape(self, unit):
        tiles, _, seg_rows, _, lanes = self.units[unit]
        return len(tiles) * seg_rows, lanes


def kernel(plan, *refs):
    nf, nt, ng = plan.nf, plan.nt, plan.ng
    nu = len(plan.units)
    operands, refs = refs[:8], refs[8:]
    vis_hbm, gains_hbm, beams_hbm = refs[:3]
    refs = refs[3:]

    def take(count):
        nonlocal refs
        taken, refs = refs[:count], refs[count:]
        return taken

    src, corr, keep, cosine, sine, to_held, to_natural, left, right, beams_out, vis_out, gains_out, gram = take(13)
    priors, updates, z, gains = take(4)
    stage_a, landed_a, stage_b, landed_b = (take(nu) for _ in range(4))
    first_src, mid, second_src, landed = (take(nu) for _ in range(4))
    zs, zr, ys, yr, own_sem, qs, qr, us, ur, gs, gr, as_, ar, bs, br, fs, fr, ss, sr, out_sem, in_sem = take(21)
    held = refs
    voltages, prior, flags, slots, coords, pointing, corr_channels, beam_channels = held
    loads = [pltpu.make_async_copy(operands[i], held[i], in_sem.at[i]) for i in range(8)]
    for load in loads:
        load.start()
    f = lax.axis_index("freq")
    t = lax.axis_index("tm")
    g = lax.axis_index("grp")
    per_input, samples = plan.per_input, plan.samples
    inputs, rows, cols = plan.inputs, plan.rows, plan.cols
    stations = inputs // 2
    chunks = plan.chunks
    offsets = [(dt, dg) for dg in range(ng) for dt in range(nt) if (dt, dg) != (0, 0)]
    masks = list(range(nf - 1, 0, -1))
    peers = {k: partner(f, k, nf) for k in range(nf)}
    tiles = {d: partner(t, d, nt) for d in range(nt)}

    def group(dt, dg):
        return {"freq": f, "tm": (t + dt) % nt, "grp": (g + dg) % ng}

    def along_freq(k):
        return {"freq": peers[k], "tm": t, "grp": g}

    def along_tm(d):
        return {"freq": f, "tm": tiles[d], "grp": g}

    def await_all(ref, sem):
        pltpu.make_async_copy(ref, ref, sem).wait()

    barrier = pltpu.get_barrier_semaphore()
    for k in masks:
        pl.semaphore_signal(barrier, inc=1, device_id=along_freq(k), device_id_type=MESH)
    for dt, dg in offsets:
        pl.semaphore_signal(barrier, inc=1, device_id=group(dt, dg), device_id_type=MESH)
    for load in loads:
        load.wait()

    slot_rows = jnp.broadcast_to(slots[...].astype(jnp.float32), (LANES, stations)).T
    flagged = jnp.zeros((stations, LANES), jnp.float32)
    for first in range(0, stations, LANES):
        lane = lax.broadcasted_iota(jnp.int32, (stations, LANES), 1) + first
        flag = flags[0:1, first : first + LANES].astype(jnp.float32)
        flagged += jnp.where(slot_rows == lane.astype(jnp.float32), flag, 0.0)
    flagged = jnp.sum(flagged, axis=1, keepdims=True)
    keep[...] = jnp.broadcast_to(1.0 - flagged, (stations, LANES))
    first_slot = pl.multiple_of(((f * ng + g) * per_input) % stations, per_input)
    kept = keep[pl.ds(first_slot, per_input), 0:1].astype(jnp.bfloat16)

    for k in masks + [0]:
        for part in (0, 1):
            src[peers[k], part] = voltages[beam_channels[peers[k]], part] * kept

    pl.semaphore_wait(barrier, len(masks) + len(offsets))

    def held_start(owner, member, first):
        block = owner * ng + member
        level = first // plan.step
        start = (block // plan.blocks) * cols + level * plan.level_rows + (block % plan.blocks) * plan.step
        return pl.multiple_of(start + first % plan.step, math.gcd(plan.step, 16))

    def place(owner, chunk):
        part, first, count = chunk
        return corr.at[part, pl.ds(held_start(owner, g, first), count), :]

    def z_copy(k, ci):
        part, first, count = chunks[ci]
        return pltpu.make_async_remote_copy(
            src_ref=src.at[peers[k], part, pl.ds(first, count), :],
            dst_ref=place(f, chunks[ci]),
            send_sem=zs,
            recv_sem=zr.at[k - 1, ci],
            device_id=along_freq(k),
            device_id_type=MESH,
        )

    def y_copy(k, ci, dg):
        part, first, count = chunks[ci]
        spot = place(peers[k], chunks[ci])
        return pltpu.make_async_remote_copy(
            src_ref=src.at[f, part, pl.ds(first, count), :] if k == 0 else spot,
            dst_ref=spot,
            send_sem=ys.at[dg - 1],
            recv_sem=yr.at[first // plan.step],
            device_id=group(0, dg),
            device_id_type=MESH,
        )

    def forward(k, ci):
        for dg in range(1, ng):
            y_copy(k, ci, dg).start()

    own_copies = [
        pltpu.make_async_copy(
            src.at[f, :, pl.ds(first, plan.step), :],
            corr.at[:, pl.ds(held_start(f, g, first), plan.step), :],
            own_sem.at[first // plan.step],
        )
        for first in range(0, per_input, plan.step)
    ]

    def prior_copy(k):
        return pltpu.make_async_remote_copy(
            src_ref=prior.at[0],
            dst_ref=priors.at[f],
            send_sem=qs,
            recv_sem=qr,
            device_id=along_freq(k),
            device_id_type=MESH,
        )

    all_chunks = range(len(chunks))
    ahead = 2

    def send_chunk(ci):
        if ci < len(chunks):
            for k in masks:
                z_copy(k, ci).start()

    for ci in range(ahead):
        send_chunk(ci)
        if ci == 0:
            for k in masks:
                prior_copy(k).start()
    for ci in all_chunks:
        forward(0, ci)
    for copy in own_copies:
        copy.start()
    priors[f] = prior[0]

    n_beams = pointing.shape[1]
    beams = n_beams // ng
    my_beam = beam_channels[f]
    permuted = plan.levels > 1

    def natural(held_index):
        result = held_index
        for start, size, target in plan.segments:
            inside = (held_index >= start) & (held_index < start + size)
            result = jnp.where(inside, held_index + (target - start), result)
        return result

    if permuted:
        along_rows = lax.broadcasted_iota(jnp.int32, (cols, cols), 0)
        along_lanes = lax.broadcasted_iota(jnp.int32, (cols, cols), 1)
        to_held[...] = jnp.where(natural(along_lanes) == along_rows, 1.0, 0.0)
        to_natural[...] = jnp.where(natural(along_rows) == along_lanes, 1.0, 0.0)

    def reorder(row_vector, matrix):
        if not permuted:
            return row_vector
        moved = [
            jnp.dot(
                row_vector[:, first : first + cols],
                matrix[...],
                precision=lax.Precision.HIGHEST,
                preferred_element_type=jnp.float32,
            )
            for first in range(0, row_vector.shape[1], cols)
        ]
        return jnp.concatenate(moved, axis=1)

    def point_phases():
        ratio = 0.875 + 0.25 * (my_beam.astype(jnp.float32) + 0.5) / nf
        mine = pl.ds(pl.multiple_of(g * beams, beams), beams)
        east_dir, north_dir = (
            jnp.broadcast_to((pointing[d : d + 1, mine].astype(jnp.float32) + 0.5) / grid_cells - 0.5, (LANES, beams)).T
            for d in (0, 1)
        )
        east, north = (jnp.broadcast_to(coords[d : d + 1, :], (LANES, stations)).T for d in (0, 1))
        station = lax.broadcasted_iota(jnp.int32, (stations, LANES), 0)
        slot_east, slot_north = [], []
        for first in range(0, stations, LANES):
            lanes = slice(first, first + LANES)
            match = station == slots[0:1, lanes]
            slot_east.append(jnp.sum(jnp.where(match, east, 0.0), axis=0, keepdims=True))
            slot_north.append(jnp.sum(jnp.where(match, north, 0.0), axis=0, keepdims=True))
        where = jnp.concatenate(
            [jnp.concatenate(slot_east, axis=1), jnp.concatenate(slot_north, axis=1)] * 4, axis=0
        )
        where = reorder(where, to_held)
        for first in range(0, stations, LANES):
            lanes = slice(first, first + LANES)
            phase = 2.0 * math.pi * ratio * (east_dir * where[0:1, lanes] + north_dir * where[1:2, lanes])
            cosine[:, lanes] = jnp.cos(phase)
            sine[:, lanes] = jnp.sin(phase)

    point_phases()

    scale = 1.0 / (samples * nt)
    odds = list(range(nt - 1, 0, -2))
    evens = [d - 1 for d in odds]

    def a_copy(u):
        return pltpu.make_async_remote_copy(
            src_ref=stage_a[u],
            dst_ref=landed_a[u],
            send_sem=as_.at[u],
            recv_sem=ar.at[u],
            device_id=along_tm(1),
            device_id_type=MESH,
        )

    def b_copy(u, d):
        return pltpu.make_async_remote_copy(
            src_ref=stage_b[u].at[d // 2 - 1],
            dst_ref=landed_b[u].at[d // 2 - 1],
            send_sem=bs.at[u, d // 2 - 1],
            recv_sem=br.at[u, d // 2 - 1],
            device_id=along_tm(d),
            device_id_type=MESH,
        )

    def first_copy(u, k):
        return pltpu.make_async_remote_copy(
            src_ref=first_src[u].at[peers[k]],
            dst_ref=mid[u].at[f],
            send_sem=fs.at[u],
            recv_sem=fr.at[u],
            device_id=along_freq(k),
            device_id_type=MESH,
        )

    def second_copy(u, k):
        return pltpu.make_async_remote_copy(
            src_ref=second_src[u].at[k - 1],
            dst_ref=landed[u].at[f],
            send_sem=ss.at[u],
            recv_sem=sr.at[u],
            device_id=along_freq(k),
            device_id_type=MESH,
        )

    def correlate(seg, seg_rows, lane, lanes):
        def stacked(part):
            pieces = []
            for r in range(plan.row_tiles):
                start = pl.multiple_of(g * rows + r * cols + seg, plan.level_rows)
                pieces.append(corr[part, pl.ds(start, seg_rows), :])
            return pieces

        mine = jnp.concatenate(stacked(0) + stacked(1), axis=0)
        count = plan.row_tiles * seg_rows
        others = [
            jnp.concatenate(
                [corr[part, tile * cols + lane : tile * cols + lane + lanes, :] for tile in range(nt)], axis=0
            )
            for part in (0, 1)
        ]
        with_r = nt_dot(mine, others[0])
        with_i = nt_dot(mine, others[1])
        real = (with_r[:count] + with_i[count:]) * scale
        imag = (with_r[count:] - with_i[:count]) * scale
        for part, value in ((0, real), (1, imag)):
            for tile in range(nt):
                for r in range(plan.row_tiles):
                    gram[part, tile, r * cols + seg : r * cols + seg + seg_rows, lane : lane + lanes] = value[
                        r * seg_rows : (r + 1) * seg_rows, tile * lanes : (tile + 1) * lanes
                    ]

    def correlate_level(q):
        size = plan.level_rows
        correlate(0, (q + 1) * size, q * size, size)
        if q >= 2:
            correlate(q * size, size, 0, 2 * size)
        if q % 2:
            correlate(q * size, size, (q - 1) * size, size)

    def from_gram(u, part, d):
        row_tiles, seg, seg_rows, lane, lanes = plan.units[u]
        return jnp.concatenate(
            [
                gram[part, tiles[d], r * cols + seg : r * cols + seg + seg_rows, lane : lane + lanes]
                for r in row_tiles
            ],
            axis=0,
        )

    def send_pair(u):
        lanes = plan.units[u][4]
        for j, d in enumerate(odds):
            for part in (0, 1):
                stage_a[u][part, :, j * lanes : (j + 1) * lanes] = from_gram(u, part, d).astype(jnp.bfloat16)
        a_copy(u).start()

    def sum_pair(u):
        lanes = plan.units[u][4]
        a_copy(u).wait_recv()
        for j, d in enumerate(evens):
            if d:
                for part in (0, 1):
                    theirs = landed_a[u][part, :, j * lanes : (j + 1) * lanes].astype(jnp.float32)
                    stage_b[u][d // 2 - 1, part] = (from_gram(u, part, d) + theirs).astype(jnp.bfloat16)
        for d in evens:
            if d:
                b_copy(u, d).start()

    def sum_rest(u):
        total_rows, lanes = plan.unit_shape(u)
        piece = total_rows // nf
        for d in evens:
            if d:
                b_copy(u, d).wait_recv()
        j = len(evens) - 1
        for part in (0, 1):
            total = from_gram(u, part, 0) + landed_a[u][part, :, j * lanes : (j + 1) * lanes].astype(jnp.float32)
            for d in evens:
                if d:
                    total = total + landed_b[u][d // 2 - 1, part].astype(jnp.float32)
            total = total.astype(jnp.bfloat16)
            for p in range(nf):
                first_src[u][p, part] = total[p * piece : (p + 1) * piece]
        mid[u][f] = first_src[u][f]
        for k in masks:
            first_copy(u, k).start()

    def source_of(slot):
        wanted = corr_channels[slot]
        source = 0
        for s in range(nf):
            source = jnp.where(beam_channels[s] == wanted, s, source)
        return source

    def hand_on(u):
        await_all(mid[u].at[pl.ds(0, nf - 1)], fr.at[u])
        for k in masks:
            second_src[u][k - 1] = mid[u][source_of(peers[k])]
        landed[u][f] = mid[u][source_of(f)]
        for k in masks:
            second_copy(u, k).start()

    nearest_first = [1] + masks[:-1] if nf > 1 else []

    def relay(ci):
        for k in nearest_first:
            z_copy(k, ci).wait_recv()
            forward(k, ci)
        send_chunk(ci + ahead)

    def of_level(q):
        return [ci for ci in all_chunks if chunks[ci][1] // plan.step == q]

    def await_level(q):
        own_copies[q].wait()
        await_all(corr.at[:, pl.ds(0, (ng - 1) * nf * plan.step), :], yr.at[q])

    last = plan.levels - 1
    early_units = list(range(plan.row_tiles)) if last else []
    late_units = [u for u in range(nu) if u not in early_units]
    for q in range(plan.levels):
        members = of_level(q)
        relay(members[0])
        if q:
            await_level(q - 1)
            correlate_level(q - 1)
        if q == last:
            for u in early_units:
                send_pair(u)
        relay(members[1])
        if q == last:
            for u in early_units:
                sum_pair(u)
        for ci in members[2:]:
            relay(ci)
    for u in early_units:
        sum_rest(u)
    await_level(last)
    correlate_level(last)
    for u in late_units:
        send_pair(u)

    await_all(priors.at[pl.ds(0, nf - 1)], qr)
    slot_of_mine = 0
    for k in range(nf):
        slot_of_mine = jnp.where(corr_channels[k] == my_beam, k, slot_of_mine)
    z[...] = reorder(priors[slot_of_mine], to_held)
    slot = g * nt + t
    strip = LANES
    per_tile = cols // LANES

    def update_copy(iteration, o):
        dt, dg = offsets[o]
        return pltpu.make_async_remote_copy(
            src_ref=updates.at[iteration, slot],
            dst_ref=updates.at[iteration, slot],
            send_sem=us,
            recv_sem=ur.at[iteration],
            device_id=group(dt, dg),
            device_id_type=MESH,
        )

    beside = {i: [] for i in range(ITERS + 1)}

    def plan_work(iteration, work, u):
        beside[min(iteration, ITERS)].append(functools.partial(work, u))

    for i, u in enumerate(late_units):
        plan_work(i // 2, sum_pair, u)
    for i, u in enumerate(late_units):
        plan_work(i // 2 + 1, sum_rest, u)
    for u in early_units:
        plan_work(0, hand_on, u)
    for i, u in enumerate(late_units):
        plan_work(i // 2 + 2, hand_on, u)
    for iteration in range(ITERS):
        power = jnp.sum(z[...] * z[...]) + 1e-06

        def product(r, carry):
            here = pl.ds(pl.multiple_of(r * strip, strip), strip)
            total_r = jnp.zeros((strip, LANES), jnp.float32)
            total_i = jnp.zeros((strip, LANES), jnp.float32)
            for c in range(inputs // LANES):
                lanes = slice(c * LANES, (c + 1) * LANES)
                tile, inner = c // per_tile, slice(c % per_tile * LANES, (c % per_tile + 1) * LANES)
                part_r = gram[0, tile, here, inner]
                part_i = gram[1, tile, here, inner]
                gain_r = z[0:1, lanes]
                gain_i = z[1:2, lanes]
                total_r += part_r * gain_r - part_i * gain_i
                total_i += part_i * gain_r + part_r * gain_i
            updates[iteration, slot, 0:1, here] = jnp.sum(total_r.T, axis=0, keepdims=True)
            updates[iteration, slot, 1:2, here] = jnp.sum(total_i.T, axis=0, keepdims=True)
            return carry

        lax.fori_loop(0, rows // strip, product, 0)
        for o in range(len(offsets)):
            update_copy(iteration, o).start()
        for work in beside[iteration]:
            work()
        await_all(updates.at[iteration, pl.ds(0, len(offsets))], ur.at[iteration])
        for h in range(ng):
            total = updates[iteration, h * nt]
            for other in range(1, nt):
                total = total + updates[iteration, h * nt + other]
            lanes = slice(h * rows, (h + 1) * rows)
            z[:, lanes] = 0.5 * (z[:, lanes] + inputs * total / power)

    gains[f] = reorder(z[...], to_natural)

    def gain_copy(k):
        return pltpu.make_async_remote_copy(
            src_ref=gains.at[f],
            dst_ref=gains.at[f],
            send_sem=gs,
            recv_sem=gr,
            device_id=along_freq(k),
            device_id_type=MESH,
        )

    factor = 1.0 / math.sqrt(stations)
    for p in (0, 1):
        gain_r = z[0:1, p * stations : (p + 1) * stations]
        gain_i = z[1:2, p * stations : (p + 1) * stations]
        denom = jnp.maximum(gain_r * gain_r + gain_i * gain_i, 0.5)
        along_r = gain_r / denom
        along_i = gain_i / denom
        cos = cosine[...]
        sin = sine[...]
        w_r = ((cos * along_r - sin * along_i) * factor).astype(jnp.bfloat16)
        w_i = (-(cos * along_i + sin * along_r) * factor).astype(jnp.bfloat16)
        left[p, 0:beams] = w_r
        left[p, beams:] = w_i
        right[p, 0:beams] = -w_i
        right[p, beams:] = w_r
    for k in masks:
        gain_copy(k).start()

    beam_copies = [
        pltpu.make_async_copy(beams_out.at[:, p], beams_hbm.at[:, p], out_sem.at[p]) for p in (0, 1)
    ]

    def beamform(p):
        rows_p = slice(p * stations, (p + 1) * stations)
        result = jnp.dot(left[p], corr[0, rows_p, :], preferred_element_type=jnp.float32)
        result = result + jnp.dot(right[p], corr[1, rows_p, :], preferred_element_type=jnp.float32)
        result = result.astype(jnp.bfloat16)
        beams_out[0, p, 0] = result[:beams]
        beams_out[0, p, 1] = result[beams:]

    for work in beside[ITERS]:
        work()
    for p in (0, 1):
        beamform(p)
        beam_copies[p].start()

    await_all(gains.at[pl.ds(0, nf - 1)], gr)
    gains_out[0] = gains[source_of(f)]
    gains_write = pltpu.make_async_copy(gains_out, gains_hbm, out_sem.at[4])
    gains_write.start()

    for u in range(nu):
        await_all(landed[u].at[pl.ds(0, nf - 1)], sr.at[u])
    vis_copies = [pltpu.make_async_copy(vis_out.at[:, part], vis_hbm.at[:, part], out_sem.at[2 + part]) for part in (0, 1)]
    for part in (0, 1):
        strips = [
            jnp.concatenate([landed[u][p, part] for p in range(nf)], axis=0) for u in range(nu)
        ]
        for r in range(plan.row_tiles):
            here = slice(r * cols, (r + 1) * cols)
            if permuted:
                tile_rows = [
                    jnp.concatenate([strips[r], strips[plan.row_tiles + r]], axis=1),
                    strips[-1][r * plan.level_rows : (r + 1) * plan.level_rows],
                ]
            else:
                tile_rows = [jnp.concatenate([strips[0][here], strips[1][here]], axis=1)]
            tile = jnp.concatenate(tile_rows, axis=0)
            if not permuted:
                vis_out[0, part, r * cols : (r + 1) * cols, :] = tile
                continue
            tile = jnp.dot(
                tile, to_natural[...].astype(jnp.bfloat16), preferred_element_type=jnp.float32
            ).astype(jnp.bfloat16)
            for start, size, target in plan.segments:
                vis_out[0, part, r * cols + target : r * cols + target + size, :] = tile[start : start + size]
    for copy in vis_copies:
        copy.start()

    await_all(priors.at[pl.ds(0, nf - 1)], qs)
    await_all(gains.at[pl.ds(0, nf - 1)], gs)
    await_all(src.at[pl.ds(0, nf - 1)], zs)
    for dg in range(1, ng):
        await_all(src, ys.at[dg - 1])
    for u in range(nu):
        a_copy(u).wait_send()
        for d in evens:
            if d:
                b_copy(u, d).wait_send()
        await_all(mid[u].at[pl.ds(0, nf - 1)], fs.at[u])
        await_all(landed[u].at[pl.ds(0, nf - 1)], ss.at[u])
    await_all(updates.at[:, pl.ds(0, len(offsets))], us)
    for copy in beam_copies + vis_copies + [gains_write]:
        copy.wait()


def body(
    voltages,
    prior_gains,
    station_flags,
    ingest_map,
    station_coords,
    pointing,
    corr_channels,
    beam_channels,
):
    nf = lax.axis_size("freq")
    nt = lax.axis_size("tm")
    ng = lax.axis_size("grp")
    _, _, per_input, samples = voltages.shape
    stations = ingest_map.shape[0]
    plan = Plan(nf, nt, ng, per_input, samples)
    inputs, rows, cols = plan.inputs, plan.rows, plan.cols
    part_beams = pointing.shape[1] // ng
    nc, nu = len(plan.chunks), len(plan.units)
    pairs = nt // 2
    dma = pltpu.SemaphoreType.DMA
    hbm = pl.BlockSpec(memory_space=pltpu.HBM)
    shapes = [plan.unit_shape(u) for u in range(nu)]

    def bf16(*shape):
        return pltpu.VMEM(shape, jnp.bfloat16)

    def f32(*shape):
        return pltpu.VMEM(shape, jnp.float32)

    vis, gains, beams = pl.pallas_call(
        functools.partial(kernel, plan),
        out_shape=(
            jax.ShapeDtypeStruct((1, 2, rows, cols), jnp.bfloat16),
            jax.ShapeDtypeStruct((1, 2, inputs), jnp.float32),
            jax.ShapeDtypeStruct((1, 2, 2, part_beams, samples), jnp.bfloat16),
        ),
        in_specs=[hbm] * 8,
        out_specs=(hbm, hbm, hbm),
        scratch_shapes=[
            bf16(nf, 2, per_input, samples),
            bf16(2, inputs, samples),
            f32(stations, LANES),
            f32(part_beams, stations),
            f32(part_beams, stations),
            f32(cols, cols),
            f32(cols, cols),
            bf16(2, 2 * part_beams, stations),
            bf16(2, 2 * part_beams, stations),
            bf16(1, 2, 2, part_beams, samples),
            bf16(1, 2, rows, cols),
            f32(1, 2, inputs),
            f32(2, nt, rows, cols),
            f32(nf, 2, inputs),
            f32(ITERS, ng * nt, 2, rows),
            f32(2, inputs),
            f32(nf, 2, inputs),
        ]
        + [bf16(2, r, pairs * w) for r, w in shapes] * 2
        + [bf16(pairs - 1, 2, r, w) for r, w in shapes] * 2
        + [bf16(nf, 2, r // nf, w) for r, w in shapes] * 2
        + [bf16(nf - 1, 2, r // nf, w) for r, w in shapes]
        + [bf16(nf, 2, r // nf, w) for r, w in shapes]
        + [
            dma,
            dma((nf - 1, nc)),
            dma((ng - 1,)),
            dma((plan.levels,)),
            dma((plan.levels,)),
            dma,
            dma,
            dma,
            dma((ITERS,)),
            dma,
            dma,
            dma((nu,)),
            dma((nu,)),
            dma((nu, pairs - 1)),
            dma((nu, pairs - 1)),
            dma((nu,)),
            dma((nu,)),
            dma((nu,)),
            dma((nu,)),
            dma((5,)),
            dma((8,)),
            pltpu.VMEM(voltages.shape, jnp.bfloat16),
            pltpu.VMEM(prior_gains.shape, jnp.float32),
            pltpu.VMEM((1, stations), jnp.int32),
            pltpu.VMEM((1, stations), jnp.int32),
            pltpu.VMEM(station_coords.shape, jnp.float32),
            pltpu.VMEM(pointing.shape, jnp.int32),
            pltpu.SMEM(corr_channels.shape, jnp.int32),
            pltpu.SMEM(beam_channels.shape, jnp.int32),
        ],
        compiler_params=pltpu.CompilerParams(
            collective_id=0, has_side_effects=True, vmem_limit_bytes=67043328
        ),
    )(
        voltages,
        prior_gains,
        station_flags[None],
        ingest_map[None],
        station_coords,
        pointing,
        corr_channels,
        beam_channels,
    )
    return vis.astype(jnp.float32), gains, beams


def solution(mesh):
    return jax.shard_map(
        body,
        mesh=mesh,
        in_specs=(
            P(None, None, ("freq", "grp"), "tm"),
            P("freq", None, None),
            P(),
            P(),
            P(),
            P(),
            P(),
            P(),
        ),
        out_specs=(
            P("freq", None, "grp", "tm"),
            P("freq", None, None),
            P("freq", None, None, "grp", "tm"),
        ),
        check_vma=False,
    )
```

```python
import functools
import math

import jax
import jax.numpy as jnp
from jax import lax
from jax.experimental import pallas as pl
from jax.experimental.pallas import tpu as pltpu
from jax.sharding import PartitionSpec as P

ITERS = 4
LANES = 128
grid_cells = 64.0
MESH = pl.DeviceIdType.MESH


def partner(index, mask, count):
    result, bit = 0, 1
    while bit < count:
        digit = (index // bit) % 2
        result = result + bit * ((1 - digit) if mask & bit else digit)
        bit *= 2
    return result


def nt_dot(a, b):
    return lax.dot_general(a, b, (((1,), (1,)), ((), ())), preferred_element_type=jnp.float32)


class Plan:
    def __init__(self, nf, nt, ng, per_input, samples):
        self.nf, self.nt, self.ng = nf, nt, ng
        self.per_input, self.samples = per_input, samples
        self.inputs = nf * ng * per_input
        self.rows = self.inputs // ng
        self.cols = self.inputs // nt
        self.blocks = self.cols // per_input
        self.row_tiles = nt // ng
        self.levels = 4 if per_input % 64 == 0 else 1
        self.step = per_input // self.levels
        self.level_rows = self.cols // self.levels
        count = 16 if self.step % 16 == 0 else self.step
        self.chunks = tuple((part, first, count) for first in range(0, per_input, count) for part in (0, 1))
        half, tiles = self.cols // 2, tuple(range(self.row_tiles))
        if self.levels > 1:
            most = self.cols - self.level_rows
            units = [(tiles, 0, half, 0, half), (tiles, half, most - half, 0, half)]
            units += [((r,), 0, most, half, half) for r in tiles]
            units += [(tiles, most, self.level_rows, 0, self.cols)]
        else:
            units = [(tiles, 0, self.cols, 0, half), (tiles, 0, self.cols, half, half)]
        self.units = tuple(units)
        self.segments = tuple(
            (q * self.level_rows + b * self.step, self.step, b * per_input + q * self.step)
            for q in range(self.levels)
            for b in range(self.blocks)
        )

    def unit_shape(self, unit):
        tiles, _, seg_rows, _, lanes = self.units[unit]
        return len(tiles) * seg_rows, lanes


def kernel(plan, *refs):
    nf, nt, ng = plan.nf, plan.nt, plan.ng
    nu = len(plan.units)
    operands, refs = refs[:8], refs[8:]
    vis_hbm, gains_hbm, beams_hbm = refs[:3]
    refs = refs[3:]

    def take(count):
        nonlocal refs
        taken, refs = refs[:count], refs[count:]
        return taken

    src, corr, keep, cosine, sine, to_held, to_natural, left, right, beams_out, vis_out, gains_out, gram = take(13)
    priors, updates, z, gains = take(4)
    stage_a, landed_a, stage_b, landed_b = (take(nu) for _ in range(4))
    first_src, mid, second_src, landed = (take(nu) for _ in range(4))
    zs, zr, ys, yr, own_sem, qs, qr, us, ur, gs, gr, as_, ar, bs, br, fs, fr, ss, sr, out_sem, in_sem = take(21)
    held = refs
    voltages, prior, flags, slots, coords, pointing, corr_channels, beam_channels = held
    loads = [pltpu.make_async_copy(operands[i], held[i], in_sem.at[i]) for i in range(8)]
    for load in loads:
        load.start()
    f = lax.axis_index("freq")
    t = lax.axis_index("tm")
    g = lax.axis_index("grp")
    per_input, samples = plan.per_input, plan.samples
    inputs, rows, cols = plan.inputs, plan.rows, plan.cols
    stations = inputs // 2
    chunks = plan.chunks
    offsets = [(dt, dg) for dg in range(ng) for dt in range(nt) if (dt, dg) != (0, 0)]
    masks = list(range(nf - 1, 0, -1))
    peers = {k: partner(f, k, nf) for k in range(nf)}
    tiles = {d: partner(t, d, nt) for d in range(nt)}

    def group(dt, dg):
        return {"freq": f, "tm": (t + dt) % nt, "grp": (g + dg) % ng}

    def along_freq(k):
        return {"freq": peers[k], "tm": t, "grp": g}

    def along_tm(d):
        return {"freq": f, "tm": tiles[d], "grp": g}

    def await_all(ref, sem):
        pltpu.make_async_copy(ref, ref, sem).wait()

    barrier = pltpu.get_barrier_semaphore()
    for k in masks:
        pl.semaphore_signal(barrier, inc=1, device_id=along_freq(k), device_id_type=MESH)
    for dt, dg in offsets:
        pl.semaphore_signal(barrier, inc=1, device_id=group(dt, dg), device_id_type=MESH)
    for load in loads:
        load.wait()

    slot_rows = jnp.broadcast_to(slots[...].astype(jnp.float32), (LANES, stations)).T
    flagged = jnp.zeros((stations, LANES), jnp.float32)
    for first in range(0, stations, LANES):
        lane = lax.broadcasted_iota(jnp.int32, (stations, LANES), 1) + first
        flag = flags[0:1, first : first + LANES].astype(jnp.float32)
        flagged += jnp.where(slot_rows == lane.astype(jnp.float32), flag, 0.0)
    flagged = jnp.sum(flagged, axis=1, keepdims=True)
    keep[...] = jnp.broadcast_to(1.0 - flagged, (stations, LANES))
    first_slot = pl.multiple_of(((f * ng + g) * per_input) % stations, per_input)
    kept = keep[pl.ds(first_slot, per_input), 0:1].astype(jnp.bfloat16)

    for k in masks + [0]:
        for part in (0, 1):
            src[peers[k], part] = voltages[beam_channels[peers[k]], part] * kept

    pl.semaphore_wait(barrier, len(masks) + len(offsets))

    def held_start(owner, member, first):
        block = owner * ng + member
        level = first // plan.step
        start = (block // plan.blocks) * cols + level * plan.level_rows + (block % plan.blocks) * plan.step
        return pl.multiple_of(start + first % plan.step, math.gcd(plan.step, 16))

    def place(owner, chunk):
        part, first, count = chunk
        return corr.at[part, pl.ds(held_start(owner, g, first), count), :]

    def z_copy(k, ci):
        part, first, count = chunks[ci]
        return pltpu.make_async_remote_copy(
            src_ref=src.at[peers[k], part, pl.ds(first, count), :],
            dst_ref=place(f, chunks[ci]),
            send_sem=zs,
            recv_sem=zr.at[k - 1, ci],
            device_id=along_freq(k),
            device_id_type=MESH,
        )

    def y_copy(k, ci, dg):
        part, first, count = chunks[ci]
        spot = place(peers[k], chunks[ci])
        return pltpu.make_async_remote_copy(
            src_ref=src.at[f, part, pl.ds(first, count), :] if k == 0 else spot,
            dst_ref=spot,
            send_sem=ys.at[dg - 1],
            recv_sem=yr.at[first // plan.step],
            device_id=group(0, dg),
            device_id_type=MESH,
        )

    def forward(k, ci):
        for dg in range(1, ng):
            y_copy(k, ci, dg).start()

    own_copies = [
        pltpu.make_async_copy(
            src.at[f, :, pl.ds(first, plan.step), :],
            corr.at[:, pl.ds(held_start(f, g, first), plan.step), :],
            own_sem.at[first // plan.step],
        )
        for first in range(0, per_input, plan.step)
    ]

    def prior_copy(k):
        return pltpu.make_async_remote_copy(
            src_ref=prior.at[0],
            dst_ref=priors.at[f],
            send_sem=qs,
            recv_sem=qr,
            device_id=along_freq(k),
            device_id_type=MESH,
        )

    all_chunks = range(len(chunks))
    ahead = 2

    def send_chunk(ci):
        if ci < len(chunks):
            for k in masks:
                z_copy(k, ci).start()

    for ci in range(ahead):
        send_chunk(ci)
        if ci == 0:
            for k in masks:
                prior_copy(k).start()
    for ci in all_chunks:
        forward(0, ci)
    for copy in own_copies:
        copy.start()
    priors[f] = prior[0]

    n_beams = pointing.shape[1]
    beams = n_beams // ng
    my_beam = beam_channels[f]
    permuted = plan.levels > 1

    def natural(held_index):
        result = held_index
        for start, size, target in plan.segments:
            inside = (held_index >= start) & (held_index < start + size)
            result = jnp.where(inside, held_index + (target - start), result)
        return result

    if permuted:
        along_rows = lax.broadcasted_iota(jnp.int32, (cols, cols), 0)
        along_lanes = lax.broadcasted_iota(jnp.int32, (cols, cols), 1)
        to_held[...] = jnp.where(natural(along_lanes) == along_rows, 1.0, 0.0)
        to_natural[...] = jnp.where(natural(along_rows) == along_lanes, 1.0, 0.0)

    def reorder(row_vector, matrix):
        if not permuted:
            return row_vector
        moved = [
            jnp.dot(
                row_vector[:, first : first + cols],
                matrix[...],
                precision=lax.Precision.HIGHEST,
                preferred_element_type=jnp.float32,
            )
            for first in range(0, row_vector.shape[1], cols)
        ]
        return jnp.concatenate(moved, axis=1)

    def point_phases():
        ratio = 0.875 + 0.25 * (my_beam.astype(jnp.float32) + 0.5) / nf
        mine = pl.ds(pl.multiple_of(g * beams, beams), beams)
        east_dir, north_dir = (
            jnp.broadcast_to((pointing[d : d + 1, mine].astype(jnp.float32) + 0.5) / grid_cells - 0.5, (LANES, beams)).T
            for d in (0, 1)
        )
        east, north = (jnp.broadcast_to(coords[d : d + 1, :], (LANES, stations)).T for d in (0, 1))
        station = lax.broadcasted_iota(jnp.int32, (stations, LANES), 0)
        slot_east, slot_north = [], []
        for first in range(0, stations, LANES):
            lanes = slice(first, first + LANES)
            match = station == slots[0:1, lanes]
            slot_east.append(jnp.sum(jnp.where(match, east, 0.0), axis=0, keepdims=True))
            slot_north.append(jnp.sum(jnp.where(match, north, 0.0), axis=0, keepdims=True))
        where = jnp.concatenate(
            [jnp.concatenate(slot_east, axis=1), jnp.concatenate(slot_north, axis=1)] * 4, axis=0
        )
        where = reorder(where, to_held)
        for first in range(0, stations, LANES):
            lanes = slice(first, first + LANES)
            phase = 2.0 * math.pi * ratio * (east_dir * where[0:1, lanes] + north_dir * where[1:2, lanes])
            cosine[:, lanes] = jnp.cos(phase)
            sine[:, lanes] = jnp.sin(phase)

    point_phases()

    scale = 1.0 / (samples * nt)
    odds = list(range(nt - 1, 0, -2))
    evens = [d - 1 for d in odds]

    def a_copy(u):
        return pltpu.make_async_remote_copy(
            src_ref=stage_a[u],
            dst_ref=landed_a[u],
            send_sem=as_.at[u],
            recv_sem=ar.at[u],
            device_id=along_tm(1),
            device_id_type=MESH,
        )

    def b_copy(u, d):
        return pltpu.make_async_remote_copy(
            src_ref=stage_b[u].at[d // 2 - 1],
            dst_ref=landed_b[u].at[d // 2 - 1],
            send_sem=bs.at[u, d // 2 - 1],
            recv_sem=br.at[u, d // 2 - 1],
            device_id=along_tm(d),
            device_id_type=MESH,
        )

    def first_copy(u, k):
        return pltpu.make_async_remote_copy(
            src_ref=first_src[u].at[peers[k]],
            dst_ref=mid[u].at[f],
            send_sem=fs.at[u],
            recv_sem=fr.at[u],
            device_id=along_freq(k),
            device_id_type=MESH,
        )

    def second_copy(u, k):
        return pltpu.make_async_remote_copy(
            src_ref=second_src[u].at[k - 1],
            dst_ref=landed[u].at[f],
            send_sem=ss.at[u],
            recv_sem=sr.at[u],
            device_id=along_freq(k),
            device_id_type=MESH,
        )

    def correlate(seg, seg_rows, lane, lanes):
        def stacked(part):
            pieces = []
            for r in range(plan.row_tiles):
                start = pl.multiple_of(g * rows + r * cols + seg, plan.level_rows)
                pieces.append(corr[part, pl.ds(start, seg_rows), :])
            return pieces

        mine = jnp.concatenate(stacked(0) + stacked(1), axis=0)
        count = plan.row_tiles * seg_rows
        others = [
            jnp.concatenate(
                [corr[part, tile * cols + lane : tile * cols + lane + lanes, :] for tile in range(nt)], axis=0
            )
            for part in (0, 1)
        ]
        with_r = nt_dot(mine, others[0])
        with_i = nt_dot(mine, others[1])
        real = (with_r[:count] + with_i[count:]) * scale
        imag = (with_r[count:] - with_i[:count]) * scale
        for part, value in ((0, real), (1, imag)):
            for tile in range(nt):
                for r in range(plan.row_tiles):
                    gram[part, tile, r * cols + seg : r * cols + seg + seg_rows, lane : lane + lanes] = value[
                        r * seg_rows : (r + 1) * seg_rows, tile * lanes : (tile + 1) * lanes
                    ]

    def correlate_level(q):
        size = plan.level_rows
        correlate(0, (q + 1) * size, q * size, size)
        if q >= 2:
            correlate(q * size, size, 0, 2 * size)
        if q % 2:
            correlate(q * size, size, (q - 1) * size, size)

    def from_gram(u, part, d):
        row_tiles, seg, seg_rows, lane, lanes = plan.units[u]
        return jnp.concatenate(
            [
                gram[part, tiles[d], r * cols + seg : r * cols + seg + seg_rows, lane : lane + lanes]
                for r in row_tiles
            ],
            axis=0,
        )

    def send_pair(u):
        lanes = plan.units[u][4]
        for j, d in enumerate(odds):
            for part in (0, 1):
                stage_a[u][part, :, j * lanes : (j + 1) * lanes] = from_gram(u, part, d).astype(jnp.bfloat16)
        a_copy(u).start()

    def sum_pair(u):
        lanes = plan.units[u][4]
        a_copy(u).wait_recv()
        for j, d in enumerate(evens):
            if d:
                for part in (0, 1):
                    theirs = landed_a[u][part, :, j * lanes : (j + 1) * lanes].astype(jnp.float32)
                    stage_b[u][d // 2 - 1, part] = (from_gram(u, part, d) + theirs).astype(jnp.bfloat16)
        for d in evens:
            if d:
                b_copy(u, d).start()

    def sum_rest(u):
        total_rows, lanes = plan.unit_shape(u)
        piece = total_rows // nf
        for d in evens:
            if d:
                b_copy(u, d).wait_recv()
        j = len(evens) - 1
        for part in (0, 1):
            total = from_gram(u, part, 0) + landed_a[u][part, :, j * lanes : (j + 1) * lanes].astype(jnp.float32)
            for d in evens:
                if d:
                    total = total + landed_b[u][d // 2 - 1, part].astype(jnp.float32)
            total = total.astype(jnp.bfloat16)
            for p in range(nf):
                first_src[u][p, part] = total[p * piece : (p + 1) * piece]
        mid[u][f] = first_src[u][f]
        for k in masks:
            first_copy(u, k).start()

    def source_of(slot):
        wanted = corr_channels[slot]
        source = 0
        for s in range(nf):
            source = jnp.where(beam_channels[s] == wanted, s, source)
        return source

    def hand_on(u):
        await_all(mid[u].at[pl.ds(0, nf - 1)], fr.at[u])
        for k in masks:
            second_src[u][k - 1] = mid[u][source_of(peers[k])]
        landed[u][f] = mid[u][source_of(f)]
        for k in masks:
            second_copy(u, k).start()

    nearest_first = [1] + masks[:-1] if nf > 1 else []

    sent = [ahead]

    def send_until(count):
        while sent[0] < count:
            send_chunk(sent[0])
            sent[0] += 1

    def relay(ci, spare=0):
        for k in nearest_first:
            z_copy(k, ci).wait_recv()
            forward(k, ci)
        send_until(ci + 1 + ahead + spare)

    def of_level(q):
        return [ci for ci in all_chunks if chunks[ci][1] // plan.step == q]

    def await_level(q):
        own_copies[q].wait()
        await_all(corr.at[:, pl.ds(0, (ng - 1) * nf * plan.step), :], yr.at[q])

    last = plan.levels - 1
    early_units = [0, 1] if last else []
    late_units = [u for u in range(nu) if u not in early_units]
    ready = {last - 1: [0], last: [1]} if last else {}
    for q in range(plan.levels):
        members = of_level(q)
        relay(members[0], spare=1)
        if q:
            await_level(q - 1)
            correlate_level(q - 1)
        for u in ready.get(q, []):
            send_pair(u)
        relay(members[1])
        for u in ready.get(q, []):
            sum_pair(u)
            if u:
                sum_rest(u - 1)
        for ci in members[2:]:
            relay(ci)
    for u in early_units[1:]:
        sum_rest(u)
    await_level(last)
    correlate_level(last)
    for u in late_units:
        send_pair(u)
    for u in early_units[:1]:
        hand_on(u)

    await_all(priors.at[pl.ds(0, nf - 1)], qr)
    slot_of_mine = 0
    for k in range(nf):
        slot_of_mine = jnp.where(corr_channels[k] == my_beam, k, slot_of_mine)
    z[...] = reorder(priors[slot_of_mine], to_held)
    slot = g * nt + t
    strip = LANES
    per_tile = cols // LANES

    def update_copy(iteration, o):
        dt, dg = offsets[o]
        return pltpu.make_async_remote_copy(
            src_ref=updates.at[iteration, slot],
            dst_ref=updates.at[iteration, slot],
            send_sem=us,
            recv_sem=ur.at[iteration],
            device_id=group(dt, dg),
            device_id_type=MESH,
        )

    beside = {i: [] for i in range(ITERS + 1)}

    def plan_work(iteration, work, u):
        beside[min(iteration, ITERS)].append(functools.partial(work, u))

    for i, u in enumerate(late_units):
        plan_work(i // 2, sum_pair, u)
    for i, u in enumerate(late_units):
        plan_work(i // 2 + 1, sum_rest, u)
    for u in early_units[1:]:
        plan_work(0, hand_on, u)
    for i, u in enumerate(late_units):
        plan_work(i // 2 + 2, hand_on, u)
    for iteration in range(ITERS):
        power = jnp.sum(z[...] * z[...]) + 1e-06

        def product(r, carry):
            here = pl.ds(pl.multiple_of(r * strip, strip), strip)
            total_r = jnp.zeros((strip, LANES), jnp.float32)
            total_i = jnp.zeros((strip, LANES), jnp.float32)
            for c in range(inputs // LANES):
                lanes = slice(c * LANES, (c + 1) * LANES)
                tile, inner = c // per_tile, slice(c % per_tile * LANES, (c % per_tile + 1) * LANES)
                part_r = gram[0, tile, here, inner]
                part_i = gram[1, tile, here, inner]
                gain_r = z[0:1, lanes]
                gain_i = z[1:2, lanes]
                total_r += part_r * gain_r - part_i * gain_i
                total_i += part_i * gain_r + part_r * gain_i
            updates[iteration, slot, 0:1, here] = jnp.sum(total_r.T, axis=0, keepdims=True)
            updates[iteration, slot, 1:2, here] = jnp.sum(total_i.T, axis=0, keepdims=True)
            return carry

        lax.fori_loop(0, rows // strip, product, 0)
        for o in range(len(offsets)):
            update_copy(iteration, o).start()
        for work in beside[iteration]:
            work()
        await_all(updates.at[iteration, pl.ds(0, len(offsets))], ur.at[iteration])
        for h in range(ng):
            total = updates[iteration, h * nt]
            for other in range(1, nt):
                total = total + updates[iteration, h * nt + other]
            lanes = slice(h * rows, (h + 1) * rows)
            z[:, lanes] = 0.5 * (z[:, lanes] + inputs * total / power)

    gains[f] = reorder(z[...], to_natural)

    def gain_copy(k):
        return pltpu.make_async_remote_copy(
            src_ref=gains.at[f],
            dst_ref=gains.at[f],
            send_sem=gs,
            recv_sem=gr,
            device_id=along_freq(k),
            device_id_type=MESH,
        )

    factor = 1.0 / math.sqrt(stations)
    for p in (0, 1):
        gain_r = z[0:1, p * stations : (p + 1) * stations]
        gain_i = z[1:2, p * stations : (p + 1) * stations]
        denom = jnp.maximum(gain_r * gain_r + gain_i * gain_i, 0.5)
        along_r = gain_r / denom
        along_i = gain_i / denom
        cos = cosine[...]
        sin = sine[...]
        w_r = ((cos * along_r - sin * along_i) * factor).astype(jnp.bfloat16)
        w_i = (-(cos * along_i + sin * along_r) * factor).astype(jnp.bfloat16)
        left[p, 0:beams] = w_r
        left[p, beams:] = w_i
        right[p, 0:beams] = -w_i
        right[p, beams:] = w_r
    for k in masks:
        gain_copy(k).start()

    beam_copies = [
        pltpu.make_async_copy(beams_out.at[:, p], beams_hbm.at[:, p], out_sem.at[p]) for p in (0, 1)
    ]

    def beamform(p):
        rows_p = slice(p * stations, (p + 1) * stations)
        result = jnp.dot(left[p], corr[0, rows_p, :], preferred_element_type=jnp.float32)
        result = result + jnp.dot(right[p], corr[1, rows_p, :], preferred_element_type=jnp.float32)
        result = result.astype(jnp.bfloat16)
        beams_out[0, p, 0] = result[:beams]
        beams_out[0, p, 1] = result[beams:]

    for work in beside[ITERS]:
        work()
    for p in (0, 1):
        beamform(p)
        beam_copies[p].start()

    await_all(gains.at[pl.ds(0, nf - 1)], gr)
    gains_out[0] = gains[source_of(f)]
    gains_write = pltpu.make_async_copy(gains_out, gains_hbm, out_sem.at[4])
    gains_write.start()

    for u in range(nu):
        await_all(landed[u].at[pl.ds(0, nf - 1)], sr.at[u])
    vis_copies = [pltpu.make_async_copy(vis_out.at[:, part], vis_hbm.at[:, part], out_sem.at[2 + part]) for part in (0, 1)]
    for part in (0, 1):
        strips = [
            jnp.concatenate([landed[u][p, part] for p in range(nf)], axis=0) for u in range(nu)
        ]
        for r in range(plan.row_tiles):
            if permuted:
                first, second = plan.units[0][2], plan.units[1][2]
                early = jnp.concatenate(
                    [strips[0][r * first : (r + 1) * first], strips[1][r * second : (r + 1) * second]], axis=0
                )
                tile_rows = [
                    jnp.concatenate([early, strips[2 + r]], axis=1),
                    strips[-1][r * plan.level_rows : (r + 1) * plan.level_rows],
                ]
            else:
                here = slice(r * cols, (r + 1) * cols)
                tile_rows = [jnp.concatenate([strips[0][here], strips[1][here]], axis=1)]
            tile = jnp.concatenate(tile_rows, axis=0)
            if not permuted:
                vis_out[0, part, r * cols : (r + 1) * cols, :] = tile
                continue
            tile = jnp.dot(
                tile, to_natural[...].astype(jnp.bfloat16), preferred_element_type=jnp.float32
            ).astype(jnp.bfloat16)
            for start, size, target in plan.segments:
                vis_out[0, part, r * cols + target : r * cols + target + size, :] = tile[start : start + size]
    for copy in vis_copies:
        copy.start()

    await_all(priors.at[pl.ds(0, nf - 1)], qs)
    await_all(gains.at[pl.ds(0, nf - 1)], gs)
    await_all(src.at[pl.ds(0, nf - 1)], zs)
    for dg in range(1, ng):
        await_all(src, ys.at[dg - 1])
    for u in range(nu):
        a_copy(u).wait_send()
        for d in evens:
            if d:
                b_copy(u, d).wait_send()
        await_all(mid[u].at[pl.ds(0, nf - 1)], fs.at[u])
        await_all(landed[u].at[pl.ds(0, nf - 1)], ss.at[u])
    await_all(updates.at[:, pl.ds(0, len(offsets))], us)
    for copy in beam_copies + vis_copies + [gains_write]:
        copy.wait()


def finish(vis_in, gains_in, beams_in, vis_out, gains_out, beams_out, narrow, wide, gains, beams, sem, out_sem):
    takes = [pltpu.make_async_copy(vis_in.at[:, part], narrow.at[:, part], sem.at[part]) for part in (0, 1)]
    takes += [pltpu.make_async_copy(beams_in.at[:, p], beams.at[:, p], sem.at[2 + p]) for p in (0, 1)]
    takes.append(pltpu.make_async_copy(gains_in, gains, sem.at[4]))
    puts = [pltpu.make_async_copy(wide.at[:, part], vis_out.at[:, part], out_sem.at[part]) for part in (0, 1)]
    puts += [pltpu.make_async_copy(beams.at[:, p], beams_out.at[:, p], out_sem.at[2 + p]) for p in (0, 1)]
    puts.append(pltpu.make_async_copy(gains, gains_out, out_sem.at[4]))
    for take in takes:
        take.start()
    for i in range(5):
        takes[i].wait()
        if i < 2:
            wide[:, i] = narrow[:, i].astype(jnp.float32)
        puts[i].start()
    for put in puts:
        put.wait()


def body(
    voltages,
    prior_gains,
    station_flags,
    ingest_map,
    station_coords,
    pointing,
    corr_channels,
    beam_channels,
):
    nf = lax.axis_size("freq")
    nt = lax.axis_size("tm")
    ng = lax.axis_size("grp")
    _, _, per_input, samples = voltages.shape
    stations = ingest_map.shape[0]
    plan = Plan(nf, nt, ng, per_input, samples)
    inputs, rows, cols = plan.inputs, plan.rows, plan.cols
    part_beams = pointing.shape[1] // ng
    nc, nu = len(plan.chunks), len(plan.units)
    pairs = nt // 2
    dma = pltpu.SemaphoreType.DMA
    hbm = pl.BlockSpec(memory_space=pltpu.HBM)
    shapes = [plan.unit_shape(u) for u in range(nu)]

    def bf16(*shape):
        return pltpu.VMEM(shape, jnp.bfloat16)

    def f32(*shape):
        return pltpu.VMEM(shape, jnp.float32)

    vis, gains, beams = pl.pallas_call(
        functools.partial(kernel, plan),
        out_shape=(
            jax.ShapeDtypeStruct((1, 2, rows, cols), jnp.bfloat16),
            jax.ShapeDtypeStruct((1, 2, inputs), jnp.float32),
            jax.ShapeDtypeStruct((1, 2, 2, part_beams, samples), jnp.bfloat16),
        ),
        in_specs=[hbm] * 8,
        out_specs=(hbm, hbm, hbm),
        scratch_shapes=[
            bf16(nf, 2, per_input, samples),
            bf16(2, inputs, samples),
            f32(stations, LANES),
            f32(part_beams, stations),
            f32(part_beams, stations),
            f32(cols, cols),
            f32(cols, cols),
            bf16(2, 2 * part_beams, stations),
            bf16(2, 2 * part_beams, stations),
            bf16(1, 2, 2, part_beams, samples),
            bf16(1, 2, rows, cols),
            f32(1, 2, inputs),
            f32(2, nt, rows, cols),
            f32(nf, 2, inputs),
            f32(ITERS, ng * nt, 2, rows),
            f32(2, inputs),
            f32(nf, 2, inputs),
        ]
        + [bf16(2, r, pairs * w) for r, w in shapes] * 2
        + [bf16(pairs - 1, 2, r, w) for r, w in shapes] * 2
        + [bf16(nf, 2, r // nf, w) for r, w in shapes] * 2
        + [bf16(nf - 1, 2, r // nf, w) for r, w in shapes]
        + [bf16(nf, 2, r // nf, w) for r, w in shapes]
        + [
            dma,
            dma((nf - 1, nc)),
            dma((ng - 1,)),
            dma((plan.levels,)),
            dma((plan.levels,)),
            dma,
            dma,
            dma,
            dma((ITERS,)),
            dma,
            dma,
            dma((nu,)),
            dma((nu,)),
            dma((nu, pairs - 1)),
            dma((nu, pairs - 1)),
            dma((nu,)),
            dma((nu,)),
            dma((nu,)),
            dma((nu,)),
            dma((5,)),
            dma((8,)),
            pltpu.VMEM(voltages.shape, jnp.bfloat16),
            pltpu.VMEM(prior_gains.shape, jnp.float32),
            pltpu.VMEM((1, stations), jnp.int32),
            pltpu.VMEM((1, stations), jnp.int32),
            pltpu.VMEM(station_coords.shape, jnp.float32),
            pltpu.VMEM(pointing.shape, jnp.int32),
            pltpu.SMEM(corr_channels.shape, jnp.int32),
            pltpu.SMEM(beam_channels.shape, jnp.int32),
        ],
        compiler_params=pltpu.CompilerParams(
            collective_id=0, has_side_effects=True, vmem_limit_bytes=67043328
        ),
    )(
        voltages,
        prior_gains,
        station_flags[None],
        ingest_map[None],
        station_coords,
        pointing,
        corr_channels,
        beam_channels,
    )
    results = (jax.ShapeDtypeStruct(vis.shape, jnp.float32), gains, beams)
    return pl.pallas_call(
        finish,
        out_shape=tuple(jax.ShapeDtypeStruct(r.shape, r.dtype) for r in results),
        in_specs=[hbm] * 3,
        out_specs=(hbm,) * 3,
        scratch_shapes=[
            bf16(*vis.shape),
            f32(*vis.shape),
            f32(*gains.shape),
            bf16(*beams.shape),
            dma((5,)),
            dma((5,)),
        ],
    )(vis, gains, beams)


def solution(mesh):
    return jax.shard_map(
        body,
        mesh=mesh,
        in_specs=(
            P(None, None, ("freq", "grp"), "tm"),
            P("freq", None, None),
            P(),
            P(),
            P(),
            P(),
            P(),
            P(),
        ),
        out_specs=(
            P("freq", None, "grp", "tm"),
            P("freq", None, None),
            P("freq", None, None, "grp", "tm"),
        ),
        check_vma=False,
    )
```

```python
import functools
import math

import jax
import jax.numpy as jnp
from jax import lax
from jax.experimental import pallas as pl
from jax.experimental.pallas import tpu as pltpu
from jax.sharding import PartitionSpec as P

ITERS = 4
LANES = 128
grid_cells = 64.0
MESH = pl.DeviceIdType.MESH


def partner(index, mask, count):
    result, bit = 0, 1
    while bit < count:
        digit = (index // bit) % 2
        result = result + bit * ((1 - digit) if mask & bit else digit)
        bit *= 2
    return result


def nt_dot(a, b):
    return lax.dot_general(a, b, (((1,), (1,)), ((), ())), preferred_element_type=jnp.float32)


class Plan:
    def __init__(self, nf, nt, ng, per_input, samples):
        self.nf, self.nt, self.ng = nf, nt, ng
        self.per_input, self.samples = per_input, samples
        self.inputs = nf * ng * per_input
        self.rows = self.inputs // ng
        self.cols = self.inputs // nt
        self.blocks = self.cols // per_input
        self.row_tiles = nt // ng
        self.levels = 4 if per_input % 64 == 0 else 1
        self.step = per_input // self.levels
        self.level_rows = self.cols // self.levels
        count = 16 if self.step % 16 == 0 else self.step
        self.chunks = tuple((part, first, count) for first in range(0, per_input, count) for part in (0, 1))
        half = self.cols // 2
        if self.levels > 1:
            most = self.cols - self.level_rows
            units = [(0, half, 0, half, False), (half, most - half, 0, half, False)]
            units += [(0, most, lane, self.level_rows, True) for lane in (half, most)]
            units += [(most, self.level_rows, 0, self.cols, False)]
        else:
            units = [(0, self.cols, 0, half, False), (0, self.cols, half, half, False)]
        self.units = tuple(units)
        self.segments = tuple(
            (q * self.level_rows + b * self.step, self.step, b * per_input + q * self.step)
            for q in range(self.levels)
            for b in range(self.blocks)
        )

    def unit_shape(self, unit):
        _, seg_rows, _, lanes, beside = self.units[unit]
        return (seg_rows, self.row_tiles * lanes) if beside else (self.row_tiles * seg_rows, lanes)


def kernel(plan, *refs):
    nf, nt, ng = plan.nf, plan.nt, plan.ng
    nu = len(plan.units)
    operands, refs = refs[:8], refs[8:]
    vis_out, gains_out, beams_out = refs[:3]
    refs = refs[3:]

    def take(count):
        nonlocal refs
        taken, refs = refs[:count], refs[count:]
        return taken

    src, corr, keep, cosine, sine, to_held, to_natural, left, right, gram = take(10)
    priors, updates, z, gains = take(4)
    stage_a, landed_a, stage_b, landed_b = (take(nu) for _ in range(4))
    first_src, mid, second_src, landed = (take(nu) for _ in range(4))
    zs, zr, ys, yr, own_sem, qs, qr, us, ur, gs, gr, as_, ar, bs, br, fs, fr, ss, sr, in_sem = take(20)
    held = refs
    voltages, prior, flags, slots, coords, pointing, corr_channels, beam_channels = held
    loads = [pltpu.make_async_copy(operands[i], held[i], in_sem.at[i]) for i in range(8)]
    for load in loads:
        load.start()
    f = lax.axis_index("freq")
    t = lax.axis_index("tm")
    g = lax.axis_index("grp")
    per_input, samples = plan.per_input, plan.samples
    inputs, rows, cols = plan.inputs, plan.rows, plan.cols
    stations = inputs // 2
    chunks = plan.chunks
    offsets = [(dt, dg) for dg in range(ng) for dt in range(nt) if (dt, dg) != (0, 0)]
    masks = list(range(nf - 1, 0, -1))
    peers = {k: partner(f, k, nf) for k in range(nf)}
    tiles = {d: partner(t, d, nt) for d in range(nt)}

    def group(dt, dg):
        return {"freq": f, "tm": (t + dt) % nt, "grp": (g + dg) % ng}

    def along_freq(k):
        return {"freq": peers[k], "tm": t, "grp": g}

    def along_tm(d):
        return {"freq": f, "tm": tiles[d], "grp": g}

    def await_all(ref, sem):
        pltpu.make_async_copy(ref, ref, sem).wait()

    barrier = pltpu.get_barrier_semaphore()
    for k in masks:
        pl.semaphore_signal(barrier, inc=1, device_id=along_freq(k), device_id_type=MESH)
    for dt, dg in offsets:
        pl.semaphore_signal(barrier, inc=1, device_id=group(dt, dg), device_id_type=MESH)
    for load in loads:
        load.wait()

    slot_rows = jnp.broadcast_to(slots[...].astype(jnp.float32), (LANES, stations)).T
    flagged = jnp.zeros((stations, LANES), jnp.float32)
    for first in range(0, stations, LANES):
        lane = lax.broadcasted_iota(jnp.int32, (stations, LANES), 1) + first
        flag = flags[0:1, first : first + LANES].astype(jnp.float32)
        flagged += jnp.where(slot_rows == lane.astype(jnp.float32), flag, 0.0)
    flagged = jnp.sum(flagged, axis=1, keepdims=True)
    keep[...] = jnp.broadcast_to(1.0 - flagged, (stations, LANES))
    first_slot = pl.multiple_of(((f * ng + g) * per_input) % stations, per_input)
    kept = keep[pl.ds(first_slot, per_input), 0:1].astype(jnp.bfloat16)

    for k in masks + [0]:
        for part in (0, 1):
            src[peers[k], part] = voltages[beam_channels[peers[k]], part] * kept

    pl.semaphore_wait(barrier, len(masks) + len(offsets))

    def held_start(owner, member, first):
        block = owner * ng + member
        level = first // plan.step
        start = (block // plan.blocks) * cols + level * plan.level_rows + (block % plan.blocks) * plan.step
        return pl.multiple_of(start + first % plan.step, math.gcd(plan.step, 16))

    def place(owner, chunk):
        part, first, count = chunk
        return corr.at[part, pl.ds(held_start(owner, g, first), count), :]

    def z_copy(k, ci):
        part, first, count = chunks[ci]
        return pltpu.make_async_remote_copy(
            src_ref=src.at[peers[k], part, pl.ds(first, count), :],
            dst_ref=place(f, chunks[ci]),
            send_sem=zs,
            recv_sem=zr.at[k - 1, ci],
            device_id=along_freq(k),
            device_id_type=MESH,
        )

    def y_copy(k, ci, dg):
        part, first, count = chunks[ci]
        spot = place(peers[k], chunks[ci])
        return pltpu.make_async_remote_copy(
            src_ref=src.at[f, part, pl.ds(first, count), :] if k == 0 else spot,
            dst_ref=spot,
            send_sem=ys.at[dg - 1],
            recv_sem=yr.at[first // plan.step],
            device_id=group(0, dg),
            device_id_type=MESH,
        )

    def forward(k, ci):
        for dg in range(1, ng):
            y_copy(k, ci, dg).start()

    own_copies = [
        pltpu.make_async_copy(
            src.at[f, :, pl.ds(first, plan.step), :],
            corr.at[:, pl.ds(held_start(f, g, first), plan.step), :],
            own_sem.at[first // plan.step],
        )
        for first in range(0, per_input, plan.step)
    ]

    def prior_copy(k):
        return pltpu.make_async_remote_copy(
            src_ref=prior.at[0],
            dst_ref=priors.at[f],
            send_sem=qs,
            recv_sem=qr,
            device_id=along_freq(k),
            device_id_type=MESH,
        )

    all_chunks = range(len(chunks))
    ahead = 2

    def send_chunk(ci):
        if ci < len(chunks):
            for k in masks:
                z_copy(k, ci).start()

    for ci in range(ahead):
        send_chunk(ci)
        if ci == 0:
            for k in masks:
                prior_copy(k).start()
    for ci in all_chunks:
        forward(0, ci)
    for copy in own_copies:
        copy.start()
    priors[f] = prior[0]

    n_beams = pointing.shape[1]
    beams = n_beams // ng
    my_beam = beam_channels[f]
    permuted = plan.levels > 1

    def natural(held_index):
        result = held_index
        for start, size, target in plan.segments:
            inside = (held_index >= start) & (held_index < start + size)
            result = jnp.where(inside, held_index + (target - start), result)
        return result

    if permuted:
        along_rows = lax.broadcasted_iota(jnp.int32, (cols, cols), 0)
        along_lanes = lax.broadcasted_iota(jnp.int32, (cols, cols), 1)
        to_held[...] = jnp.where(natural(along_lanes) == along_rows, 1.0, 0.0)
        to_natural[...] = jnp.where(natural(along_rows) == along_lanes, 1.0, 0.0)

    def reorder(row_vector, matrix):
        if not permuted:
            return row_vector
        moved = [
            jnp.dot(
                row_vector[:, first : first + cols],
                matrix[...],
                precision=lax.Precision.HIGHEST,
                preferred_element_type=jnp.float32,
            )
            for first in range(0, row_vector.shape[1], cols)
        ]
        return jnp.concatenate(moved, axis=1)

    def point_phases():
        ratio = 0.875 + 0.25 * (my_beam.astype(jnp.float32) + 0.5) / nf
        mine = pl.ds(pl.multiple_of(g * beams, beams), beams)
        east_dir, north_dir = (
            jnp.broadcast_to((pointing[d : d + 1, mine].astype(jnp.float32) + 0.5) / grid_cells - 0.5, (LANES, beams)).T
            for d in (0, 1)
        )
        east, north = (jnp.broadcast_to(coords[d : d + 1, :], (LANES, stations)).T for d in (0, 1))
        station = lax.broadcasted_iota(jnp.int32, (stations, LANES), 0)
        slot_east, slot_north = [], []
        for first in range(0, stations, LANES):
            lanes = slice(first, first + LANES)
            match = station == slots[0:1, lanes]
            slot_east.append(jnp.sum(jnp.where(match, east, 0.0), axis=0, keepdims=True))
            slot_north.append(jnp.sum(jnp.where(match, north, 0.0), axis=0, keepdims=True))
        where = jnp.concatenate(
            [jnp.concatenate(slot_east, axis=1), jnp.concatenate(slot_north, axis=1)] * 4, axis=0
        )
        where = reorder(where, to_held)
        for first in range(0, stations, LANES):
            lanes = slice(first, first + LANES)
            phase = 2.0 * math.pi * ratio * (east_dir * where[0:1, lanes] + north_dir * where[1:2, lanes])
            cosine[:, lanes] = jnp.cos(phase)
            sine[:, lanes] = jnp.sin(phase)

    point_phases()

    scale = 1.0 / (samples * nt)
    odds = list(range(nt - 1, 0, -2))
    evens = [d - 1 for d in odds]

    def a_copy(u):
        return pltpu.make_async_remote_copy(
            src_ref=stage_a[u],
            dst_ref=landed_a[u],
            send_sem=as_.at[u],
            recv_sem=ar.at[u],
            device_id=along_tm(1),
            device_id_type=MESH,
        )

    def b_copy(u, d):
        return pltpu.make_async_remote_copy(
            src_ref=stage_b[u].at[d // 2 - 1],
            dst_ref=landed_b[u].at[d // 2 - 1],
            send_sem=bs.at[u, d // 2 - 1],
            recv_sem=br.at[u, d // 2 - 1],
            device_id=along_tm(d),
            device_id_type=MESH,
        )

    def first_copy(u, k):
        return pltpu.make_async_remote_copy(
            src_ref=first_src[u].at[peers[k]],
            dst_ref=mid[u].at[f],
            send_sem=fs.at[u],
            recv_sem=fr.at[u],
            device_id=along_freq(k),
            device_id_type=MESH,
        )

    def second_copy(u, k):
        return pltpu.make_async_remote_copy(
            src_ref=second_src[u].at[k - 1],
            dst_ref=landed[u].at[f],
            send_sem=ss.at[u],
            recv_sem=sr.at[u],
            device_id=along_freq(k),
            device_id_type=MESH,
        )

    def correlate(seg, seg_rows, lane, lanes):
        def stacked(part):
            pieces = []
            for r in range(plan.row_tiles):
                start = pl.multiple_of(g * rows + r * cols + seg, plan.level_rows)
                pieces.append(corr[part, pl.ds(start, seg_rows), :])
            return pieces

        mine = jnp.concatenate(stacked(0) + stacked(1), axis=0)
        count = plan.row_tiles * seg_rows
        others = [
            jnp.concatenate(
                [corr[part, tile * cols + lane : tile * cols + lane + lanes, :] for tile in range(nt)], axis=0
            )
            for part in (0, 1)
        ]
        with_r = nt_dot(mine, others[0])
        with_i = nt_dot(mine, others[1])
        real = (with_r[:count] + with_i[count:]) * scale
        imag = (with_r[count:] - with_i[:count]) * scale
        for part, value in ((0, real), (1, imag)):
            for tile in range(nt):
                for r in range(plan.row_tiles):
                    gram[part, tile, r * cols + seg : r * cols + seg + seg_rows, lane : lane + lanes] = value[
                        r * seg_rows : (r + 1) * seg_rows, tile * lanes : (tile + 1) * lanes
                    ]

    def correlate_level(q):
        size = plan.level_rows
        correlate(0, (q + 1) * size, q * size, size)
        if q >= 2:
            correlate(q * size, size, 0, 2 * size)
        if q % 2:
            correlate(q * size, size, (q - 1) * size, size)

    def from_gram(u, part, d):
        seg, seg_rows, lane, lanes, side_by_side = plan.units[u]
        return jnp.concatenate(
            [
                gram[part, tiles[d], r * cols + seg : r * cols + seg + seg_rows, lane : lane + lanes]
                for r in range(plan.row_tiles)
            ],
            axis=1 if side_by_side else 0,
        )

    def send_pair(u):
        lanes = plan.unit_shape(u)[1]
        for j, d in enumerate(odds):
            for part in (0, 1):
                stage_a[u][part, :, j * lanes : (j + 1) * lanes] = from_gram(u, part, d).astype(jnp.bfloat16)
        a_copy(u).start()

    def sum_pair(u):
        lanes = plan.unit_shape(u)[1]
        a_copy(u).wait_recv()
        for j, d in enumerate(evens):
            if d:
                for part in (0, 1):
                    theirs = landed_a[u][part, :, j * lanes : (j + 1) * lanes].astype(jnp.float32)
                    stage_b[u][d // 2 - 1, part] = (from_gram(u, part, d) + theirs).astype(jnp.bfloat16)
        for d in evens:
            if d:
                b_copy(u, d).start()

    def sum_rest(u):
        total_rows, lanes = plan.unit_shape(u)
        piece = total_rows // nf
        for d in evens:
            if d:
                b_copy(u, d).wait_recv()
        j = len(evens) - 1
        for part in (0, 1):
            total = from_gram(u, part, 0) + landed_a[u][part, :, j * lanes : (j + 1) * lanes].astype(jnp.float32)
            for d in evens:
                if d:
                    total = total + landed_b[u][d // 2 - 1, part].astype(jnp.float32)
            total = total.astype(jnp.bfloat16)
            for p in range(nf):
                first_src[u][p, part] = total[p * piece : (p + 1) * piece]
        mid[u][f] = first_src[u][f]
        for k in masks:
            first_copy(u, k).start()

    def source_of(slot):
        wanted = corr_channels[slot]
        source = 0
        for s in range(nf):
            source = jnp.where(beam_channels[s] == wanted, s, source)
        return source

    def hand_on(u):
        await_all(mid[u].at[pl.ds(0, nf - 1)], fr.at[u])
        for k in masks:
            second_src[u][k - 1] = mid[u][source_of(peers[k])]
        landed[u][f] = mid[u][source_of(f)]
        for k in masks:
            second_copy(u, k).start()

    nearest_first = [1] + masks[:-1] if nf > 1 else []

    sent = [ahead]

    def send_until(count):
        while sent[0] < count:
            send_chunk(sent[0])
            sent[0] += 1

    def relay(ci, spare=0):
        for k in nearest_first:
            z_copy(k, ci).wait_recv()
            forward(k, ci)
        send_until(ci + 1 + ahead + spare)

    def of_level(q):
        return [ci for ci in all_chunks if chunks[ci][1] // plan.step == q]

    def await_level(q):
        own_copies[q].wait()
        await_all(corr.at[:, pl.ds(0, (ng - 1) * nf * plan.step), :], yr.at[q])

    last = plan.levels - 1
    early_units = [0, 1, 2] if last else []
    late_units = [u for u in range(nu) if u not in early_units][::-1]
    ready = {last - 1: [0], last: [1, 2]} if last else {}
    for q in range(plan.levels):
        members = of_level(q)
        relay(members[0], spare=1)
        if q:
            await_level(q - 1)
            correlate_level(q - 1)
        for u in ready.get(q, []):
            send_pair(u)
        relay(members[1])
        for u in ready.get(q, []):
            sum_pair(u)
        if q == last:
            for u in early_units[:1]:
                sum_rest(u)
        for ci in members[2:]:
            relay(ci)
    for u in early_units[1:]:
        sum_rest(u)
    await_all(priors.at[pl.ds(0, nf - 1)], qr)
    slot_of_mine = 0
    for k in range(nf):
        slot_of_mine = jnp.where(corr_channels[k] == my_beam, k, slot_of_mine)
    z[...] = reorder(priors[slot_of_mine], to_held)
    await_level(last)
    correlate_level(last)
    for u in late_units:
        send_pair(u)
    for u in early_units[:1]:
        hand_on(u)
    slot = g * nt + t
    strip = LANES
    per_tile = cols // LANES

    def update_copy(iteration, o):
        dt, dg = offsets[o]
        return pltpu.make_async_remote_copy(
            src_ref=updates.at[iteration, slot],
            dst_ref=updates.at[iteration, slot],
            send_sem=us,
            recv_sem=ur.at[iteration],
            device_id=group(dt, dg),
            device_id_type=MESH,
        )

    beside = {i: [] for i in range(ITERS + 1)}

    def plan_work(iteration, work, u):
        beside[min(iteration, ITERS)].append(functools.partial(work, u))

    for u in late_units:
        plan_work(0, sum_pair, u)
    for u in early_units[1:]:
        plan_work(0, hand_on, u)
    for i, u in enumerate(late_units):
        plan_work(i + 1, sum_rest, u)
    for i, u in enumerate(late_units):
        plan_work(i + 2, hand_on, u)
    for iteration in range(ITERS):
        power = jnp.sum(z[...] * z[...]) + 1e-06

        def product(r, carry):
            here = pl.ds(pl.multiple_of(r * strip, strip), strip)
            total_r = jnp.zeros((strip, LANES), jnp.float32)
            total_i = jnp.zeros((strip, LANES), jnp.float32)
            for c in range(inputs // LANES):
                lanes = slice(c * LANES, (c + 1) * LANES)
                tile, inner = c // per_tile, slice(c % per_tile * LANES, (c % per_tile + 1) * LANES)
                part_r = gram[0, tile, here, inner]
                part_i = gram[1, tile, here, inner]
                gain_r = z[0:1, lanes]
                gain_i = z[1:2, lanes]
                total_r += part_r * gain_r - part_i * gain_i
                total_i += part_i * gain_r + part_r * gain_i
            updates[iteration, slot, 0:1, here] = jnp.sum(total_r.T, axis=0, keepdims=True)
            updates[iteration, slot, 1:2, here] = jnp.sum(total_i.T, axis=0, keepdims=True)
            return carry

        lax.fori_loop(0, rows // strip, product, 0)
        for o in range(len(offsets)):
            update_copy(iteration, o).start()
        for work in beside[iteration]:
            work()
        await_all(updates.at[iteration, pl.ds(0, len(offsets))], ur.at[iteration])
        for h in range(ng):
            total = updates[iteration, h * nt]
            for other in range(1, nt):
                total = total + updates[iteration, h * nt + other]
            lanes = slice(h * rows, (h + 1) * rows)
            z[:, lanes] = 0.5 * (z[:, lanes] + inputs * total / power)

    gains[f] = reorder(z[...], to_natural)

    def gain_copy(k):
        return pltpu.make_async_remote_copy(
            src_ref=gains.at[f],
            dst_ref=gains.at[f],
            send_sem=gs,
            recv_sem=gr,
            device_id=along_freq(k),
            device_id_type=MESH,
        )

    for k in masks:
        gain_copy(k).start()

    factor = 1.0 / math.sqrt(stations)
    for p in (0, 1):
        gain_r = z[0:1, p * stations : (p + 1) * stations]
        gain_i = z[1:2, p * stations : (p + 1) * stations]
        denom = jnp.maximum(gain_r * gain_r + gain_i * gain_i, 0.5)
        along_r = gain_r / denom
        along_i = gain_i / denom
        cos = cosine[...]
        sin = sine[...]
        w_r = ((cos * along_r - sin * along_i) * factor).astype(jnp.bfloat16)
        w_i = (-(cos * along_i + sin * along_r) * factor).astype(jnp.bfloat16)
        left[p, 0:beams] = w_r
        left[p, beams:] = w_i
        right[p, 0:beams] = -w_i
        right[p, beams:] = w_r

    def beamform(p):
        rows_p = slice(p * stations, (p + 1) * stations)
        result = jnp.dot(left[p], corr[0, rows_p, :], preferred_element_type=jnp.float32)
        result = result + jnp.dot(right[p], corr[1, rows_p, :], preferred_element_type=jnp.float32)
        result = result.astype(jnp.bfloat16)
        beams_out[0, p, 0] = result[:beams]
        beams_out[0, p, 1] = result[beams:]

    for work in beside[ITERS]:
        work()
    for p in (0, 1):
        beamform(p)

    await_all(gains.at[pl.ds(0, nf - 1)], gr)
    gains_out[0] = gains[source_of(f)]

    for u in range(nu):
        await_all(landed[u].at[pl.ds(0, nf - 1)], sr.at[u])
    for part in (0, 1):
        strips = [
            jnp.concatenate([landed[u][p, part] for p in range(nf)], axis=0) for u in range(nu)
        ]
        for r in range(plan.row_tiles):
            if permuted:
                first, second = plan.units[0][1], plan.units[1][1]
                early = jnp.concatenate(
                    [strips[0][r * first : (r + 1) * first], strips[1][r * second : (r + 1) * second]], axis=0
                )
                side = slice(r * plan.level_rows, (r + 1) * plan.level_rows)
                tile_rows = [
                    jnp.concatenate([early, strips[2][:, side], strips[3][:, side]], axis=1),
                    strips[4][side],
                ]
            else:
                here = slice(r * cols, (r + 1) * cols)
                tile_rows = [jnp.concatenate([strips[0][here], strips[1][here]], axis=1)]
            tile = jnp.concatenate(tile_rows, axis=0)
            if not permuted:
                vis_out[0, part, r * cols : (r + 1) * cols, :] = tile
                continue
            tile = jnp.dot(
                tile, to_natural[...].astype(jnp.bfloat16), preferred_element_type=jnp.float32
            ).astype(jnp.bfloat16)
            for start, size, target in plan.segments:
                vis_out[0, part, r * cols + target : r * cols + target + size, :] = tile[start : start + size]

    await_all(priors.at[pl.ds(0, nf - 1)], qs)
    await_all(gains.at[pl.ds(0, nf - 1)], gs)
    await_all(src.at[pl.ds(0, nf - 1)], zs)
    for dg in range(1, ng):
        await_all(src, ys.at[dg - 1])
    for u in range(nu):
        a_copy(u).wait_send()
        for d in evens:
            if d:
                b_copy(u, d).wait_send()
        await_all(mid[u].at[pl.ds(0, nf - 1)], fs.at[u])
        await_all(landed[u].at[pl.ds(0, nf - 1)], ss.at[u])
    await_all(updates.at[:, pl.ds(0, len(offsets))], us)


def finish(vis_in, gains_in, beams_in, vis_out, gains_out, beams_out, wide, sem):
    puts = [pltpu.make_async_copy(beams_in, beams_out, sem.at[0]), pltpu.make_async_copy(gains_in, gains_out, sem.at[1])]
    for put in puts:
        put.start()
    for part in (0, 1):
        wide[:, part] = vis_in[:, part].astype(jnp.float32)
        puts.append(pltpu.make_async_copy(wide.at[:, part], vis_out.at[:, part], sem.at[2 + part]))
        puts[-1].start()
    for put in puts:
        put.wait()


def body(
    voltages,
    prior_gains,
    station_flags,
    ingest_map,
    station_coords,
    pointing,
    corr_channels,
    beam_channels,
):
    nf = lax.axis_size("freq")
    nt = lax.axis_size("tm")
    ng = lax.axis_size("grp")
    _, _, per_input, samples = voltages.shape
    stations = ingest_map.shape[0]
    plan = Plan(nf, nt, ng, per_input, samples)
    inputs, rows, cols = plan.inputs, plan.rows, plan.cols
    part_beams = pointing.shape[1] // ng
    nc, nu = len(plan.chunks), len(plan.units)
    pairs = nt // 2
    dma = pltpu.SemaphoreType.DMA
    hbm = pl.BlockSpec(memory_space=pltpu.HBM)
    vmem = pl.BlockSpec(memory_space=pltpu.VMEM)
    shapes = [plan.unit_shape(u) for u in range(nu)]

    def bf16(*shape):
        return pltpu.VMEM(shape, jnp.bfloat16)

    def f32(*shape):
        return pltpu.VMEM(shape, jnp.float32)

    kept_bytes = 4 * rows * cols + 8 * inputs + 8 * part_beams * samples + 61440

    vis, gains, beams = pl.pallas_call(
        functools.partial(kernel, plan),
        out_shape=(
            pltpu.VMEM((1, 2, rows, cols), jnp.bfloat16),
            pltpu.VMEM((1, 2, inputs), jnp.float32),
            pltpu.VMEM((1, 2, 2, part_beams, samples), jnp.bfloat16),
        ),
        in_specs=[hbm] * 8,
        out_specs=(vmem, vmem, vmem),
        scratch_shapes=[
            bf16(nf, 2, per_input, samples),
            bf16(2, inputs, samples),
            f32(stations, LANES),
            f32(part_beams, stations),
            f32(part_beams, stations),
            f32(cols, cols),
            f32(cols, cols),
            bf16(2, 2 * part_beams, stations),
            bf16(2, 2 * part_beams, stations),
            f32(2, nt, rows, cols),
            f32(nf, 2, inputs),
            f32(ITERS, ng * nt, 2, rows),
            f32(2, inputs),
            f32(nf, 2, inputs),
        ]
        + [bf16(2, r, pairs * w) for r, w in shapes] * 2
        + [bf16(pairs - 1, 2, r, w) for r, w in shapes] * 2
        + [bf16(nf, 2, r // nf, w) for r, w in shapes] * 2
        + [bf16(nf - 1, 2, r // nf, w) for r, w in shapes]
        + [bf16(nf, 2, r // nf, w) for r, w in shapes]
        + [
            dma,
            dma((nf - 1, nc)),
            dma((ng - 1,)),
            dma((plan.levels,)),
            dma((plan.levels,)),
            dma,
            dma,
            dma,
            dma((ITERS,)),
            dma,
            dma,
            dma((nu,)),
            dma((nu,)),
            dma((nu, pairs - 1)),
            dma((nu, pairs - 1)),
            dma((nu,)),
            dma((nu,)),
            dma((nu,)),
            dma((nu,)),
            dma((8,)),
            pltpu.VMEM(voltages.shape, jnp.bfloat16),
            pltpu.VMEM(prior_gains.shape, jnp.float32),
            pltpu.VMEM((1, stations), jnp.int32),
            pltpu.VMEM((1, stations), jnp.int32),
            pltpu.VMEM(station_coords.shape, jnp.float32),
            pltpu.VMEM(pointing.shape, jnp.int32),
            pltpu.SMEM(corr_channels.shape, jnp.int32),
            pltpu.SMEM(beam_channels.shape, jnp.int32),
        ],
        compiler_params=pltpu.CompilerParams(
            collective_id=0, has_side_effects=True, vmem_limit_bytes=67043328 - kept_bytes
        ),
    )(
        voltages,
        prior_gains,
        station_flags[None],
        ingest_map[None],
        station_coords,
        pointing,
        corr_channels,
        beam_channels,
    )
    results = (jax.ShapeDtypeStruct(vis.shape, jnp.float32), gains, beams)
    return pl.pallas_call(
        finish,
        out_shape=tuple(jax.ShapeDtypeStruct(r.shape, r.dtype) for r in results),
        in_specs=[vmem] * 3,
        out_specs=(hbm,) * 3,
        scratch_shapes=[
            f32(*vis.shape),
            dma((4,)),
        ],
        compiler_params=pltpu.CompilerParams(vmem_limit_bytes=4 * 1024 * 1024),
    )(vis, gains, beams)


def solution(mesh):
    return jax.shard_map(
        body,
        mesh=mesh,
        in_specs=(
            P(None, None, ("freq", "grp"), "tm"),
            P("freq", None, None),
            P(),
            P(),
            P(),
            P(),
            P(),
            P(),
        ),
        out_specs=(
            P("freq", None, "grp", "tm"),
            P("freq", None, None),
            P("freq", None, None, "grp", "tm"),
        ),
        check_vma=False,
    )
```

```python
import functools
import math

import jax
import jax.numpy as jnp
from jax import lax
from jax.experimental import pallas as pl
from jax.experimental.pallas import tpu as pltpu
from jax.sharding import PartitionSpec as P

ITERS = 4
LANES = 128
grid_cells = 64.0
MESH = pl.DeviceIdType.MESH


def partner(index, mask, count):
    result, bit = 0, 1
    while bit < count:
        digit = (index // bit) % 2
        result = result + bit * ((1 - digit) if mask & bit else digit)
        bit *= 2
    return result


def nt_dot(a, b):
    return lax.dot_general(a, b, (((1,), (1,)), ((), ())), preferred_element_type=jnp.float32)


def exact_parts(values):
    high = values.astype(jnp.bfloat16)
    rest = values - high.astype(jnp.float32)
    middle = rest.astype(jnp.bfloat16)
    low = (rest - middle.astype(jnp.float32)).astype(jnp.bfloat16)
    return jnp.concatenate([high, middle, low], axis=0)


def add_parts(values):
    count = values.shape[0] // 3
    return (values[2 * count :] + values[count : 2 * count]) + values[:count]


class Plan:
    def __init__(self, nf, nt, ng, per_input, samples):
        self.nf, self.nt, self.ng = nf, nt, ng
        self.per_input, self.samples = per_input, samples
        self.inputs = nf * ng * per_input
        self.rows = self.inputs // ng
        self.cols = self.inputs // nt
        self.blocks = self.cols // per_input
        self.row_tiles = nt // ng
        self.levels = 4 if per_input % 64 == 0 else 1
        self.step = per_input // self.levels
        self.level_rows = self.cols // self.levels
        count = 16 if self.step % 16 == 0 else self.step
        self.chunks = tuple((part, first, count) for first in range(0, per_input, count) for part in (0, 1))
        half = self.cols // 2
        if self.levels > 1:
            most = self.cols - self.level_rows
            units = [(0, half, 0, half, False), (half, most - half, 0, half, False)]
            units += [(0, most, lane, self.level_rows, True) for lane in (half, most)]
            units += [(most, self.level_rows, 0, self.cols, False)]
        else:
            units = [(0, self.cols, 0, half, False), (0, self.cols, half, half, False)]
        self.units = tuple(units)
        self.segments = tuple(
            (q * self.level_rows + b * self.step, self.step, b * per_input + q * self.step)
            for q in range(self.levels)
            for b in range(self.blocks)
        )

    def unit_shape(self, unit):
        _, seg_rows, _, lanes, beside = self.units[unit]
        return (seg_rows, self.row_tiles * lanes) if beside else (self.row_tiles * seg_rows, lanes)


def kernel(plan, *refs):
    nf, nt, ng = plan.nf, plan.nt, plan.ng
    nu = len(plan.units)
    operands, refs = refs[:8], refs[8:]
    vis_out, gains_out, beams_out = refs[:3]
    refs = refs[3:]

    def take(count):
        nonlocal refs
        taken, refs = refs[:count], refs[count:]
        return taken

    src, corr, keep, cosine, sine, to_held, to_natural, left, right, gram = take(10)
    priors, updates, z, gains, first_gains, gathered = take(6)
    stage_a, landed_a, stage_b, landed_b = (take(nu) for _ in range(4))
    first_src, mid, second_src, landed = (take(nu) for _ in range(4))
    zs, zr, ys, yr, own_sem, qs, qr, us, ur, gs, gr, as_, ar, bs, br, fs, fr, ss, sr, in_sem = take(20)
    held = refs
    voltages, prior, flags, slots, coords, pointing, corr_channels, beam_channels = held
    loads = [pltpu.make_async_copy(operands[i], held[i], in_sem.at[i]) for i in range(8)]
    for load in loads:
        load.start()
    f = lax.axis_index("freq")
    t = lax.axis_index("tm")
    g = lax.axis_index("grp")
    per_input, samples = plan.per_input, plan.samples
    inputs, rows, cols = plan.inputs, plan.rows, plan.cols
    stations = inputs // 2
    chunks = plan.chunks
    offsets = [(dt, dg) for dg in range(ng) for dt in range(nt) if (dt, dg) != (0, 0)]
    masks = list(range(nf - 1, 0, -1))
    peers = {k: partner(f, k, nf) for k in range(nf)}
    tiles = {d: partner(t, d, nt) for d in range(nt)}

    def group(dt, dg):
        return {"freq": f, "tm": (t + dt) % nt, "grp": (g + dg) % ng}

    def along_freq(k):
        return {"freq": peers[k], "tm": t, "grp": g}

    def along_tm(d):
        return {"freq": f, "tm": tiles[d], "grp": g}

    def await_all(ref, sem):
        pltpu.make_async_copy(ref, ref, sem).wait()

    barrier = pltpu.get_barrier_semaphore()
    for k in masks:
        pl.semaphore_signal(barrier, inc=1, device_id=along_freq(k), device_id_type=MESH)
    for dt, dg in offsets:
        pl.semaphore_signal(barrier, inc=1, device_id=group(dt, dg), device_id_type=MESH)
    for load in loads:
        load.wait()

    slot_rows = jnp.broadcast_to(slots[...].astype(jnp.float32), (LANES, stations)).T
    flagged = jnp.zeros((stations, LANES), jnp.float32)
    for first in range(0, stations, LANES):
        lane = lax.broadcasted_iota(jnp.int32, (stations, LANES), 1) + first
        flag = flags[0:1, first : first + LANES].astype(jnp.float32)
        flagged += jnp.where(slot_rows == lane.astype(jnp.float32), flag, 0.0)
    flagged = jnp.sum(flagged, axis=1, keepdims=True)
    keep[...] = jnp.broadcast_to(1.0 - flagged, (stations, LANES))
    first_slot = pl.multiple_of(((f * ng + g) * per_input) % stations, per_input)
    kept = keep[pl.ds(first_slot, per_input), 0:1].astype(jnp.bfloat16)

    for k in masks + [0]:
        for part in (0, 1):
            src[peers[k], part] = voltages[beam_channels[peers[k]], part] * kept

    pl.semaphore_wait(barrier, len(masks) + len(offsets))

    def held_start(owner, member, first):
        block = owner * ng + member
        level = first // plan.step
        start = (block // plan.blocks) * cols + level * plan.level_rows + (block % plan.blocks) * plan.step
        return pl.multiple_of(start + first % plan.step, math.gcd(plan.step, 16))

    def place(owner, chunk):
        part, first, count = chunk
        return corr.at[part, pl.ds(held_start(owner, g, first), count), :]

    def z_copy(k, ci):
        part, first, count = chunks[ci]
        return pltpu.make_async_remote_copy(
            src_ref=src.at[peers[k], part, pl.ds(first, count), :],
            dst_ref=place(f, chunks[ci]),
            send_sem=zs,
            recv_sem=zr.at[k - 1, ci],
            device_id=along_freq(k),
            device_id_type=MESH,
        )

    def y_copy(k, ci, dg):
        part, first, count = chunks[ci]
        spot = place(peers[k], chunks[ci])
        return pltpu.make_async_remote_copy(
            src_ref=src.at[f, part, pl.ds(first, count), :] if k == 0 else spot,
            dst_ref=spot,
            send_sem=ys.at[dg - 1],
            recv_sem=yr.at[first // plan.step],
            device_id=group(0, dg),
            device_id_type=MESH,
        )

    def forward(k, ci):
        for dg in range(1, ng):
            y_copy(k, ci, dg).start()

    own_copies = [
        pltpu.make_async_copy(
            src.at[f, :, pl.ds(first, plan.step), :],
            corr.at[:, pl.ds(held_start(f, g, first), plan.step), :],
            own_sem.at[first // plan.step],
        )
        for first in range(0, per_input, plan.step)
    ]

    def prior_copy(k):
        return pltpu.make_async_remote_copy(
            src_ref=prior.at[0],
            dst_ref=priors.at[f],
            send_sem=qs,
            recv_sem=qr,
            device_id=along_freq(k),
            device_id_type=MESH,
        )

    all_chunks = range(len(chunks))
    ahead = 2

    def send_chunk(ci):
        if ci < len(chunks):
            for k in masks:
                z_copy(k, ci).start()

    for ci in range(ahead):
        send_chunk(ci)
        if ci == 0:
            for k in masks:
                prior_copy(k).start()
    for ci in all_chunks:
        forward(0, ci)
    for copy in own_copies:
        copy.start()
    priors[f] = prior[0]

    n_beams = pointing.shape[1]
    beams = n_beams // ng
    my_beam = beam_channels[f]
    permuted = plan.levels > 1

    def natural(held_index):
        result = held_index
        for start, size, target in plan.segments:
            inside = (held_index >= start) & (held_index < start + size)
            result = jnp.where(inside, held_index + (target - start), result)
        return result

    if permuted:
        along_rows = lax.broadcasted_iota(jnp.int32, (cols, cols), 0)
        along_lanes = lax.broadcasted_iota(jnp.int32, (cols, cols), 1)
        to_held[...] = jnp.where(natural(along_lanes) == along_rows, 1.0, 0.0).astype(jnp.bfloat16)
        to_natural[...] = jnp.where(natural(along_rows) == along_lanes, 1.0, 0.0).astype(jnp.bfloat16)

    def reorder(rows_in, matrix):
        if not permuted:
            return rows_in
        parts = exact_parts(rows_in)
        moved = [
            jnp.dot(parts[:, first : first + cols], matrix[...], preferred_element_type=jnp.float32)
            for first in range(0, rows_in.shape[1], cols)
        ]
        return add_parts(jnp.concatenate(moved, axis=1))

    def point_phases():
        ratio = 0.875 + 0.25 * (my_beam.astype(jnp.float32) + 0.5) / nf
        mine = pl.ds(pl.multiple_of(g * beams, beams), beams)
        east_dir, north_dir = (
            jnp.broadcast_to((pointing[d : d + 1, mine].astype(jnp.float32) + 0.5) / grid_cells - 0.5, (LANES, beams)).T
            for d in (0, 1)
        )
        east, north = (jnp.broadcast_to(coords[d : d + 1, :], (LANES, stations)).T for d in (0, 1))
        station = lax.broadcasted_iota(jnp.int32, (stations, LANES), 0)
        slot_east, slot_north = [], []
        for first in range(0, stations, LANES):
            lanes = slice(first, first + LANES)
            match = station == slots[0:1, lanes]
            slot_east.append(jnp.sum(jnp.where(match, east, 0.0), axis=0, keepdims=True))
            slot_north.append(jnp.sum(jnp.where(match, north, 0.0), axis=0, keepdims=True))
        where = jnp.concatenate(
            [jnp.concatenate(slot_east, axis=1), jnp.concatenate(slot_north, axis=1)], axis=0
        )
        where = reorder(where, to_held)
        for first in range(0, stations, LANES):
            lanes = slice(first, first + LANES)
            phase = 2.0 * math.pi * ratio * (east_dir * where[0:1, lanes] + north_dir * where[1:2, lanes])
            cosine[:, lanes] = jnp.cos(phase)
            sine[:, lanes] = jnp.sin(phase)

    point_phases()

    await_all(priors.at[pl.ds(0, nf - 1)], qr)
    slot_of_mine = 0
    for k in range(nf):
        slot_of_mine = jnp.where(corr_channels[k] == my_beam, k, slot_of_mine)
    z[...] = reorder(priors[slot_of_mine], to_held)
    start_parts = exact_parts(z[...])
    size = plan.level_rows
    for q in range(plan.levels):
        pieces = [start_parts[:, tile * cols + q * size : tile * cols + (q + 1) * size] for tile in range(nt)]
        first_gains[q] = jnp.concatenate(pieces, axis=1)

    scale = 1.0 / (samples * nt)
    odds = list(range(nt - 1, 0, -2))
    evens = [d - 1 for d in odds]

    def a_copy(u):
        return pltpu.make_async_remote_copy(
            src_ref=stage_a[u],
            dst_ref=landed_a[u],
            send_sem=as_,
            recv_sem=ar.at[u],
            device_id=along_tm(1),
            device_id_type=MESH,
        )

    def b_copy(u, d):
        return pltpu.make_async_remote_copy(
            src_ref=stage_b[u].at[d // 2 - 1],
            dst_ref=landed_b[u].at[d // 2 - 1],
            send_sem=bs,
            recv_sem=br.at[u, d // 2 - 1],
            device_id=along_tm(d),
            device_id_type=MESH,
        )

    def first_copy(u, k):
        return pltpu.make_async_remote_copy(
            src_ref=first_src[u].at[peers[k]],
            dst_ref=mid[u].at[f],
            send_sem=fs,
            recv_sem=fr.at[u],
            device_id=along_freq(k),
            device_id_type=MESH,
        )

    def second_copy(u, k):
        return pltpu.make_async_remote_copy(
            src_ref=second_src[u].at[k - 1],
            dst_ref=landed[u].at[f],
            send_sem=ss,
            recv_sem=sr.at[u],
            device_id=along_freq(k),
            device_id_type=MESH,
        )

    def correlate(seg, seg_rows, lane, lanes):
        def stacked(part):
            pieces = []
            for r in range(plan.row_tiles):
                start = pl.multiple_of(g * rows + r * cols + seg, plan.level_rows)
                pieces.append(corr[part, pl.ds(start, seg_rows), :])
            return pieces

        mine = jnp.concatenate(stacked(0) + stacked(1), axis=0)
        count = plan.row_tiles * seg_rows
        others = [
            jnp.concatenate(
                [corr[part, tile * cols + lane : tile * cols + lane + lanes, :] for tile in range(nt)], axis=0
            )
            for part in (0, 1)
        ]
        with_r = nt_dot(mine, others[0])
        with_i = nt_dot(mine, others[1])
        real = (with_r[:count] + with_i[count:]) * scale
        imag = (with_r[count:] - with_i[:count]) * scale
        for part, value in ((0, real), (1, imag)):
            for tile in range(nt):
                for r in range(plan.row_tiles):
                    gram[part, tile, r * cols + seg : r * cols + seg + seg_rows, lane : lane + lanes] = value[
                        r * seg_rows : (r + 1) * seg_rows, tile * lanes : (tile + 1) * lanes
                    ]

    def correlate_level(q):
        size = plan.level_rows
        correlate(0, (q + 1) * size, q * size, size)
        if q >= 2:
            correlate(q * size, size, 0, 2 * size)
        if q % 2:
            correlate(q * size, size, (q - 1) * size, size)

    def gather_level(q):
        pieces = [
            jnp.concatenate([corr[part, tile * cols + q * size : tile * cols + (q + 1) * size, :] for tile in range(nt)], axis=0)
            for part in (0, 1)
        ]
        with_r, with_i = (
            add_parts(jnp.dot(first_gains[q], piece, preferred_element_type=jnp.float32)) for piece in pieces
        )
        real = with_r[0:1] + with_i[1:2]
        imag = with_r[1:2] - with_i[0:1]
        if q:
            real = real + gathered[0:1]
            imag = imag + gathered[1:2]
        gathered[0:1] = real
        gathered[1:2] = imag

    def first_product():
        parts = exact_parts(gathered[...] * scale)
        mine = pl.ds(pl.multiple_of(g * rows, rows), rows)
        with_r = add_parts(nt_dot(parts, corr[0, mine, :]))
        with_i = add_parts(nt_dot(parts, corr[1, mine, :]))
        updates[0, slot, 0:1] = with_r[0:1] - with_i[1:2]
        updates[0, slot, 1:2] = with_r[1:2] + with_i[0:1]

    slot = g * nt + t

    def update_copy(iteration, o):
        dt, dg = offsets[o]
        return pltpu.make_async_remote_copy(
            src_ref=updates.at[iteration, slot],
            dst_ref=updates.at[iteration, slot],
            send_sem=us,
            recv_sem=ur.at[iteration],
            device_id=group(dt, dg),
            device_id_type=MESH,
        )

    def send_updates(iteration):
        for o in range(len(offsets)):
            update_copy(iteration, o).start()

    def from_gram(u, part, d):
        seg, seg_rows, lane, lanes, side_by_side = plan.units[u]
        return jnp.concatenate(
            [
                gram[part, tiles[d], r * cols + seg : r * cols + seg + seg_rows, lane : lane + lanes]
                for r in range(plan.row_tiles)
            ],
            axis=1 if side_by_side else 0,
        )

    def send_pair(u):
        lanes = plan.unit_shape(u)[1]
        for j, d in enumerate(odds):
            for part in (0, 1):
                stage_a[u][part, :, j * lanes : (j + 1) * lanes] = from_gram(u, part, d).astype(jnp.bfloat16)
        a_copy(u).start()

    def sum_pair(u):
        lanes = plan.unit_shape(u)[1]
        a_copy(u).wait_recv()
        for j, d in enumerate(evens):
            if d:
                for part in (0, 1):
                    theirs = landed_a[u][part, :, j * lanes : (j + 1) * lanes].astype(jnp.float32)
                    stage_b[u][d // 2 - 1, part] = (from_gram(u, part, d) + theirs).astype(jnp.bfloat16)
        for d in evens:
            if d:
                b_copy(u, d).start()

    def sum_rest(u):
        total_rows, lanes = plan.unit_shape(u)
        piece = total_rows // nf
        for d in evens:
            if d:
                b_copy(u, d).wait_recv()
        j = len(evens) - 1
        for part in (0, 1):
            total = from_gram(u, part, 0) + landed_a[u][part, :, j * lanes : (j + 1) * lanes].astype(jnp.float32)
            for d in evens:
                if d:
                    total = total + landed_b[u][d // 2 - 1, part].astype(jnp.float32)
            total = total.astype(jnp.bfloat16)
            for p in range(nf):
                first_src[u][p, part] = total[p * piece : (p + 1) * piece]
        mid[u][f] = first_src[u][f]
        for k in masks:
            first_copy(u, k).start()

    def source_of(slot):
        wanted = corr_channels[slot]
        source = 0
        for s in range(nf):
            source = jnp.where(beam_channels[s] == wanted, s, source)
        return source

    def hand_on(u):
        await_all(mid[u].at[pl.ds(0, nf - 1)], fr.at[u])
        for k in masks:
            second_src[u][k - 1] = mid[u][source_of(peers[k])]
        landed[u][f] = mid[u][source_of(f)]
        for k in masks:
            second_copy(u, k).start()

    nearest_first = [1] + masks[:-1] if nf > 1 else []

    sent = [ahead]

    def send_until(count):
        while sent[0] < count:
            send_chunk(sent[0])
            sent[0] += 1

    def relay(ci, spare=0):
        for k in nearest_first:
            z_copy(k, ci).wait_recv()
            forward(k, ci)
        send_until(ci + 1 + ahead + spare)

    def of_level(q):
        return [ci for ci in all_chunks if chunks[ci][1] // plan.step == q]

    def await_level(q):
        own_copies[q].wait()
        await_all(corr.at[:, pl.ds(0, (ng - 1) * nf * plan.step), :], yr.at[q])

    last = plan.levels - 1
    early_units = [0, 1, 2] if last else []
    late_units = [u for u in range(nu) if u not in early_units]
    ready = {last - 1: [0], last: [1, 2]} if last else {}
    for q in range(plan.levels):
        members = of_level(q)
        relay(members[0], spare=1)
        if q:
            await_level(q - 1)
            gather_level(q - 1)
            correlate_level(q - 1)
        for u in ready.get(q, []):
            send_pair(u)
        relay(members[1])
        for u in ready.get(q, []):
            sum_pair(u)
        if q == last:
            for u in early_units[:1]:
                sum_rest(u)
        for ci in members[2:]:
            relay(ci)
    for u in early_units[1:]:
        sum_rest(u)
    await_level(last)
    gather_level(last)
    first_product()
    send_updates(0)
    correlate_level(last)
    for u in late_units:
        send_pair(u)
    for u in early_units[:1]:
        hand_on(u)
    strip = LANES
    per_tile = cols // LANES

    beside = {i: [] for i in range(ITERS + 1)}

    def plan_work(iteration, work, u):
        beside[min(iteration, ITERS)].append(functools.partial(work, u))

    for u in late_units:
        plan_work(1, sum_pair, u)
    for u in early_units[1:]:
        plan_work(1, hand_on, u)
    for u in late_units:
        plan_work(2, sum_rest, u)
    for i, u in enumerate(late_units):
        plan_work(i + 3, hand_on, u)
    for iteration in range(ITERS):
        power = jnp.sum(z[...] * z[...]) + 1e-06

        def product(r, carry):
            here = pl.ds(pl.multiple_of(r * strip, strip), strip)
            total_r = jnp.zeros((strip, LANES), jnp.float32)
            total_i = jnp.zeros((strip, LANES), jnp.float32)
            for c in range(inputs // LANES):
                lanes = slice(c * LANES, (c + 1) * LANES)
                tile, inner = c // per_tile, slice(c % per_tile * LANES, (c % per_tile + 1) * LANES)
                part_r = gram[0, tile, here, inner]
                part_i = gram[1, tile, here, inner]
                gain_r = z[0:1, lanes]
                gain_i = z[1:2, lanes]
                total_r += part_r * gain_r - part_i * gain_i
                total_i += part_i * gain_r + part_r * gain_i
            updates[iteration, slot, 0:1, here] = jnp.sum(total_r.T, axis=0, keepdims=True)
            updates[iteration, slot, 1:2, here] = jnp.sum(total_i.T, axis=0, keepdims=True)
            return carry

        if iteration:
            lax.fori_loop(0, rows // strip, product, 0)
            send_updates(iteration)
        for work in beside[iteration]:
            work()
        await_all(updates.at[iteration, pl.ds(0, len(offsets))], ur.at[iteration])
        for h in range(ng):
            total = updates[iteration, h * nt]
            for other in range(1, nt):
                total = total + updates[iteration, h * nt + other]
            lanes = slice(h * rows, (h + 1) * rows)
            z[:, lanes] = 0.5 * (z[:, lanes] + inputs * total / power)

    gains[f] = reorder(z[...], to_natural)

    def gain_copy(k):
        return pltpu.make_async_remote_copy(
            src_ref=gains.at[f],
            dst_ref=gains.at[f],
            send_sem=gs,
            recv_sem=gr,
            device_id=along_freq(k),
            device_id_type=MESH,
        )

    for k in masks:
        gain_copy(k).start()

    for work in beside[ITERS]:
        work()

    factor = 1.0 / math.sqrt(stations)
    for p in (0, 1):
        gain_r = z[0:1, p * stations : (p + 1) * stations]
        gain_i = z[1:2, p * stations : (p + 1) * stations]
        denom = jnp.maximum(gain_r * gain_r + gain_i * gain_i, 0.5)
        along_r = gain_r / denom
        along_i = gain_i / denom
        cos = cosine[...]
        sin = sine[...]
        w_r = ((cos * along_r - sin * along_i) * factor).astype(jnp.bfloat16)
        w_i = (-(cos * along_i + sin * along_r) * factor).astype(jnp.bfloat16)
        left[p, 0:beams] = w_r
        left[p, beams:] = w_i
        right[p, 0:beams] = -w_i
        right[p, beams:] = w_r

    def beamform(p):
        rows_p = slice(p * stations, (p + 1) * stations)
        result = jnp.dot(left[p], corr[0, rows_p, :], preferred_element_type=jnp.float32)
        result = result + jnp.dot(right[p], corr[1, rows_p, :], preferred_element_type=jnp.float32)
        result = result.astype(jnp.bfloat16)
        beams_out[0, p, 0] = result[:beams]
        beams_out[0, p, 1] = result[beams:]

    for p in (0, 1):
        beamform(p)

    for u in range(nu):
        await_all(landed[u].at[pl.ds(0, nf - 1)], sr.at[u])
    for part in (0, 1):
        strips = [
            jnp.concatenate([landed[u][p, part] for p in range(nf)], axis=0) for u in range(nu)
        ]
        for r in range(plan.row_tiles):
            if permuted:
                first, second = plan.units[0][1], plan.units[1][1]
                early = jnp.concatenate(
                    [strips[0][r * first : (r + 1) * first], strips[1][r * second : (r + 1) * second]], axis=0
                )
                side = slice(r * plan.level_rows, (r + 1) * plan.level_rows)
                tile_rows = [
                    jnp.concatenate([early, strips[2][:, side], strips[3][:, side]], axis=1),
                    strips[4][side],
                ]
            else:
                here = slice(r * cols, (r + 1) * cols)
                tile_rows = [jnp.concatenate([strips[0][here], strips[1][here]], axis=1)]
            tile = jnp.concatenate(tile_rows, axis=0)
            if not permuted:
                vis_out[0, part, r * cols : (r + 1) * cols, :] = tile
                continue
            tile = jnp.dot(
                tile, to_natural[...], preferred_element_type=jnp.float32
            ).astype(jnp.bfloat16)
            for start, size, target in plan.segments:
                vis_out[0, part, r * cols + target : r * cols + target + size, :] = tile[start : start + size]

    await_all(gains.at[pl.ds(0, nf - 1)], gr)
    gains_out[0] = gains[source_of(f)]

    await_all(priors.at[pl.ds(0, nf - 1)], qs)
    await_all(gains.at[pl.ds(0, nf - 1)], gs)
    await_all(src.at[pl.ds(0, nf - 1)], zs)
    for dg in range(1, ng):
        await_all(src, ys.at[dg - 1])
    await_all(gram.at[0, pl.ds(0, len(odds))], as_)
    if len(odds) > 1:
        await_all(gram.at[0, pl.ds(0, len(odds) - 1)], bs)
    for sem in (fs, ss):
        await_all(gram.at[0, 0, pl.ds(0, rows // nf * (nf - 1))], sem)
    await_all(updates.at[:, pl.ds(0, len(offsets))], us)


def finish(vis_in, gains_in, beams_in, vis_out, gains_out, beams_out, wide, sem):
    puts = [pltpu.make_async_copy(beams_in, beams_out, sem.at[0]), pltpu.make_async_copy(gains_in, gains_out, sem.at[1])]
    for put in puts:
        put.start()
    for part in (0, 1):
        wide[:, part] = vis_in[:, part].astype(jnp.float32)
        puts.append(pltpu.make_async_copy(wide.at[:, part], vis_out.at[:, part], sem.at[2 + part]))
        puts[-1].start()
    for put in puts:
        put.wait()


def body(
    voltages,
    prior_gains,
    station_flags,
    ingest_map,
    station_coords,
    pointing,
    corr_channels,
    beam_channels,
):
    nf = lax.axis_size("freq")
    nt = lax.axis_size("tm")
    ng = lax.axis_size("grp")
    _, _, per_input, samples = voltages.shape
    stations = ingest_map.shape[0]
    plan = Plan(nf, nt, ng, per_input, samples)
    inputs, rows, cols = plan.inputs, plan.rows, plan.cols
    part_beams = pointing.shape[1] // ng
    nc, nu = len(plan.chunks), len(plan.units)
    pairs = nt // 2
    dma = pltpu.SemaphoreType.DMA
    hbm = pl.BlockSpec(memory_space=pltpu.HBM)
    vmem = pl.BlockSpec(memory_space=pltpu.VMEM)
    shapes = [plan.unit_shape(u) for u in range(nu)]

    def bf16(*shape):
        return pltpu.VMEM(shape, jnp.bfloat16)

    def f32(*shape):
        return pltpu.VMEM(shape, jnp.float32)

    kept_bytes = 4 * rows * cols + 8 * inputs + 8 * part_beams * samples + 61440

    vis, gains, beams = pl.pallas_call(
        functools.partial(kernel, plan),
        out_shape=(
            pltpu.VMEM((1, 2, rows, cols), jnp.bfloat16),
            pltpu.VMEM((1, 2, inputs), jnp.float32),
            pltpu.VMEM((1, 2, 2, part_beams, samples), jnp.bfloat16),
        ),
        in_specs=[hbm] * 8,
        out_specs=(vmem, vmem, vmem),
        scratch_shapes=[
            bf16(nf, 2, per_input, samples),
            bf16(2, inputs, samples),
            f32(stations, LANES),
            f32(part_beams, stations),
            f32(part_beams, stations),
            bf16(cols, cols),
            bf16(cols, cols),
            bf16(2, 2 * part_beams, stations),
            bf16(2, 2 * part_beams, stations),
            f32(2, nt, rows, cols),
            f32(nf, 2, inputs),
            f32(ITERS, ng * nt, 2, rows),
            f32(2, inputs),
            f32(nf, 2, inputs),
            bf16(plan.levels, 6, inputs // plan.levels),
            f32(2, samples),
        ]
        + [bf16(2, r, pairs * w) for r, w in shapes] * 2
        + [bf16(pairs - 1, 2, r, w) for r, w in shapes] * 2
        + [bf16(nf, 2, r // nf, w) for r, w in shapes] * 2
        + [bf16(nf - 1, 2, r // nf, w) for r, w in shapes]
        + [bf16(nf, 2, r // nf, w) for r, w in shapes]
        + [
            dma,
            dma((nf - 1, nc)),
            dma((ng - 1,)),
            dma((plan.levels,)),
            dma((plan.levels,)),
            dma,
            dma,
            dma,
            dma((ITERS,)),
            dma,
            dma,
            dma,
            dma((nu,)),
            dma,
            dma((nu, pairs - 1)),
            dma,
            dma((nu,)),
            dma,
            dma((nu,)),
            dma((8,)),
            pltpu.VMEM(voltages.shape, jnp.bfloat16),
            pltpu.VMEM(prior_gains.shape, jnp.float32),
            pltpu.VMEM((1, stations), jnp.int32),
            pltpu.VMEM((1, stations), jnp.int32),
            pltpu.VMEM(station_coords.shape, jnp.float32),
            pltpu.VMEM(pointing.shape, jnp.int32),
            pltpu.SMEM(corr_channels.shape, jnp.int32),
            pltpu.SMEM(beam_channels.shape, jnp.int32),
        ],
        compiler_params=pltpu.CompilerParams(
            collective_id=0, has_side_effects=True, vmem_limit_bytes=67043328 - kept_bytes
        ),
    )(
        voltages,
        prior_gains,
        station_flags[None],
        ingest_map[None],
        station_coords,
        pointing,
        corr_channels,
        beam_channels,
    )
    results = (jax.ShapeDtypeStruct(vis.shape, jnp.float32), gains, beams)
    return pl.pallas_call(
        finish,
        out_shape=tuple(jax.ShapeDtypeStruct(r.shape, r.dtype) for r in results),
        in_specs=[vmem] * 3,
        out_specs=(hbm,) * 3,
        scratch_shapes=[
            f32(*vis.shape),
            dma((4,)),
        ],
        compiler_params=pltpu.CompilerParams(vmem_limit_bytes=4 * 1024 * 1024),
    )(vis, gains, beams)


def solution(mesh):
    return jax.shard_map(
        body,
        mesh=mesh,
        in_specs=(
            P(None, None, ("freq", "grp"), "tm"),
            P("freq", None, None),
            P(),
            P(),
            P(),
            P(),
            P(),
            P(),
        ),
        out_specs=(
            P("freq", None, "grp", "tm"),
            P("freq", None, None),
            P("freq", None, None, "grp", "tm"),
        ),
        check_vma=False,
    )
```

```python
import functools
import math

import jax
import jax.numpy as jnp
from jax import lax
from jax.experimental import pallas as pl
from jax.experimental.pallas import tpu as pltpu
from jax.sharding import PartitionSpec as P

ITERS = 4
LANES = 128
grid_cells = 64.0
MESH = pl.DeviceIdType.MESH


def partner(index, mask, count):
    result, bit = 0, 1
    while bit < count:
        digit = (index // bit) % 2
        result = result + bit * ((1 - digit) if mask & bit else digit)
        bit *= 2
    return result


def nt_dot(a, b):
    return lax.dot_general(a, b, (((1,), (1,)), ((), ())), preferred_element_type=jnp.float32)


def exact_parts(values):
    high = values.astype(jnp.bfloat16)
    rest = values - high.astype(jnp.float32)
    middle = rest.astype(jnp.bfloat16)
    low = (rest - middle.astype(jnp.float32)).astype(jnp.bfloat16)
    return jnp.concatenate([high, middle, low], axis=0)


def add_parts(values):
    count = values.shape[0] // 3
    return (values[2 * count :] + values[count : 2 * count]) + values[:count]


class Plan:
    def __init__(self, nf, nt, ng, per_input, samples):
        self.nf, self.nt, self.ng = nf, nt, ng
        self.per_input, self.samples = per_input, samples
        self.inputs = nf * ng * per_input
        self.rows = self.inputs // ng
        self.cols = self.inputs // nt
        self.blocks = self.cols // per_input
        self.row_tiles = nt // ng
        self.levels = 4 if per_input % 64 == 0 else 1
        self.step = per_input // self.levels
        self.level_rows = self.cols // self.levels
        count = 16 if self.step % 16 == 0 else self.step
        self.chunks = tuple((part, first, count) for first in range(0, per_input, count) for part in (0, 1))
        half = self.cols // 2
        if self.levels > 1:
            most = self.cols - self.level_rows
            units = [(0, half, 0, half, False), (half, most - half, 0, half, False)]
            units += [(0, most, lane, self.level_rows, True) for lane in (half, most)]
            rest = self.level_rows // 2
            units += [(first, rest, 0, self.cols, False) for first in (most, most + rest)]
        else:
            units = [(0, self.cols, 0, half, False), (0, self.cols, half, half, False)]
        self.units = tuple(units)
        self.segments = tuple(
            (q * self.level_rows + b * self.step, self.step, b * per_input + q * self.step)
            for q in range(self.levels)
            for b in range(self.blocks)
        )

    def unit_shape(self, unit):
        _, seg_rows, _, lanes, beside = self.units[unit]
        return (seg_rows, self.row_tiles * lanes) if beside else (self.row_tiles * seg_rows, lanes)


def kernel(plan, *refs):
    nf, nt, ng = plan.nf, plan.nt, plan.ng
    nu = len(plan.units)
    operands, refs = refs[:8], refs[8:]
    vis_out, gains_out, beams_out = refs[:3]
    refs = refs[3:]

    def take(count):
        nonlocal refs
        taken, refs = refs[:count], refs[count:]
        return taken

    src, corr, keep, cosine, sine, to_held, to_natural, left, right, gram = take(10)
    priors, updates, z, gains, first_gains, gathered = take(6)
    stage_a, landed_a, stage_b, landed_b = (take(nu) for _ in range(4))
    first_src, mid, second_src, landed = (take(nu) for _ in range(4))
    zs, zr, ys, yr, own_sem, qs, qr, us, ur, gs, gr, as_, ar, bs, br, fs, fr, ss, sr, in_sem = take(20)
    held = refs
    voltages, prior, flags, slots, coords, pointing, corr_channels, beam_channels = held
    loads = [pltpu.make_async_copy(operands[i], held[i], in_sem.at[i]) for i in range(8)]
    for load in loads:
        load.start()
    f = lax.axis_index("freq")
    t = lax.axis_index("tm")
    g = lax.axis_index("grp")
    per_input, samples = plan.per_input, plan.samples
    inputs, rows, cols = plan.inputs, plan.rows, plan.cols
    stations = inputs // 2
    chunks = plan.chunks
    offsets = [(dt, dg) for dg in range(ng) for dt in range(nt) if (dt, dg) != (0, 0)]
    masks = list(range(nf - 1, 0, -1))
    peers = {k: partner(f, k, nf) for k in range(nf)}
    tiles = {d: partner(t, d, nt) for d in range(nt)}

    def group(dt, dg):
        return {"freq": f, "tm": (t + dt) % nt, "grp": (g + dg) % ng}

    def along_freq(k):
        return {"freq": peers[k], "tm": t, "grp": g}

    def along_tm(d):
        return {"freq": f, "tm": tiles[d], "grp": g}

    def await_all(ref, sem):
        pltpu.make_async_copy(ref, ref, sem).wait()

    barrier = pltpu.get_barrier_semaphore()
    for k in masks:
        pl.semaphore_signal(barrier, inc=1, device_id=along_freq(k), device_id_type=MESH)
    for dt, dg in offsets:
        pl.semaphore_signal(barrier, inc=1, device_id=group(dt, dg), device_id_type=MESH)
    for load in loads:
        load.wait()

    slot_rows = jnp.broadcast_to(slots[...].astype(jnp.float32), (LANES, stations)).T
    flagged = jnp.zeros((stations, LANES), jnp.float32)
    for first in range(0, stations, LANES):
        lane = lax.broadcasted_iota(jnp.int32, (stations, LANES), 1) + first
        flag = flags[0:1, first : first + LANES].astype(jnp.float32)
        flagged += jnp.where(slot_rows == lane.astype(jnp.float32), flag, 0.0)
    flagged = jnp.sum(flagged, axis=1, keepdims=True)
    keep[...] = jnp.broadcast_to(1.0 - flagged, (stations, LANES))
    first_slot = pl.multiple_of(((f * ng + g) * per_input) % stations, per_input)
    kept = keep[pl.ds(first_slot, per_input), 0:1].astype(jnp.bfloat16)

    for k in masks + [0]:
        for part in (0, 1):
            src[peers[k], part] = voltages[beam_channels[peers[k]], part] * kept

    pl.semaphore_wait(barrier, len(masks) + len(offsets))

    def held_start(owner, member, first):
        block = owner * ng + member
        level = first // plan.step
        start = (block // plan.blocks) * cols + level * plan.level_rows + (block % plan.blocks) * plan.step
        return pl.multiple_of(start + first % plan.step, math.gcd(plan.step, 16))

    def place(owner, chunk):
        part, first, count = chunk
        return corr.at[part, pl.ds(held_start(owner, g, first), count), :]

    def z_copy(k, ci):
        part, first, count = chunks[ci]
        return pltpu.make_async_remote_copy(
            src_ref=src.at[peers[k], part, pl.ds(first, count), :],
            dst_ref=place(f, chunks[ci]),
            send_sem=zs,
            recv_sem=zr.at[k - 1, ci],
            device_id=along_freq(k),
            device_id_type=MESH,
        )

    def y_copy(k, ci, dg):
        part, first, count = chunks[ci]
        spot = place(peers[k], chunks[ci])
        return pltpu.make_async_remote_copy(
            src_ref=src.at[f, part, pl.ds(first, count), :] if k == 0 else spot,
            dst_ref=spot,
            send_sem=ys.at[dg - 1],
            recv_sem=yr.at[first // plan.step],
            device_id=group(0, dg),
            device_id_type=MESH,
        )

    def forward(k, ci):
        for dg in range(1, ng):
            y_copy(k, ci, dg).start()

    own_copies = [
        pltpu.make_async_copy(
            src.at[f, :, pl.ds(first, plan.step), :],
            corr.at[:, pl.ds(held_start(f, g, first), plan.step), :],
            own_sem.at[first // plan.step],
        )
        for first in range(0, per_input, plan.step)
    ]

    def prior_copy(k):
        return pltpu.make_async_remote_copy(
            src_ref=prior.at[0],
            dst_ref=priors.at[f],
            send_sem=qs,
            recv_sem=qr,
            device_id=along_freq(k),
            device_id_type=MESH,
        )

    all_chunks = range(len(chunks))
    ahead = 2

    sent = [0]

    def send_until(count):
        while sent[0] < min(count, len(chunks)):
            for k in masks:
                z_copy(k, sent[0]).start()
            sent[0] += 1

    send_until(1)
    for k in masks:
        prior_copy(k).start()
    send_until(ahead)
    for ci in all_chunks:
        forward(0, ci)
    for copy in own_copies:
        copy.start()
    priors[f] = prior[0]

    n_beams = pointing.shape[1]
    beams = n_beams // ng
    my_beam = beam_channels[f]
    permuted = plan.levels > 1

    def natural(held_index):
        result = held_index
        for start, size, target in plan.segments:
            inside = (held_index >= start) & (held_index < start + size)
            result = jnp.where(inside, held_index + (target - start), result)
        return result

    if permuted:
        along_rows = lax.broadcasted_iota(jnp.int32, (cols, cols), 0)
        along_lanes = lax.broadcasted_iota(jnp.int32, (cols, cols), 1)
        to_held[...] = jnp.where(natural(along_lanes) == along_rows, 1.0, 0.0).astype(jnp.bfloat16)
        to_natural[...] = jnp.where(natural(along_rows) == along_lanes, 1.0, 0.0).astype(jnp.bfloat16)

    def reorder(rows_in, matrix):
        if not permuted:
            return rows_in
        parts = exact_parts(rows_in)
        moved = [
            jnp.dot(parts[:, first : first + cols], matrix[...], preferred_element_type=jnp.float32)
            for first in range(0, rows_in.shape[1], cols)
        ]
        return add_parts(jnp.concatenate(moved, axis=1))

    def point_phases():
        ratio = 0.875 + 0.25 * (my_beam.astype(jnp.float32) + 0.5) / nf
        mine = pl.ds(pl.multiple_of(g * beams, beams), beams)
        east_dir, north_dir = (
            jnp.broadcast_to((pointing[d : d + 1, mine].astype(jnp.float32) + 0.5) / grid_cells - 0.5, (LANES, beams)).T
            for d in (0, 1)
        )
        east, north = (jnp.broadcast_to(coords[d : d + 1, :], (LANES, stations)).T for d in (0, 1))
        station = lax.broadcasted_iota(jnp.int32, (stations, LANES), 0)
        slot_east, slot_north = [], []
        for first in range(0, stations, LANES):
            lanes = slice(first, first + LANES)
            match = station == slots[0:1, lanes]
            slot_east.append(jnp.sum(jnp.where(match, east, 0.0), axis=0, keepdims=True))
            slot_north.append(jnp.sum(jnp.where(match, north, 0.0), axis=0, keepdims=True))
        where = jnp.concatenate(
            [jnp.concatenate(slot_east, axis=1), jnp.concatenate(slot_north, axis=1)], axis=0
        )
        where = reorder(where, to_held)
        for first in range(0, stations, LANES):
            lanes = slice(first, first + LANES)
            phase = 2.0 * math.pi * ratio * (east_dir * where[0:1, lanes] + north_dir * where[1:2, lanes])
            cosine[:, lanes] = jnp.cos(phase)
            sine[:, lanes] = jnp.sin(phase)

    point_phases()

    await_all(priors.at[pl.ds(0, nf - 1)], qr)
    slot_of_mine = 0
    for k in range(nf):
        slot_of_mine = jnp.where(corr_channels[k] == my_beam, k, slot_of_mine)
    z[...] = reorder(priors[slot_of_mine], to_held)
    start_parts = exact_parts(z[...])
    size = plan.level_rows
    for q in range(plan.levels):
        pieces = [start_parts[:, tile * cols + q * size : tile * cols + (q + 1) * size] for tile in range(nt)]
        first_gains[q] = jnp.concatenate(pieces, axis=1)

    scale = 1.0 / (samples * nt)
    odds = list(range(nt - 1, 0, -2))
    evens = [d - 1 for d in odds]

    def a_copy(u):
        return pltpu.make_async_remote_copy(
            src_ref=stage_a[u],
            dst_ref=landed_a[u],
            send_sem=as_,
            recv_sem=ar.at[u],
            device_id=along_tm(1),
            device_id_type=MESH,
        )

    def b_copy(u, d):
        return pltpu.make_async_remote_copy(
            src_ref=stage_b[u].at[d // 2 - 1],
            dst_ref=landed_b[u].at[d // 2 - 1],
            send_sem=bs,
            recv_sem=br.at[u, d // 2 - 1],
            device_id=along_tm(d),
            device_id_type=MESH,
        )

    def first_copy(u, k):
        return pltpu.make_async_remote_copy(
            src_ref=first_src[u].at[peers[k]],
            dst_ref=mid[u].at[f],
            send_sem=fs,
            recv_sem=fr.at[u],
            device_id=along_freq(k),
            device_id_type=MESH,
        )

    def second_copy(u, k):
        return pltpu.make_async_remote_copy(
            src_ref=second_src[u].at[k - 1],
            dst_ref=landed[u].at[f],
            send_sem=ss,
            recv_sem=sr.at[u],
            device_id=along_freq(k),
            device_id_type=MESH,
        )

    def correlate(seg, seg_rows, lane, lanes):
        def stacked(part):
            pieces = []
            for r in range(plan.row_tiles):
                start = pl.multiple_of(g * rows + r * cols + seg, plan.level_rows)
                pieces.append(corr[part, pl.ds(start, seg_rows), :])
            return pieces

        mine = jnp.concatenate(stacked(0) + stacked(1), axis=0)
        count = plan.row_tiles * seg_rows
        others = [
            jnp.concatenate(
                [corr[part, tile * cols + lane : tile * cols + lane + lanes, :] for tile in range(nt)], axis=0
            )
            for part in (0, 1)
        ]
        with_r = nt_dot(mine, others[0])
        with_i = nt_dot(mine, others[1])
        real = (with_r[:count] + with_i[count:]) * scale
        imag = (with_r[count:] - with_i[:count]) * scale
        for part, value in ((0, real), (1, imag)):
            for tile in range(nt):
                for r in range(plan.row_tiles):
                    gram[part, tile, r * cols + seg : r * cols + seg + seg_rows, lane : lane + lanes] = value[
                        r * seg_rows : (r + 1) * seg_rows, tile * lanes : (tile + 1) * lanes
                    ]

    def correlate_level(q):
        size = plan.level_rows
        correlate(0, (q + 1) * size, q * size, size)
        if q >= 2:
            correlate(q * size, size, 0, 2 * size)
        if q % 2:
            correlate(q * size, size, (q - 1) * size, size)

    def gather_level(q):
        pieces = [
            jnp.concatenate([corr[part, tile * cols + q * size : tile * cols + (q + 1) * size, :] for tile in range(nt)], axis=0)
            for part in (0, 1)
        ]
        with_r, with_i = (
            add_parts(jnp.dot(first_gains[q], piece, preferred_element_type=jnp.float32)) for piece in pieces
        )
        real = with_r[0:1] + with_i[1:2]
        imag = with_r[1:2] - with_i[0:1]
        if q:
            real = real + gathered[0:1]
            imag = imag + gathered[1:2]
        gathered[0:1] = real
        gathered[1:2] = imag

    def first_product():
        parts = exact_parts(gathered[...] * scale)
        mine = pl.ds(pl.multiple_of(g * rows, rows), rows)
        with_r = add_parts(nt_dot(parts, corr[0, mine, :]))
        with_i = add_parts(nt_dot(parts, corr[1, mine, :]))
        updates[0, slot, 0:1] = with_r[0:1] - with_i[1:2]
        updates[0, slot, 1:2] = with_r[1:2] + with_i[0:1]

    slot = g * nt + t

    def update_copy(iteration, o):
        dt, dg = offsets[o]
        return pltpu.make_async_remote_copy(
            src_ref=updates.at[iteration, slot],
            dst_ref=updates.at[iteration, slot],
            send_sem=us,
            recv_sem=ur.at[iteration],
            device_id=group(dt, dg),
            device_id_type=MESH,
        )

    def send_updates(iteration):
        for o in range(len(offsets)):
            update_copy(iteration, o).start()

    def from_gram(u, part, d):
        seg, seg_rows, lane, lanes, side_by_side = plan.units[u]
        return jnp.concatenate(
            [
                gram[part, tiles[d], r * cols + seg : r * cols + seg + seg_rows, lane : lane + lanes]
                for r in range(plan.row_tiles)
            ],
            axis=1 if side_by_side else 0,
        )

    def send_pair(u):
        lanes = plan.unit_shape(u)[1]
        for j, d in enumerate(odds):
            for part in (0, 1):
                stage_a[u][part, :, j * lanes : (j + 1) * lanes] = from_gram(u, part, d).astype(jnp.bfloat16)
        a_copy(u).start()

    def sum_pair(u):
        lanes = plan.unit_shape(u)[1]
        a_copy(u).wait_recv()
        for j, d in enumerate(evens):
            if d:
                for part in (0, 1):
                    theirs = landed_a[u][part, :, j * lanes : (j + 1) * lanes].astype(jnp.float32)
                    stage_b[u][d // 2 - 1, part] = (from_gram(u, part, d) + theirs).astype(jnp.bfloat16)
        for d in evens:
            if d:
                b_copy(u, d).start()

    def sum_rest(u):
        total_rows, lanes = plan.unit_shape(u)
        piece = total_rows // nf
        for d in evens:
            if d:
                b_copy(u, d).wait_recv()
        j = len(evens) - 1
        for part in (0, 1):
            total = from_gram(u, part, 0) + landed_a[u][part, :, j * lanes : (j + 1) * lanes].astype(jnp.float32)
            for d in evens:
                if d:
                    total = total + landed_b[u][d // 2 - 1, part].astype(jnp.float32)
            total = total.astype(jnp.bfloat16)
            for p in range(nf):
                first_src[u][p, part] = total[p * piece : (p + 1) * piece]
        mid[u][f] = first_src[u][f]
        for k in masks:
            first_copy(u, k).start()

    def source_of(slot):
        wanted = corr_channels[slot]
        source = 0
        for s in range(nf):
            source = jnp.where(beam_channels[s] == wanted, s, source)
        return source

    def hand_on(u):
        await_all(mid[u].at[pl.ds(0, nf - 1)], fr.at[u])
        for k in masks:
            second_src[u][k - 1] = mid[u][source_of(peers[k])]
        landed[u][f] = mid[u][source_of(f)]
        for k in masks:
            second_copy(u, k).start()

    nearest_first = masks[-1:] + masks[:-1]

    def relay(ci, spare=0):
        for k in nearest_first:
            z_copy(k, ci).wait_recv()
            forward(k, ci)
        send_until(ci + 1 + ahead + spare)

    def of_level(q):
        return [ci for ci in all_chunks if chunks[ci][1] // plan.step == q]

    def await_level(q):
        own_copies[q].wait()
        await_all(corr.at[:, pl.ds(0, (ng - 1) * nf * plan.step), :], yr.at[q])

    last = plan.levels - 1
    early_units = [0, 1, 2] if last else []
    late_units = [u for u in range(nu) if u not in early_units]
    ready = {last - 1: [0], last: [1, 2]} if last else {}
    for q in range(plan.levels):
        members = of_level(q)
        relay(members[0], spare=1)
        if q:
            await_level(q - 1)
            gather_level(q - 1)
            correlate_level(q - 1)
        for u in ready.get(q, []):
            send_pair(u)
        relay(members[1])
        for u in ready.get(q, []):
            sum_pair(u)
        if q == last:
            for u in early_units[:1]:
                sum_rest(u)
        for ci in members[2:]:
            relay(ci)
    for u in early_units[1:]:
        sum_rest(u)
    await_level(last)
    gather_level(last)
    first_product()
    send_updates(0)
    for u in early_units[:1]:
        hand_on(u)
    correlate_level(last)
    for u in late_units:
        send_pair(u)
    strip = LANES
    per_tile = cols // LANES

    beside = {i: [] for i in range(ITERS + 1)}

    def plan_work(iteration, work, u):
        beside[min(iteration, ITERS)].append(functools.partial(work, u))

    for u in late_units:
        plan_work(1, sum_pair, u)
    for u in early_units[1:]:
        plan_work(1, hand_on, u)
    for u in late_units:
        plan_work(2, sum_rest, u)
    for i, u in enumerate(late_units):
        plan_work(4 if i > 1 else 3, hand_on, u)
    for iteration in range(ITERS):
        power = jnp.sum(z[...] * z[...]) + 1e-06

        def product(r, carry):
            here = pl.ds(pl.multiple_of(r * strip, strip), strip)
            total_r = jnp.zeros((strip, LANES), jnp.float32)
            total_i = jnp.zeros((strip, LANES), jnp.float32)
            for c in range(inputs // LANES):
                lanes = slice(c * LANES, (c + 1) * LANES)
                tile, inner = c // per_tile, slice(c % per_tile * LANES, (c % per_tile + 1) * LANES)
                part_r = gram[0, tile, here, inner]
                part_i = gram[1, tile, here, inner]
                gain_r = z[0:1, lanes]
                gain_i = z[1:2, lanes]
                total_r += part_r * gain_r - part_i * gain_i
                total_i += part_i * gain_r + part_r * gain_i
            updates[iteration, slot, 0:1, here] = jnp.sum(total_r.T, axis=0, keepdims=True)
            updates[iteration, slot, 1:2, here] = jnp.sum(total_i.T, axis=0, keepdims=True)
            return carry

        if iteration:
            lax.fori_loop(0, rows // strip, product, 0)
            send_updates(iteration)
        for work in beside[iteration]:
            work()
        await_all(updates.at[iteration, pl.ds(0, len(offsets))], ur.at[iteration])
        for h in range(ng):
            total = updates[iteration, h * nt]
            for other in range(1, nt):
                total = total + updates[iteration, h * nt + other]
            lanes = slice(h * rows, (h + 1) * rows)
            z[:, lanes] = 0.5 * (z[:, lanes] + inputs * total / power)

    gains[f] = reorder(z[...], to_natural)

    def gain_copy(k):
        return pltpu.make_async_remote_copy(
            src_ref=gains.at[f],
            dst_ref=gains.at[f],
            send_sem=gs,
            recv_sem=gr,
            device_id=along_freq(k),
            device_id_type=MESH,
        )

    for k in masks:
        gain_copy(k).start()

    for work in beside[ITERS]:
        work()

    factor = 1.0 / math.sqrt(stations)
    for p in (0, 1):
        gain_r = z[0:1, p * stations : (p + 1) * stations]
        gain_i = z[1:2, p * stations : (p + 1) * stations]
        denom = jnp.maximum(gain_r * gain_r + gain_i * gain_i, 0.5)
        along_r = gain_r / denom
        along_i = gain_i / denom
        cos = cosine[...]
        sin = sine[...]
        w_r = ((cos * along_r - sin * along_i) * factor).astype(jnp.bfloat16)
        w_i = (-(cos * along_i + sin * along_r) * factor).astype(jnp.bfloat16)
        left[p, 0:beams] = w_r
        left[p, beams:] = w_i
        right[p, 0:beams] = -w_i
        right[p, beams:] = w_r

    def beamform(p):
        rows_p = slice(p * stations, (p + 1) * stations)
        result = jnp.dot(left[p], corr[0, rows_p, :], preferred_element_type=jnp.float32)
        result = result + jnp.dot(right[p], corr[1, rows_p, :], preferred_element_type=jnp.float32)
        result = result.astype(jnp.bfloat16)
        beams_out[0, p, 0] = result[:beams]
        beams_out[0, p, 1] = result[beams:]

    for p in (0, 1):
        beamform(p)

    def unpack(first, count, blocks_of):
        for part in (0, 1):
            for r in range(plan.row_tiles):
                block = blocks_of(part, r)
                if not permuted:
                    vis_out[0, part, r * cols + first : r * cols + first + count, :] = block
                    continue
                block = jnp.dot(block, to_natural[...], preferred_element_type=jnp.float32).astype(jnp.bfloat16)
                at = first
                while at < first + count:
                    start, extent, target = next(s for s in plan.segments if s[0] <= at < s[0] + s[1])
                    run = min(start + extent, first + count) - at
                    goal = r * cols + target + at - start
                    vis_out[0, part, goal : goal + run, :] = block[at - first : at - first + run]
                    at += run

    def arrived(u, part):
        return jnp.concatenate([landed[u][p, part] for p in range(nf)], axis=0)

    def early_block(part, r):
        top, below = arrived(0, part), arrived(1, part)
        first, second = plan.units[0][1], plan.units[1][1]
        if not permuted:
            return jnp.concatenate([top[r * first : (r + 1) * first], below[r * second : (r + 1) * second]], axis=1)
        left_half = jnp.concatenate(
            [top[r * first : (r + 1) * first], below[r * second : (r + 1) * second]], axis=0
        )
        side = slice(r * plan.level_rows, (r + 1) * plan.level_rows)
        return jnp.concatenate([left_half, arrived(2, part)[:, side], arrived(3, part)[:, side]], axis=1)

    def late_block(u, part, r):
        count = plan.units[u][1]
        return arrived(u, part)[r * count : (r + 1) * count]

    early_end = cols - plan.level_rows if permuted else cols
    for u in range(4 if permuted else nu):
        await_all(landed[u].at[pl.ds(0, nf - 1)], sr.at[u])
    unpack(0, early_end, early_block)
    for u in range(4, nu):
        await_all(landed[u].at[pl.ds(0, nf - 1)], sr.at[u])
        unpack(plan.units[u][0], plan.units[u][1], functools.partial(late_block, u))

    await_all(gains.at[pl.ds(0, nf - 1)], gr)
    gains_out[0] = gains[source_of(f)]

    await_all(priors.at[pl.ds(0, nf - 1)], qs)
    await_all(gains.at[pl.ds(0, nf - 1)], gs)
    await_all(src.at[pl.ds(0, nf - 1)], zs)
    for dg in range(1, ng):
        await_all(src, ys.at[dg - 1])
    await_all(gram.at[0, pl.ds(0, len(odds))], as_)
    if len(odds) > 1:
        await_all(gram.at[0, pl.ds(0, len(odds) - 1)], bs)
    for sem in (fs, ss):
        await_all(gram.at[0, 0, pl.ds(0, rows // nf * (nf - 1))], sem)
    await_all(updates.at[:, pl.ds(0, len(offsets))], us)


def finish(vis_in, gains_in, beams_in, vis_out, gains_out, beams_out, wide, sem):
    puts = [pltpu.make_async_copy(beams_in, beams_out, sem.at[0]), pltpu.make_async_copy(gains_in, gains_out, sem.at[1])]
    for put in puts:
        put.start()
    for part in (0, 1):
        wide[:, part] = vis_in[:, part].astype(jnp.float32)
        puts.append(pltpu.make_async_copy(wide.at[:, part], vis_out.at[:, part], sem.at[2 + part]))
        puts[-1].start()
    for put in puts:
        put.wait()


def body(
    voltages,
    prior_gains,
    station_flags,
    ingest_map,
    station_coords,
    pointing,
    corr_channels,
    beam_channels,
):
    nf = lax.axis_size("freq")
    nt = lax.axis_size("tm")
    ng = lax.axis_size("grp")
    _, _, per_input, samples = voltages.shape
    stations = ingest_map.shape[0]
    plan = Plan(nf, nt, ng, per_input, samples)
    inputs, rows, cols = plan.inputs, plan.rows, plan.cols
    part_beams = pointing.shape[1] // ng
    nc, nu = len(plan.chunks), len(plan.units)
    pairs = nt // 2
    dma = pltpu.SemaphoreType.DMA
    hbm = pl.BlockSpec(memory_space=pltpu.HBM)
    vmem = pl.BlockSpec(memory_space=pltpu.VMEM)
    shapes = [plan.unit_shape(u) for u in range(nu)]

    def bf16(*shape):
        return pltpu.VMEM(shape, jnp.bfloat16)

    def f32(*shape):
        return pltpu.VMEM(shape, jnp.float32)

    kept_bytes = 4 * rows * cols + 8 * inputs + 8 * part_beams * samples + 61440

    vis, gains, beams = pl.pallas_call(
        functools.partial(kernel, plan),
        out_shape=(
            pltpu.VMEM((1, 2, rows, cols), jnp.bfloat16),
            pltpu.VMEM((1, 2, inputs), jnp.float32),
            pltpu.VMEM((1, 2, 2, part_beams, samples), jnp.bfloat16),
        ),
        in_specs=[hbm] * 8,
        out_specs=(vmem, vmem, vmem),
        scratch_shapes=[
            bf16(nf, 2, per_input, samples),
            bf16(2, inputs, samples),
            f32(stations, LANES),
            f32(part_beams, stations),
            f32(part_beams, stations),
            bf16(cols, cols),
            bf16(cols, cols),
            bf16(2, 2 * part_beams, stations),
            bf16(2, 2 * part_beams, stations),
            f32(2, nt, rows, cols),
            f32(nf, 2, inputs),
            f32(ITERS, ng * nt, 2, rows),
            f32(2, inputs),
            f32(nf, 2, inputs),
            bf16(plan.levels, 6, inputs // plan.levels),
            f32(2, samples),
        ]
        + [bf16(2, r, pairs * w) for r, w in shapes] * 2
        + [bf16(pairs - 1, 2, r, w) for r, w in shapes] * 2
        + [bf16(nf, 2, r // nf, w) for r, w in shapes] * 2
        + [bf16(nf - 1, 2, r // nf, w) for r, w in shapes]
        + [bf16(nf, 2, r // nf, w) for r, w in shapes]
        + [
            dma,
            dma((nf - 1, nc)),
            dma((ng - 1,)),
            dma((plan.levels,)),
            dma((plan.levels,)),
            dma,
            dma,
            dma,
            dma((ITERS,)),
            dma,
            dma,
            dma,
            dma((nu,)),
            dma,
            dma((nu, pairs - 1)),
            dma,
            dma((nu,)),
            dma,
            dma((nu,)),
            dma((8,)),
            pltpu.VMEM(voltages.shape, jnp.bfloat16),
            pltpu.VMEM(prior_gains.shape, jnp.float32),
            pltpu.VMEM((1, stations), jnp.int32),
            pltpu.VMEM((1, stations), jnp.int32),
            pltpu.VMEM(station_coords.shape, jnp.float32),
            pltpu.VMEM(pointing.shape, jnp.int32),
            pltpu.SMEM(corr_channels.shape, jnp.int32),
            pltpu.SMEM(beam_channels.shape, jnp.int32),
        ],
        compiler_params=pltpu.CompilerParams(
            collective_id=0, has_side_effects=True, vmem_limit_bytes=67043328 - kept_bytes
        ),
    )(
        voltages,
        prior_gains,
        station_flags[None],
        ingest_map[None],
        station_coords,
        pointing,
        corr_channels,
        beam_channels,
    )
    results = (jax.ShapeDtypeStruct(vis.shape, jnp.float32), gains, beams)
    return pl.pallas_call(
        finish,
        out_shape=tuple(jax.ShapeDtypeStruct(r.shape, r.dtype) for r in results),
        in_specs=[vmem] * 3,
        out_specs=(hbm,) * 3,
        scratch_shapes=[
            f32(*vis.shape),
            dma((4,)),
        ],
        compiler_params=pltpu.CompilerParams(vmem_limit_bytes=4 * 1024 * 1024),
    )(vis, gains, beams)


def solution(mesh):
    return jax.shard_map(
        body,
        mesh=mesh,
        in_specs=(
            P(None, None, ("freq", "grp"), "tm"),
            P("freq", None, None),
            P(),
            P(),
            P(),
            P(),
            P(),
            P(),
        ),
        out_specs=(
            P("freq", None, "grp", "tm"),
            P("freq", None, None),
            P("freq", None, None, "grp", "tm"),
        ),
        check_vma=False,
    )
```

```python
import functools
import math

import jax
import jax.numpy as jnp
from jax import lax
from jax.experimental import pallas as pl
from jax.experimental.pallas import tpu as pltpu
from jax.sharding import PartitionSpec as P

ITERS = 4
LANES = 128
grid_cells = 64.0
MESH = pl.DeviceIdType.MESH


def partner(index, mask, count):
    result, bit = 0, 1
    while bit < count:
        digit = (index // bit) % 2
        result = result + bit * ((1 - digit) if mask & bit else digit)
        bit *= 2
    return result


def nt_dot(a, b):
    return lax.dot_general(a, b, (((1,), (1,)), ((), ())), preferred_element_type=jnp.float32)


def exact_parts(values):
    high = values.astype(jnp.bfloat16)
    rest = values - high.astype(jnp.float32)
    middle = rest.astype(jnp.bfloat16)
    low = (rest - middle.astype(jnp.float32)).astype(jnp.bfloat16)
    return jnp.concatenate([high, middle, low], axis=0)


def add_parts(values):
    count = values.shape[0] // 3
    return (values[2 * count :] + values[count : 2 * count]) + values[:count]


class Plan:
    def __init__(self, nf, nt, ng, per_input, samples):
        self.nf, self.nt, self.ng = nf, nt, ng
        self.per_input, self.samples = per_input, samples
        self.inputs = nf * ng * per_input
        self.rows = self.inputs // ng
        self.cols = self.inputs // nt
        self.blocks = self.cols // per_input
        self.row_tiles = nt // ng
        self.levels = 4 if per_input % 64 == 0 else 1
        self.step = per_input // self.levels
        self.level_rows = self.cols // self.levels
        count = 16 if self.step % 16 == 0 else self.step
        self.chunks = tuple((part, first, count) for first in range(0, per_input, count) for part in (0, 1))
        half = self.cols // 2
        if self.levels > 1:
            most = self.cols - self.level_rows
            units = [(0, half, 0, half, False), (half, most - half, 0, half, False)]
            units += [(0, most, lane, self.level_rows, True) for lane in (half, most)]
            rest = self.level_rows // 2
            units += [(first, rest, 0, self.cols, False) for first in (most, most + rest)]
        else:
            units = [(0, self.cols, 0, half, False), (0, self.cols, half, half, False)]
        self.units = tuple(units)
        self.segments = tuple(
            (q * self.level_rows + b * self.step, self.step, b * per_input + q * self.step)
            for q in range(self.levels)
            for b in range(self.blocks)
        )

    def unit_shape(self, unit):
        _, seg_rows, _, lanes, beside = self.units[unit]
        return (seg_rows, self.row_tiles * lanes) if beside else (self.row_tiles * seg_rows, lanes)


def kernel(plan, *refs):
    nf, nt, ng = plan.nf, plan.nt, plan.ng
    nu = len(plan.units)
    operands, refs = refs[:8], refs[8:]
    vis_out, gains_out, beams_out = refs[:3]
    refs = refs[3:]

    def take(count):
        nonlocal refs
        taken, refs = refs[:count], refs[count:]
        return taken

    src, corr, keep, cosine, sine, to_held, to_natural, left, right, gram = take(10)
    priors, updates, z, gains, first_gains, gathered = take(6)
    stage_a, landed_a, stage_b, landed_b = (take(nu) for _ in range(4))
    first_src, mid, second_src, landed = (take(nu) for _ in range(4))
    zs, zr, ys, yr, own_sem, qs, qr, us, ur, gs, gr, as_, ar, bs, br, fs, fr, ss, sr, in_sem = take(20)
    held = refs
    voltages, prior, flags, slots, coords, pointing, corr_channels, beam_channels = held
    loads = [pltpu.make_async_copy(operands[i], held[i], in_sem.at[i]) for i in range(8)]
    for load in loads:
        load.start()
    f = lax.axis_index("freq")
    t = lax.axis_index("tm")
    g = lax.axis_index("grp")
    per_input, samples = plan.per_input, plan.samples
    inputs, rows, cols = plan.inputs, plan.rows, plan.cols
    stations = inputs // 2
    chunks = plan.chunks
    offsets = [(dt, dg) for dg in range(ng) for dt in range(nt) if (dt, dg) != (0, 0)]
    masks = list(range(nf - 1, 0, -1))
    peers = {k: partner(f, k, nf) for k in range(nf)}
    tiles = {d: partner(t, d, nt) for d in range(nt)}

    def group(dt, dg):
        return {"freq": f, "tm": (t + dt) % nt, "grp": (g + dg) % ng}

    def along_freq(k):
        return {"freq": peers[k], "tm": t, "grp": g}

    def along_tm(d):
        return {"freq": f, "tm": tiles[d], "grp": g}

    def await_all(ref, sem):
        pltpu.make_async_copy(ref, ref, sem).wait()

    barrier = pltpu.get_barrier_semaphore()
    for k in masks:
        pl.semaphore_signal(barrier, inc=1, device_id=along_freq(k), device_id_type=MESH)
    for dt, dg in offsets:
        pl.semaphore_signal(barrier, inc=1, device_id=group(dt, dg), device_id_type=MESH)
    for load in loads:
        load.wait()

    slot_rows = jnp.broadcast_to(slots[...].astype(jnp.float32), (LANES, stations)).T
    flagged = jnp.zeros((stations, LANES), jnp.float32)
    for first in range(0, stations, LANES):
        lane = lax.broadcasted_iota(jnp.int32, (stations, LANES), 1) + first
        flag = flags[0:1, first : first + LANES].astype(jnp.float32)
        flagged += jnp.where(slot_rows == lane.astype(jnp.float32), flag, 0.0)
    flagged = jnp.sum(flagged, axis=1, keepdims=True)
    keep[...] = jnp.broadcast_to(1.0 - flagged, (stations, LANES))
    first_slot = pl.multiple_of(((f * ng + g) * per_input) % stations, per_input)
    kept = keep[pl.ds(first_slot, per_input), 0:1].astype(jnp.bfloat16)

    for k in masks + [0]:
        for part in (0, 1):
            src[peers[k], part] = voltages[beam_channels[peers[k]], part] * kept

    pl.semaphore_wait(barrier, len(masks) + len(offsets))

    def held_start(owner, member, first):
        block = owner * ng + member
        level = first // plan.step
        start = (block // plan.blocks) * cols + level * plan.level_rows + (block % plan.blocks) * plan.step
        return pl.multiple_of(start + first % plan.step, math.gcd(plan.step, 16))

    def place(owner, chunk):
        part, first, count = chunk
        return corr.at[part, pl.ds(held_start(owner, g, first), count), :]

    def z_copy(k, ci):
        part, first, count = chunks[ci]
        return pltpu.make_async_remote_copy(
            src_ref=src.at[peers[k], part, pl.ds(first, count), :],
            dst_ref=place(f, chunks[ci]),
            send_sem=zs,
            recv_sem=zr.at[k - 1, ci],
            device_id=along_freq(k),
            device_id_type=MESH,
        )

    def y_copy(k, ci, dg):
        part, first, count = chunks[ci]
        spot = place(peers[k], chunks[ci])
        return pltpu.make_async_remote_copy(
            src_ref=src.at[f, part, pl.ds(first, count), :] if k == 0 else spot,
            dst_ref=spot,
            send_sem=ys.at[dg - 1],
            recv_sem=yr.at[first // plan.step],
            device_id=group(0, dg),
            device_id_type=MESH,
        )

    def forward(k, ci):
        for dg in range(1, ng):
            y_copy(k, ci, dg).start()

    own_copies = [
        pltpu.make_async_copy(
            src.at[f, :, pl.ds(first, plan.step), :],
            corr.at[:, pl.ds(held_start(f, g, first), plan.step), :],
            own_sem.at[first // plan.step],
        )
        for first in range(0, per_input, plan.step)
    ]

    def prior_copy(k):
        return pltpu.make_async_remote_copy(
            src_ref=prior.at[0],
            dst_ref=priors.at[f],
            send_sem=qs,
            recv_sem=qr,
            device_id=along_freq(k),
            device_id_type=MESH,
        )

    all_chunks = range(len(chunks))
    ahead = 2

    sent = [0]

    def send_until(count):
        while sent[0] < min(count, len(chunks)):
            for k in masks:
                z_copy(k, sent[0]).start()
            sent[0] += 1

    send_until(1)
    for k in masks:
        prior_copy(k).start()
    send_until(ahead)
    for ci in all_chunks:
        forward(0, ci)
    for copy in own_copies:
        copy.start()
    priors[f] = prior[0]

    n_beams = pointing.shape[1]
    beams = n_beams // ng
    my_beam = beam_channels[f]
    permuted = plan.levels > 1

    def natural(held_index):
        result = held_index
        for start, size, target in plan.segments:
            inside = (held_index >= start) & (held_index < start + size)
            result = jnp.where(inside, held_index + (target - start), result)
        return result

    if permuted:
        along_rows = lax.broadcasted_iota(jnp.int32, (cols, cols), 0)
        along_lanes = lax.broadcasted_iota(jnp.int32, (cols, cols), 1)
        to_held[...] = jnp.where(natural(along_lanes) == along_rows, 1.0, 0.0).astype(jnp.bfloat16)
        to_natural[...] = jnp.where(natural(along_rows) == along_lanes, 1.0, 0.0).astype(jnp.bfloat16)

    def reorder(rows_in, matrix):
        if not permuted:
            return rows_in
        parts = exact_parts(rows_in)
        moved = [
            jnp.dot(parts[:, first : first + cols], matrix[...], preferred_element_type=jnp.float32)
            for first in range(0, rows_in.shape[1], cols)
        ]
        return add_parts(jnp.concatenate(moved, axis=1))

    def point_phases():
        ratio = 0.875 + 0.25 * (my_beam.astype(jnp.float32) + 0.5) / nf
        mine = pl.ds(pl.multiple_of(g * beams, beams), beams)
        east_dir, north_dir = (
            jnp.broadcast_to((pointing[d : d + 1, mine].astype(jnp.float32) + 0.5) / grid_cells - 0.5, (LANES, beams)).T
            for d in (0, 1)
        )
        east, north = (jnp.broadcast_to(coords[d : d + 1, :], (LANES, stations)).T for d in (0, 1))
        station = lax.broadcasted_iota(jnp.int32, (stations, LANES), 0)
        slot_east, slot_north = [], []
        for first in range(0, stations, LANES):
            lanes = slice(first, first + LANES)
            match = station == slots[0:1, lanes]
            slot_east.append(jnp.sum(jnp.where(match, east, 0.0), axis=0, keepdims=True))
            slot_north.append(jnp.sum(jnp.where(match, north, 0.0), axis=0, keepdims=True))
        where = jnp.concatenate(
            [jnp.concatenate(slot_east, axis=1), jnp.concatenate(slot_north, axis=1)], axis=0
        )
        where = reorder(where, to_held)
        for first in range(0, stations, LANES):
            lanes = slice(first, first + LANES)
            phase = 2.0 * math.pi * ratio * (east_dir * where[0:1, lanes] + north_dir * where[1:2, lanes])
            cosine[:, lanes] = jnp.cos(phase)
            sine[:, lanes] = jnp.sin(phase)

    point_phases()

    await_all(priors.at[pl.ds(0, nf - 1)], qr)
    slot_of_mine = 0
    for k in range(nf):
        slot_of_mine = jnp.where(corr_channels[k] == my_beam, k, slot_of_mine)
    z[...] = reorder(priors[slot_of_mine], to_held)
    start_parts = exact_parts(z[...])
    size = plan.level_rows
    for q in range(plan.levels):
        pieces = [start_parts[:, tile * cols + q * size : tile * cols + (q + 1) * size] for tile in range(nt)]
        first_gains[q] = jnp.concatenate(pieces, axis=1)

    scale = 1.0 / (samples * nt)
    odds = list(range(nt - 1, 0, -2))
    evens = [d - 1 for d in odds]

    def a_copy(u):
        return pltpu.make_async_remote_copy(
            src_ref=stage_a[u],
            dst_ref=landed_a[u],
            send_sem=as_,
            recv_sem=ar.at[u],
            device_id=along_tm(1),
            device_id_type=MESH,
        )

    def b_copy(u, d):
        return pltpu.make_async_remote_copy(
            src_ref=stage_b[u].at[d // 2 - 1],
            dst_ref=landed_b[u].at[d // 2 - 1],
            send_sem=bs,
            recv_sem=br.at[u, d // 2 - 1],
            device_id=along_tm(d),
            device_id_type=MESH,
        )

    def first_copy(u, k):
        return pltpu.make_async_remote_copy(
            src_ref=first_src[u].at[peers[k]],
            dst_ref=mid[u].at[f],
            send_sem=fs,
            recv_sem=fr.at[u],
            device_id=along_freq(k),
            device_id_type=MESH,
        )

    def second_copy(u, k):
        return pltpu.make_async_remote_copy(
            src_ref=second_src[u].at[k - 1],
            dst_ref=landed[u].at[f],
            send_sem=ss,
            recv_sem=sr.at[u],
            device_id=along_freq(k),
            device_id_type=MESH,
        )

    def correlate(seg, seg_rows, lane, lanes):
        def stacked(part):
            pieces = []
            for r in range(plan.row_tiles):
                start = pl.multiple_of(g * rows + r * cols + seg, plan.level_rows)
                pieces.append(corr[part, pl.ds(start, seg_rows), :])
            return pieces

        mine = jnp.concatenate(stacked(0) + stacked(1), axis=0)
        count = plan.row_tiles * seg_rows
        others = [
            jnp.concatenate(
                [corr[part, tile * cols + lane : tile * cols + lane + lanes, :] for tile in range(nt)], axis=0
            )
            for part in (0, 1)
        ]
        with_r = nt_dot(mine, others[0])
        with_i = nt_dot(mine, others[1])
        real = (with_r[:count] + with_i[count:]) * scale
        imag = (with_r[count:] - with_i[:count]) * scale
        for part, value in ((0, real), (1, imag)):
            for tile in range(nt):
                for r in range(plan.row_tiles):
                    gram[part, tile, r * cols + seg : r * cols + seg + seg_rows, lane : lane + lanes] = value[
                        r * seg_rows : (r + 1) * seg_rows, tile * lanes : (tile + 1) * lanes
                    ]

    def correlate_level(q):
        size = plan.level_rows
        correlate(0, (q + 1) * size, q * size, size)
        if q >= 2:
            correlate(q * size, size, 0, 2 * size)
        if q % 2:
            correlate(q * size, size, (q - 1) * size, size)

    def gather_level(q):
        pieces = [
            jnp.concatenate([corr[part, tile * cols + q * size : tile * cols + (q + 1) * size, :] for tile in range(nt)], axis=0)
            for part in (0, 1)
        ]
        with_r, with_i = (
            add_parts(jnp.dot(first_gains[q], piece, preferred_element_type=jnp.float32)) for piece in pieces
        )
        real = with_r[0:1] + with_i[1:2]
        imag = with_r[1:2] - with_i[0:1]
        if q:
            real = real + gathered[0:1]
            imag = imag + gathered[1:2]
        gathered[0:1] = real
        gathered[1:2] = imag

    def first_product():
        parts = exact_parts(gathered[...] * scale)
        mine = pl.ds(pl.multiple_of(g * rows, rows), rows)
        with_r = add_parts(nt_dot(parts, corr[0, mine, :]))
        with_i = add_parts(nt_dot(parts, corr[1, mine, :]))
        updates[0, slot, 0:1] = with_r[0:1] - with_i[1:2]
        updates[0, slot, 1:2] = with_r[1:2] + with_i[0:1]

    slot = g * nt + t

    def update_copy(iteration, o):
        dt, dg = offsets[o]
        return pltpu.make_async_remote_copy(
            src_ref=updates.at[iteration, slot],
            dst_ref=updates.at[iteration, slot],
            send_sem=us,
            recv_sem=ur.at[iteration],
            device_id=group(dt, dg),
            device_id_type=MESH,
        )

    def send_updates(iteration):
        for o in range(len(offsets)):
            update_copy(iteration, o).start()

    def from_gram(u, part, d):
        seg, seg_rows, lane, lanes, side_by_side = plan.units[u]
        return jnp.concatenate(
            [
                gram[part, tiles[d], r * cols + seg : r * cols + seg + seg_rows, lane : lane + lanes]
                for r in range(plan.row_tiles)
            ],
            axis=1 if side_by_side else 0,
        )

    def send_pair(u):
        lanes = plan.unit_shape(u)[1]
        for j, d in enumerate(odds):
            for part in (0, 1):
                stage_a[u][part, :, j * lanes : (j + 1) * lanes] = from_gram(u, part, d).astype(jnp.bfloat16)
        a_copy(u).start()

    def sum_pair(u):
        lanes = plan.unit_shape(u)[1]
        a_copy(u).wait_recv()
        for j, d in enumerate(evens):
            if d:
                for part in (0, 1):
                    theirs = landed_a[u][part, :, j * lanes : (j + 1) * lanes].astype(jnp.float32)
                    stage_b[u][d // 2 - 1, part] = (from_gram(u, part, d) + theirs).astype(jnp.bfloat16)
        for d in evens:
            if d:
                b_copy(u, d).start()

    def sum_rest(u):
        total_rows, lanes = plan.unit_shape(u)
        piece = total_rows // nf
        for d in evens:
            if d:
                b_copy(u, d).wait_recv()
        j = len(evens) - 1
        for part in (0, 1):
            total = from_gram(u, part, 0) + landed_a[u][part, :, j * lanes : (j + 1) * lanes].astype(jnp.float32)
            for d in evens:
                if d:
                    total = total + landed_b[u][d // 2 - 1, part].astype(jnp.float32)
            total = total.astype(jnp.bfloat16)
            for p in range(nf):
                first_src[u][p, part] = total[p * piece : (p + 1) * piece]
        mid[u][f] = first_src[u][f]
        for k in masks:
            first_copy(u, k).start()

    def source_of(slot):
        wanted = corr_channels[slot]
        source = 0
        for s in range(nf):
            source = jnp.where(beam_channels[s] == wanted, s, source)
        return source

    def hand_on(u):
        await_all(mid[u].at[pl.ds(0, nf - 1)], fr.at[u])
        for k in masks:
            second_src[u][k - 1] = mid[u][source_of(peers[k])]
        landed[u][f] = mid[u][source_of(f)]
        for k in masks:
            second_copy(u, k).start()

    nearest_first = masks[-1:] + masks[:-1]

    def relay(ci, spare=0):
        for k in nearest_first:
            z_copy(k, ci).wait_recv()
            forward(k, ci)
        send_until(ci + 1 + ahead + spare)

    def of_level(q):
        return [ci for ci in all_chunks if chunks[ci][1] // plan.step == q]

    def await_level(q):
        own_copies[q].wait()
        await_all(corr.at[:, pl.ds(0, (ng - 1) * nf * plan.step), :], yr.at[q])

    last = plan.levels - 1
    early_units = [0, 1, 2] if last else []
    late_units = [u for u in range(nu) if u not in early_units]
    ready = {last - 1: [0], last: [1, 2]} if last else {}
    for q in range(plan.levels):
        members = of_level(q)
        relay(members[0], spare=1)
        if q:
            await_level(q - 1)
            gather_level(q - 1)
            correlate_level(q - 1)
        for u in ready.get(q, []):
            send_pair(u)
        relay(members[1])
        for u in ready.get(q, []):
            sum_pair(u)
        if q == last:
            for u in early_units[:1]:
                sum_rest(u)
        for ci in members[2:]:
            relay(ci)
    for u in early_units[1:]:
        sum_rest(u)
    await_level(last)
    gather_level(last)
    first_product()
    send_updates(0)
    for u in early_units[:1]:
        hand_on(u)
    correlate_level(last)
    for u in late_units:
        send_pair(u)
    strip = LANES
    per_tile = cols // LANES

    beside = {i: [] for i in range(ITERS + 1)}

    def plan_work(iteration, work, u):
        beside[min(iteration, ITERS)].append(functools.partial(work, u))

    for u in late_units:
        plan_work(1, sum_pair, u)
    for u in early_units[1:]:
        plan_work(1, hand_on, u)
    for u in late_units:
        plan_work(2, sum_rest, u)
    for i, u in enumerate(late_units):
        plan_work(4 if i > 1 else 3, hand_on, u)
    for iteration in range(ITERS):
        power = jnp.sum(z[...] * z[...]) + 1e-06

        def product(r, carry):
            here = pl.ds(pl.multiple_of(r * strip, strip), strip)
            total_r = jnp.zeros((strip, LANES), jnp.float32)
            total_i = jnp.zeros((strip, LANES), jnp.float32)
            for c in range(inputs // LANES):
                lanes = slice(c * LANES, (c + 1) * LANES)
                tile, inner = c // per_tile, slice(c % per_tile * LANES, (c % per_tile + 1) * LANES)
                part_r = gram[0, tile, here, inner]
                part_i = gram[1, tile, here, inner]
                gain_r = z[0:1, lanes]
                gain_i = z[1:2, lanes]
                total_r += part_r * gain_r - part_i * gain_i
                total_i += part_i * gain_r + part_r * gain_i
            updates[iteration, slot, 0:1, here] = jnp.sum(total_r.T, axis=0, keepdims=True)
            updates[iteration, slot, 1:2, here] = jnp.sum(total_i.T, axis=0, keepdims=True)
            return carry

        if iteration:
            lax.fori_loop(0, rows // strip, product, 0)
            send_updates(iteration)
        for work in beside[iteration]:
            work()
        await_all(updates.at[iteration, pl.ds(0, len(offsets))], ur.at[iteration])
        for h in range(ng):
            total = updates[iteration, h * nt]
            for other in range(1, nt):
                total = total + updates[iteration, h * nt + other]
            lanes = slice(h * rows, (h + 1) * rows)
            z[:, lanes] = 0.5 * (z[:, lanes] + inputs * total / power)

    gains[f] = reorder(z[...], to_natural)

    def gain_copy(k):
        return pltpu.make_async_remote_copy(
            src_ref=gains.at[f],
            dst_ref=gains.at[f],
            send_sem=gs,
            recv_sem=gr,
            device_id=along_freq(k),
            device_id_type=MESH,
        )

    for k in masks:
        gain_copy(k).start()

    for work in beside[ITERS]:
        work()

    factor = 1.0 / math.sqrt(stations)
    for p in (0, 1):
        gain_r = z[0:1, p * stations : (p + 1) * stations]
        gain_i = z[1:2, p * stations : (p + 1) * stations]
        denom = jnp.maximum(gain_r * gain_r + gain_i * gain_i, 0.5)
        along_r = gain_r / denom
        along_i = gain_i / denom
        cos = cosine[...]
        sin = sine[...]
        w_r = ((cos * along_r - sin * along_i) * factor).astype(jnp.bfloat16)
        w_i = (-(cos * along_i + sin * along_r) * factor).astype(jnp.bfloat16)
        left[p, 0:beams] = w_r
        left[p, beams:] = w_i
        right[p, 0:beams] = -w_i
        right[p, beams:] = w_r

    def beamform(p):
        rows_p = slice(p * stations, (p + 1) * stations)
        result = jnp.dot(left[p], corr[0, rows_p, :], preferred_element_type=jnp.float32)
        result = result + jnp.dot(right[p], corr[1, rows_p, :], preferred_element_type=jnp.float32)
        result = result.astype(jnp.bfloat16)
        beams_out[0, p, 0] = result[:beams]
        beams_out[0, p, 1] = result[beams:]

    for p in (0, 1):
        beamform(p)

    def unpack(first, count, blocks_of):
        for part in (0, 1):
            for r in range(plan.row_tiles):
                block = blocks_of(part, r)
                if not permuted:
                    vis_out[0, part, r * cols + first : r * cols + first + count, :] = block
                    continue
                block = jnp.dot(block, to_natural[...], preferred_element_type=jnp.float32).astype(jnp.bfloat16)
                at = first
                while at < first + count:
                    start, extent, target = next(s for s in plan.segments if s[0] <= at < s[0] + s[1])
                    run = min(start + extent, first + count) - at
                    goal = r * cols + target + at - start
                    vis_out[0, part, goal : goal + run, :] = block[at - first : at - first + run]
                    at += run

    def arrived(u, part):
        return jnp.concatenate([landed[u][p, part] for p in range(nf)], axis=0)

    def early_block(part, r):
        top, below = arrived(0, part), arrived(1, part)
        first, second = plan.units[0][1], plan.units[1][1]
        if not permuted:
            return jnp.concatenate([top[r * first : (r + 1) * first], below[r * second : (r + 1) * second]], axis=1)
        left_half = jnp.concatenate(
            [top[r * first : (r + 1) * first], below[r * second : (r + 1) * second]], axis=0
        )
        side = slice(r * plan.level_rows, (r + 1) * plan.level_rows)
        return jnp.concatenate([left_half, arrived(2, part)[:, side], arrived(3, part)[:, side]], axis=1)

    def late_block(u, part, r):
        count = plan.units[u][1]
        return arrived(u, part)[r * count : (r + 1) * count]

    await_all(priors.at[pl.ds(0, nf - 1)], qs)
    await_all(src.at[pl.ds(0, nf - 1)], zs)
    for dg in range(1, ng):
        await_all(src, ys.at[dg - 1])
    await_all(gram.at[0, pl.ds(0, len(odds))], as_)
    if len(odds) > 1:
        await_all(gram.at[0, pl.ds(0, len(odds) - 1)], bs)
    await_all(updates.at[:, pl.ds(0, len(offsets))], us)

    early_end = cols - plan.level_rows if permuted else cols
    for u in range(4 if permuted else nu):
        await_all(landed[u].at[pl.ds(0, nf - 1)], sr.at[u])
    unpack(0, early_end, early_block)
    for u in range(4, nu):
        await_all(landed[u].at[pl.ds(0, nf - 1)], sr.at[u])
        unpack(plan.units[u][0], plan.units[u][1], functools.partial(late_block, u))

    await_all(gains.at[pl.ds(0, nf - 1)], gr)
    gains_out[0] = gains[source_of(f)]

    await_all(gains.at[pl.ds(0, nf - 1)], gs)
    for sem in (fs, ss):
        await_all(gram.at[0, 0, pl.ds(0, rows // nf * (nf - 1))], sem)


def finish(vis_in, gains_in, beams_in, vis_out, gains_out, beams_out, wide, sem):
    puts = [pltpu.make_async_copy(beams_in, beams_out, sem.at[0]), pltpu.make_async_copy(gains_in, gains_out, sem.at[1])]
    for put in puts:
        put.start()
    for part in (0, 1):
        wide[:, part] = vis_in[:, part].astype(jnp.float32)
        puts.append(pltpu.make_async_copy(wide.at[:, part], vis_out.at[:, part], sem.at[2 + part]))
        puts[-1].start()
    for put in puts:
        put.wait()


def body(
    voltages,
    prior_gains,
    station_flags,
    ingest_map,
    station_coords,
    pointing,
    corr_channels,
    beam_channels,
):
    nf = lax.axis_size("freq")
    nt = lax.axis_size("tm")
    ng = lax.axis_size("grp")
    _, _, per_input, samples = voltages.shape
    stations = ingest_map.shape[0]
    plan = Plan(nf, nt, ng, per_input, samples)
    inputs, rows, cols = plan.inputs, plan.rows, plan.cols
    part_beams = pointing.shape[1] // ng
    nc, nu = len(plan.chunks), len(plan.units)
    pairs = nt // 2
    dma = pltpu.SemaphoreType.DMA
    hbm = pl.BlockSpec(memory_space=pltpu.HBM)
    vmem = pl.BlockSpec(memory_space=pltpu.VMEM)
    shapes = [plan.unit_shape(u) for u in range(nu)]

    def bf16(*shape):
        return pltpu.VMEM(shape, jnp.bfloat16)

    def f32(*shape):
        return pltpu.VMEM(shape, jnp.float32)

    kept_bytes = 4 * rows * cols + 8 * inputs + 8 * part_beams * samples + 61440

    vis, gains, beams = pl.pallas_call(
        functools.partial(kernel, plan),
        out_shape=(
            pltpu.VMEM((1, 2, rows, cols), jnp.bfloat16),
            pltpu.VMEM((1, 2, inputs), jnp.float32),
            pltpu.VMEM((1, 2, 2, part_beams, samples), jnp.bfloat16),
        ),
        in_specs=[hbm] * 8,
        out_specs=(vmem, vmem, vmem),
        scratch_shapes=[
            bf16(nf, 2, per_input, samples),
            bf16(2, inputs, samples),
            f32(stations, LANES),
            f32(part_beams, stations),
            f32(part_beams, stations),
            bf16(cols, cols),
            bf16(cols, cols),
            bf16(2, 2 * part_beams, stations),
            bf16(2, 2 * part_beams, stations),
            f32(2, nt, rows, cols),
            f32(nf, 2, inputs),
            f32(ITERS, ng * nt, 2, rows),
            f32(2, inputs),
            f32(nf, 2, inputs),
            bf16(plan.levels, 6, inputs // plan.levels),
            f32(2, samples),
        ]
        + [bf16(2, r, pairs * w) for r, w in shapes] * 2
        + [bf16(pairs - 1, 2, r, w) for r, w in shapes] * 2
        + [bf16(nf, 2, r // nf, w) for r, w in shapes] * 2
        + [bf16(nf - 1, 2, r // nf, w) for r, w in shapes]
        + [bf16(nf, 2, r // nf, w) for r, w in shapes]
        + [
            dma,
            dma((nf - 1, nc)),
            dma((ng - 1,)),
            dma((plan.levels,)),
            dma((plan.levels,)),
            dma,
            dma,
            dma,
            dma((ITERS,)),
            dma,
            dma,
            dma,
            dma((nu,)),
            dma,
            dma((nu, pairs - 1)),
            dma,
            dma((nu,)),
            dma,
            dma((nu,)),
            dma((8,)),
            pltpu.VMEM(voltages.shape, jnp.bfloat16),
            pltpu.VMEM(prior_gains.shape, jnp.float32),
            pltpu.VMEM((1, stations), jnp.int32),
            pltpu.VMEM((1, stations), jnp.int32),
            pltpu.VMEM(station_coords.shape, jnp.float32),
            pltpu.VMEM(pointing.shape, jnp.int32),
            pltpu.SMEM(corr_channels.shape, jnp.int32),
            pltpu.SMEM(beam_channels.shape, jnp.int32),
        ],
        compiler_params=pltpu.CompilerParams(
            collective_id=0, has_side_effects=True, vmem_limit_bytes=67043328 - kept_bytes
        ),
    )(
        voltages,
        prior_gains,
        station_flags[None],
        ingest_map[None],
        station_coords,
        pointing,
        corr_channels,
        beam_channels,
    )
    results = (jax.ShapeDtypeStruct(vis.shape, jnp.float32), gains, beams)
    return pl.pallas_call(
        finish,
        out_shape=tuple(jax.ShapeDtypeStruct(r.shape, r.dtype) for r in results),
        in_specs=[vmem] * 3,
        out_specs=(hbm,) * 3,
        scratch_shapes=[
            f32(*vis.shape),
            dma((4,)),
        ],
        compiler_params=pltpu.CompilerParams(vmem_limit_bytes=4 * 1024 * 1024),
    )(vis, gains, beams)


def solution(mesh):
    return jax.shard_map(
        body,
        mesh=mesh,
        in_specs=(
            P(None, None, ("freq", "grp"), "tm"),
            P("freq", None, None),
            P(),
            P(),
            P(),
            P(),
            P(),
            P(),
        ),
        out_specs=(
            P("freq", None, "grp", "tm"),
            P("freq", None, None),
            P("freq", None, None, "grp", "tm"),
        ),
        check_vma=False,
    )
```
